128 devices in a mesh: seq: 16 (over z_hi, y, core), head: 8 (over x, z_lo).
Axes of the slice: x: 4, y: 4, z: 4 (z_hi: 2, z_lo: 2; z = z_hi * 2 + z_lo), core: 2. Of those that a mesh axis runs over, the one named last changes fastest.
Arguments:
- queries: bfloat16 [128, 16384], P(None, 'head')
- cache_keys: bfloat16 [2, 65536, 1024], P(None, 'seq', 'head'), may hold values from -6 to 6
- cache_values: bfloat16 [2, 65536, 1024], P(None, 'seq', 'head'), may hold values from -6 to 6
- tree_keys: bfloat16 [128, 1024], P(None, 'head')
- tree_values: bfloat16 [128, 1024], P(None, 'head'), may hold values from -6 to 6
- ancestors: int32 [2, 64, 64], replicated, may hold values from 0 to 1, as said below
- filled_extents: int32 [2], replicated, may hold values from 1 to 65536, as said below
- out_weight: bfloat16 [16384, 16384], P('head', 'seq'), may hold values from -0.046875 to 0.046875
- residual: bfloat16 [128, 16384], P(None, 'seq'), may hold values from -6 to 6
- norm_gain: bfloat16 [16384], replicated, may hold values from 0.099609375 to 1.8984375
- vocab_weight: bfloat16 [16384, 65536], P(None, ('seq', 'head'))
- candidates: int32 [128], replicated, may hold values from 0 to 65535
- amateur: float32 [128], replicated, may hold values from -12 to -1
Outputs:
- hidden: bfloat16 [128, 16384], P(None, ('seq', 'head'))
- contrast: float32 [128], replicated
The draws below stay inside these ranges and needn't reach their ends.
Inputs may be any that keep to these rules, and one draw needn't show every extreme that they name: Rows are nodes; node 0 is the root; every node's parent has a smaller index; ancestors[b, i, i] = 1. Positions 0 to filled_extents[b] - 1 of request b are live; some request has length 65536.
All inputs are finite; a program needn't handle non-finite values.
Results may differ from the reference program's by a relative error of at most 0.006.
Values may be sent and summed in bfloat16 or wider, within the bound.
No kernel may reach another device: no remote copies, remote signals or barrier semaphores. Data moves between devices by JAX's collectives and lax.ppermute only.
A program may use at most 192 MiB of HBM per device.

```python
import math
import jax
import jax.numpy as jnp
from jax import lax

REQUESTS = 2
NODES_REQ = 64
D = 16384
H = 128
KVH = 8
HD = 128
V = 65536
STORE_LIMIT = 65536
NODES = 128


def tree_key_base(key):
    return jax.random.normal(jax.random.fold_in(key, 11), (NODES, KVH * HD), jnp.float32)


def draw_tree_keys(key, part):
    return tree_key_base(key).astype(jnp.bfloat16)


def draw_queries(key, part):
    base = jax.random.normal(jax.random.fold_in(key, 12), (NODES, H * HD), jnp.float32)
    return base.astype(jnp.bfloat16)


def draw_vocab_weight(key, part):
    factor = 3.0 / math.sqrt(D)
    entries = jax.random.normal(jax.random.fold_in(key, 21), (D, V), jnp.float32) * factor
    return entries.astype(jnp.bfloat16)


def draw_filled_extents(key, part):
    drawn = jax.random.randint(jax.random.fold_in(key, 31), (REQUESTS,), 1, STORE_LIMIT + 1)
    longest = jax.random.randint(jax.random.fold_in(key, 32), (), 0, REQUESTS)
    return jnp.where(jnp.arange(REQUESTS, dtype=jnp.int32) == longest, STORE_LIMIT, drawn).astype(jnp.int32)


def draw_ancestors(key, part):
    index_row = jnp.arange(NODES_REQ, dtype=jnp.int32)
    raw_parent = jax.random.randint(jax.random.fold_in(key, 41), (REQUESTS, NODES_REQ), 0, NODES_REQ)
    parent = jnp.where(index_row[None, :] > 0, raw_parent % jnp.maximum(index_row[None, :], 1), 0).astype(jnp.int32)
    start_mask = jnp.broadcast_to(jnp.eye(NODES_REQ, dtype=jnp.int32)[None], (REQUESTS, NODES_REQ, NODES_REQ))

    def extend(node, table):
        parent_now = lax.dynamic_slice_in_dim(parent, node, 1, 1)[:, 0]
        where_from = jnp.broadcast_to(parent_now[:, None, None], (REQUESTS, 1, NODES_REQ))
        inherited = jnp.take_along_axis(table, where_from, axis=1)[:, 0, :]
        new_row = inherited + (index_row == node).astype(jnp.int32)[None, :]
        return lax.dynamic_update_slice_in_dim(table, new_row[:, None, :], node, 1)
    return lax.fori_loop(1, NODES_REQ, extend, start_mask)


def place_ends(array, key, low, top_value):
    longest = array.shape.index(max(array.shape))
    spots = []
    for shift in (0, 1):
        where = [jax.random.randint(jax.random.fold_in(key, axis), (), 0, length) for axis, length in enumerate(array.shape)]
        where[longest] = (where[longest] + shift) % array.shape[longest]
        spots.append(tuple(where))
    return array.at[spots[0]].set(low).at[spots[1]].set(top_value)


def block_levels(own_key, dims, cuts, smallest, largest):
    def one(position, blocks):
        draws = jax.random.uniform(jax.random.fold_in(jax.random.fold_in(own_key, 6), position), (blocks,), jnp.float32, smallest / len(cuts), largest / len(cuts))
        return jnp.repeat(jnp.exp(draws), dims[position] // blocks).reshape((-1,) + (1,) * (len(dims) - position - 1))

    level = one(*cuts[0])
    for cut in cuts[1:]:
        level = level * one(*cut)
    return level


def gaussian(own_key, shape, width, most, cuts=(), held_as=jnp.bfloat16):
    level = block_levels(own_key, shape, cuts, -0.22, 0.18) if cuts else 1.0
    result = jax.random.normal(own_key, shape, jnp.float32) * width * level
    return jnp.minimum(jnp.maximum(result, -most), most).astype(held_as)


def setup_inputs(seed: int = 0) -> dict:
    keys = jax.random.split(jax.random.key(seed), 14)
    return {
        "queries": draw_queries(jax.random.fold_in(keys[13], 71), 0),
        "cache_keys": gaussian(keys[1], (REQUESTS, STORE_LIMIT, KVH * HD), 1.0, 6.0, ((1, 16), (2, 8))),
        "cache_values": gaussian(keys[2], (REQUESTS, STORE_LIMIT, KVH * HD), 1.0, 6.0, ((1, 16), (2, 8))),
        "tree_keys": draw_tree_keys(jax.random.fold_in(keys[13], 71), 0),
        "tree_values": gaussian(keys[4], (NODES, KVH * HD), 1.0, 6.0, ((1, 8),)),
        "ancestors": draw_ancestors(jax.random.fold_in(keys[13], 71), 0),
        "filled_extents": draw_filled_extents(jax.random.fold_in(keys[13], 71), 0),
        "out_weight": gaussian(keys[7], (H * HD, D), (H * HD) ** -0.5, 0.046875, ((0, 8), (1, 16))),
        "residual": gaussian(keys[8], (NODES, D), 1.0, 6.0, ((1, 16),)),
        "norm_gain": jnp.clip(1.0 + 0.18 * jax.random.normal(keys[9], (D,), jnp.float32), 0.099609375, 1.8984375).astype(jnp.bfloat16),
        "vocab_weight": draw_vocab_weight(jax.random.fold_in(keys[13], 71), 0),
        "candidates": place_ends(jax.random.randint(keys[11], (NODES,), 0, V), jax.random.fold_in(keys[11], 1), 0, V - 1).astype(jnp.int32),
        "amateur": jnp.clip(jax.random.uniform(keys[12], (NODES,), jnp.float32, -12.0, -1.0), -12.0, -1.0),
    }


NEG_FILL = -1e+30
EPSILON = 1e-05
HIGH = lax.Precision.HIGHEST

def separate_channel_blend(asking_embeddings, stored_lookup_entries, stored_content_entries, guessed_branch_lookups, guessed_branch_contents, entry_validity, lineage_visibility_filter):
    score_scale = HD ** (-0.5)
    query_f = asking_embeddings.astype(jnp.float32)
    cached = jnp.einsum('ngd,pd->gnp', query_f, stored_lookup_entries.astype(jnp.float32), precision=HIGH) * score_scale
    local_tree = jnp.einsum('ngd,jd->gnj', query_f, guessed_branch_lookups.astype(jnp.float32), precision=HIGH) * score_scale
    valid_stored_indices = entry_validity[None, None, :]
    live_t = (lineage_visibility_filter > 0)[None, :, :]
    cached = jnp.where(valid_stored_indices, cached, NEG_FILL)
    local_tree = jnp.where(live_t, local_tree, NEG_FILL)
    highest = jnp.maximum(cached.max(-1), local_tree.max(-1))
    weight_c = jnp.where(valid_stored_indices, jnp.exp(cached - highest[..., None]), 0.0)
    weight_t = jnp.where(live_t, jnp.exp(local_tree - highest[..., None]), 0.0)
    weight_sum = weight_c.sum(-1) + weight_t.sum(-1)
    summed = jnp.einsum('gnp,pd->gnd', weight_c.astype(jnp.bfloat16).astype(jnp.float32), stored_content_entries.astype(jnp.float32), precision=HIGH)
    summed = summed + jnp.einsum('gnj,jd->gnd', weight_t.astype(jnp.bfloat16).astype(jnp.float32), guessed_branch_contents.astype(jnp.float32), precision=HIGH)
    return summed / weight_sum[..., None]

def reference(queries, cache_keys, cache_values, tree_keys, tree_values, ancestors, filled_extents, out_weight, residual, norm_gain, vocab_weight, candidates, amateur):
    group_size = H // KVH

    def one_item(item):
        sequence_ordinal = (item // KVH).astype(jnp.int32)
        kv_head = (item % KVH).astype(jnp.int32)
        row0 = (sequence_ordinal * NODES_REQ).astype(jnp.int32)
        asking_embeddings = lax.dynamic_slice(queries, (row0, (kv_head * group_size * HD).astype(jnp.int32)), (NODES_REQ, group_size * HD)).reshape(NODES_REQ, group_size, HD)
        zero = jnp.zeros((), jnp.int32)
        stored_lookup_entries = lax.dynamic_slice(cache_keys, (sequence_ordinal, zero, (kv_head * HD).astype(jnp.int32)), (1, STORE_LIMIT, HD))[0]
        stored_content_entries = lax.dynamic_slice(cache_values, (sequence_ordinal, zero, (kv_head * HD).astype(jnp.int32)), (1, STORE_LIMIT, HD))[0]
        guessed_branch_lookups = lax.dynamic_slice(tree_keys, (row0, (kv_head * HD).astype(jnp.int32)), (NODES_REQ, HD))
        guessed_branch_contents = lax.dynamic_slice(tree_values, (row0, (kv_head * HD).astype(jnp.int32)), (NODES_REQ, HD))
        entry_validity = jnp.arange(STORE_LIMIT, dtype=jnp.int32) < filled_extents[sequence_ordinal]
        lineage_visibility_filter = ancestors[sequence_ordinal]
        blended_result_matrix = separate_channel_blend(asking_embeddings, stored_lookup_entries, stored_content_entries, guessed_branch_lookups, guessed_branch_contents, entry_validity, lineage_visibility_filter)
        return blended_result_matrix.transpose(1, 0, 2).reshape(NODES_REQ, group_size * HD)
    pieces = lax.map(one_item, jnp.arange(REQUESTS * KVH, dtype=jnp.int32))
    attended = pieces.reshape(REQUESTS, KVH, NODES_REQ, group_size * HD).transpose(0, 2, 1, 3).reshape(NODES, H * HD).astype(jnp.bfloat16)
    projected = jnp.dot(attended, out_weight, preferred_element_type=jnp.float32)
    hidden = (residual.astype(jnp.float32) + projected).astype(jnp.bfloat16)
    hidden_f = hidden.astype(jnp.float32)
    mean_sq = lax.optimization_barrier(jnp.mean(hidden_f * hidden_f, axis=1))
    normed = (hidden_f * lax.rsqrt(mean_sq + EPSILON)[:, None] * norm_gain.astype(jnp.float32)).astype(jnp.bfloat16)
    logits = jnp.dot(normed, vocab_weight, preferred_element_type=jnp.float32)
    peak_logit = logits.max(axis=1)
    log_total = peak_logit + jnp.log(lax.optimization_barrier(jnp.sum(jnp.exp(logits - peak_logit[:, None]), axis=1)))
    chosen = jnp.take_along_axis(logits, candidates[:, None].astype(jnp.int32), axis=1)[:, 0]
    contrast = chosen - log_total - amateur
    return (hidden, contrast)
```

```python
import math

import jax
import jax.numpy as jnp
from jax import lax
from jax.experimental import pallas as pl
from jax.experimental.pallas import tpu as pltpu
from jax.sharding import Mesh, PartitionSpec as P

NODES_REQ = 64
NODES = 128
D = 16384
HD = 128
EPSILON = 1e-05
NEG_FILL = -1e30
LOG2E = math.log2(math.e)
SCALE2 = HD ** (-0.5) * LOG2E

SEQ = ("zh", "y", "c")
HEAD = ("x", "zl")
CHIPS = ("zh", "y", "x", "zl")
ALL = SEQ + HEAD


F32 = jnp.float32
BF16 = jnp.bfloat16
VM = pltpu.VMEM
STAT_ROWS = 16
BLOCK_ROWS = 256
CHUNK = 1024


def nt_dot(a, b):
    return lax.dot_general(a, b, (((1,), (1,)), ((), ())), preferred_element_type=F32)


def thirds(x):
    hi = x.astype(BF16).astype(F32)
    rest = x - hi
    mid = rest.astype(BF16).astype(F32)
    return hi, mid, rest - mid


def attention(queries, keys, values, extents, first):
    requests, positions, _ = keys.shape
    heads = queries.shape[1] // HD
    per_block = BLOCK_ROWS // NODES_REQ
    blocks_req = heads // per_block
    blocks = requests * blocks_req
    chunks = positions // CHUNK

    def kernel(ext_ref, first_ref, q_ref, k_hbm, v_hbm, o_ref, qs, kv, vv, bias, s_buf, m_buf, l_buf, acc, stat, sem):
        copies = []
        for b in range(requests):
            copies.append(
                (
                    pltpu.make_async_copy(k_hbm.at[b], kv.at[b], sem.at[2 * b]),
                    pltpu.make_async_copy(v_hbm.at[b], vv.at[b], sem.at[2 * b + 1]),
                )
            )
        for pair in copies:
            for copy in pair:
                copy.start()
        lane = lax.broadcasted_iota(jnp.int32, (8, positions), 1)
        for b in range(requests):
            left = ext_ref[b] - first_ref[0]
            bias[b] = jnp.where(lane < left, 0.0, NEG_FILL).astype(F32)
            for g in range(heads):
                qs[b * blocks_req + g // per_block, (g % per_block) * NODES_REQ : (g % per_block + 1) * NODES_REQ, :] = (
                    q_ref[b * NODES_REQ : (b + 1) * NODES_REQ, g * HD : (g + 1) * HD]
                )
        stat[...] = jnp.zeros_like(stat)

        def scores(block, chunk, slot):
            b = block // blocks_req
            at = pl.multiple_of(chunk * CHUNK, CHUNK)
            s = nt_dot(qs[block], kv[b, pl.ds(at, CHUNK), :])
            best = m_buf[slot]
            for t in range(CHUNK // 128):
                piece = s[:, t * 128 : (t + 1) * 128]
                shift = bias[b, :, pl.ds(pl.multiple_of(at + t * 128, 128), 128)]
                piece = (piece.reshape(BLOCK_ROWS // 8, 8, 128) + shift[None]).reshape(BLOCK_ROWS, 128)
                s_buf[slot, chunk, :, t * 128 : (t + 1) * 128] = piece
                best = jnp.maximum(best, piece)
            m_buf[slot] = best

        def weigh(block, chunk, slot, top):
            b = block // blocks_req
            at = pl.multiple_of(chunk * CHUNK, CHUNK)
            total = l_buf[...]
            pieces = []
            for t in range(CHUNK // 128):
                w = jnp.exp2(s_buf[slot, chunk, :, t * 128 : (t + 1) * 128] * SCALE2 - top)
                total = total + w
                pieces.append(w.astype(BF16))
            l_buf[...] = total
            acc[...] += jnp.dot(
                jnp.concatenate(pieces, axis=1), vv[b, pl.ds(at, CHUNK), :], preferred_element_type=F32
            )

        copies[0][0].wait()
        m_buf[0] = jnp.full((BLOCK_ROWS, 128), NEG_FILL, F32)

        @pl.loop(0, chunks)
        def _(chunk):
            scores(0, chunk, 0)

        def finish(block, best):
            total = jnp.sum(l_buf[...], axis=1, keepdims=True)
            b = block // blocks_req
            j = block % blocks_req
            slots = lax.broadcasted_iota(jnp.int32, (NODES_REQ, 128), 1)
            row = pl.multiple_of(b * NODES_REQ, NODES_REQ)
            held = stat[pl.ds(row, NODES_REQ), :]
            for i in range(per_block):
                g = j * per_block + i
                part = slice(i * NODES_REQ, (i + 1) * NODES_REQ)
                o_ref[g, pl.ds(row, NODES_REQ), :] = acc[part, :].astype(BF16)
                for n, column in enumerate(thirds(best[part]) + thirds(total[part])):
                    held = jnp.where(slots == g * 8 + n, column, held)
            stat[pl.ds(row, NODES_REQ), :] = held

        def step(block, last):
            slot = block % 2
            best = jnp.max(m_buf[slot], axis=1, keepdims=True)
            best = jnp.maximum(best, 0.5 * NEG_FILL) * SCALE2
            top = jnp.broadcast_to(best, (BLOCK_ROWS, 128))
            l_buf[...] = jnp.zeros_like(l_buf)
            acc[...] = jnp.zeros_like(acc)
            if not last:
                m_buf[1 - slot] = jnp.full((BLOCK_ROWS, 128), NEG_FILL, F32)

            @pl.loop(0, chunks)
            def _(chunk):
                if not last:
                    scores(block + 1, chunk, 1 - slot)
                weigh(block, chunk, slot, top)

            finish(block, best)

        copies[0][1].wait()
        for b in range(requests):
            end = (b + 1) * blocks_req - 1

            @pl.loop(b * blocks_req, end)
            def _(block):
                step(block, False)

            if b + 1 < requests:
                copies[b + 1][0].wait()
                copies[b + 1][1].wait()
                step(end, False)
            else:
                step(end, True)

        turned = stat[...].T
        for g in range(heads):
            o_ref[g, NODES : NODES + STAT_ROWS, :] = jnp.concatenate(
                [turned[g * 8 : (g + 1) * 8, :], jnp.zeros((STAT_ROWS - 8, NODES), F32)], axis=0
            ).astype(BF16)

    smem = pl.BlockSpec(memory_space=pltpu.SMEM)
    vmem = pl.BlockSpec(memory_space=pltpu.VMEM)
    return pl.pallas_call(
        kernel,
        out_shape=jax.ShapeDtypeStruct((heads, NODES + STAT_ROWS, HD), BF16),
        in_specs=[smem, smem, vmem, pl.BlockSpec(memory_space=pl.ANY), pl.BlockSpec(memory_space=pl.ANY)],
        out_specs=vmem,
        scratch_shapes=[
            VM((blocks, BLOCK_ROWS, HD), BF16),
            VM((requests, positions, HD), BF16),
            VM((requests, positions, HD), BF16),
            VM((requests, 8, positions), F32),
            VM((2, chunks, BLOCK_ROWS, CHUNK), F32),
            VM((2, BLOCK_ROWS, 128), F32),
            VM((BLOCK_ROWS, 128), F32),
            VM((BLOCK_ROWS, HD), F32),
            VM((NODES, 128), F32),
            pltpu.SemaphoreType.DMA((2 * requests,)),
        ],
        compiler_params=pltpu.CompilerParams(vmem_limit_bytes=32 << 20),
        cost_estimate=pl.CostEstimate(
            flops=4 * NODES * heads * positions * HD, transcendentals=NODES * heads * positions, bytes_accessed=5 << 20
        ),
        name="attention",
    )(extents, first, queries, keys, values)


def tree_part(queries, tree_keys, tree_values, ancestors, head):
    requests = ancestors.shape[0]

    def kernel(head_ref, q_ref, k_ref, v_ref, a_ref, o_ref, st_ref):
        at = pl.multiple_of(head_ref[0] * HD, HD)
        slots = lax.broadcasted_iota(jnp.int32, (NODES_REQ, 128), 1)
        for b in range(requests):
            rows = slice(b * NODES_REQ, (b + 1) * NODES_REQ)
            s = nt_dot(q_ref[rows, pl.ds(at, HD)], k_ref[rows, :])
            live = a_ref[b] > 0
            s = jnp.where(live, s * SCALE2, NEG_FILL)
            top = jnp.max(s, axis=1, keepdims=True)
            w = jnp.where(live, jnp.exp2(s - top), 0.0)
            total = jnp.sum(w, axis=1, keepdims=True)
            o_ref[rows, :] = jnp.dot(w.astype(BF16), v_ref[rows, :], preferred_element_type=F32)
            st_ref[rows, :] = jnp.where(slots == 0, top, jnp.where(slots == 1, total, 0.0))
        st_ref[...] = st_ref[...].T

    vmem = pl.BlockSpec(memory_space=pltpu.VMEM)
    return pl.pallas_call(
        kernel,
        out_shape=(jax.ShapeDtypeStruct((NODES, HD), F32), jax.ShapeDtypeStruct((128, NODES), F32)),
        in_specs=[pl.BlockSpec(memory_space=pltpu.SMEM)] + [vmem] * 4,
        out_specs=(vmem, vmem),
        compiler_params=pltpu.CompilerParams(vmem_limit_bytes=8 << 20),
        cost_estimate=pl.CostEstimate(flops=1 << 22, transcendentals=8192, bytes_accessed=1 << 20),
        name="tree_part",
    )(head, queries, tree_keys, tree_values, ancestors)


def combine(parts, tree_sums, tree_stats):
    sources = parts.shape[0]

    def kernel(p_ref, t_ref, ts_ref, o_ref):
        tops = []
        totals = []
        for s in range(sources):
            st = p_ref[s, NODES : NODES + STAT_ROWS, :].astype(F32)
            tops.append(st[0:1] + st[1:2] + st[2:3])
            totals.append(st[3:4] + st[4:5] + st[5:6])
        tops.append(ts_ref[0:1, :])
        totals.append(ts_ref[1:2, :])
        tops = jnp.concatenate(tops + [jnp.full((24 - sources - 1, NODES), NEG_FILL, F32)], axis=0)
        totals = jnp.concatenate(totals + [jnp.zeros((24 - sources - 1, NODES), F32)], axis=0)
        best = jnp.max(tops, axis=0, keepdims=True)
        factor = jnp.exp2(tops - best)
        factor = factor / jnp.sum(factor * totals, axis=0, keepdims=True)
        factor = jnp.concatenate([factor, jnp.zeros((128 - 24, NODES), F32)], axis=0).T
        out = t_ref[...] * factor[:, sources : sources + 1]
        for s in range(sources):
            out = out + p_ref[s, 0:NODES, :].astype(F32) * factor[:, s : s + 1]
        out = out.astype(BF16)
        for s in range(sources):
            o_ref[s] = out

    vmem = pl.BlockSpec(memory_space=pltpu.VMEM)
    return pl.pallas_call(
        kernel,
        out_shape=jax.ShapeDtypeStruct((sources, NODES, HD), BF16),
        in_specs=[vmem] * 3,
        out_specs=vmem,
        compiler_params=pltpu.CompilerParams(vmem_limit_bytes=8 << 20),
        cost_estimate=pl.CostEstimate(flops=1 << 20, transcendentals=4096, bytes_accessed=1 << 20),
        name="combine",
    )(parts, tree_sums, tree_stats)


def project(attended, weight):
    heads = attended.shape[0]
    rows, columns = weight.shape
    width = 256

    def kernel(a_ref, w_ref, o_ref):
        x = jnp.concatenate([a_ref[g] for g in range(heads)], axis=1)
        y = jnp.dot(x, w_ref[...], preferred_element_type=F32).astype(BF16)
        for i in range(width // 128):
            o_ref[i] = y[:, i * 128 : (i + 1) * 128]

    return pl.pallas_call(
        kernel,
        out_shape=jax.ShapeDtypeStruct((columns // 128, NODES, 128), BF16),
        grid=(columns // width,),
        in_specs=[
            pl.BlockSpec((heads, NODES, HD), lambda i: (0, 0, 0)),
            pl.BlockSpec((rows, width), lambda i: (0, i)),
        ],
        out_specs=pl.BlockSpec((width // 128, NODES, 128), lambda i: (i, 0, 0)),
        compiler_params=pltpu.CompilerParams(vmem_limit_bytes=12 << 20),
        cost_estimate=pl.CostEstimate(flops=2 * NODES * rows * columns, transcendentals=0, bytes_accessed=5 << 20),
        name="project",
    )(attended, weight)


def finish_hidden(shares, residual, position, copies):
    sources = shares.shape[0]

    def kernel(pos_ref, s_ref, r_ref, h_ref, o_ref):
        at = pl.multiple_of(pos_ref[0] * 128, 128)
        total = s_ref[0].astype(F32)
        for s in range(1, sources):
            total = total + s_ref[s].astype(F32)
        h = (r_ref[:, pl.ds(at, 128)].astype(F32) + total).astype(BF16)
        h_ref[...] = h
        for i in range(copies):
            o_ref[i] = h

    vmem = pl.BlockSpec(memory_space=pltpu.VMEM)
    return pl.pallas_call(
        kernel,
        out_shape=(
            jax.ShapeDtypeStruct((NODES, 128), BF16),
            jax.ShapeDtypeStruct((copies, NODES, 128), BF16),
        ),
        in_specs=[pl.BlockSpec(memory_space=pltpu.SMEM), vmem, vmem],
        out_specs=(vmem, vmem),
        compiler_params=pltpu.CompilerParams(vmem_limit_bytes=8 << 20),
        cost_estimate=pl.CostEstimate(flops=1 << 18, transcendentals=0, bytes_accessed=3 << 20),
        name="finish_hidden",
    )(position, shares, residual)


def vocab_blocks(side_ref, h_ref, g_ref, w_ref, blocks):
    pieces = []
    squares = jnp.zeros((NODES, 128), F32)
    for i in range(blocks):
        h = h_ref[i].astype(F32)
        squares = squares + h * h
        pieces.append((h * g_ref[0, 0, i : i + 1, :].astype(F32)).astype(BF16))
    x = jnp.concatenate(pieces, axis=1)
    return jnp.dot(x, w_ref[0, 0], preferred_element_type=F32), squares


def vocab_specs(blocks, span, columns):
    return [
        pl.BlockSpec((blocks, NODES, 128), lambda i, side: (i, 0, 0)),
        pl.BlockSpec((1, 1, blocks, 128), lambda i, side: (i, side[0], 0, 0)),
        pl.BlockSpec((1, 1, span, columns), lambda i, side: (i, side[0], 0, 0)),
    ]


def vocab_first(side, hidden, gain, weight):
    groups, _, span, columns = weight.shape
    blocks = span // 128

    def kernel(side_ref, h_ref, g_ref, w_ref, y_ref, sq_ref):
        y, squares = vocab_blocks(side_ref, h_ref, g_ref, w_ref, blocks)

        @pl.when(pl.program_id(0) == 0)
        def _():
            y_ref[...] = y
            sq_ref[...] = squares

        @pl.when(pl.program_id(0) > 0)
        def _():
            y_ref[...] += y
            sq_ref[...] += squares

    return pl.pallas_call(
        kernel,
        out_shape=(jax.ShapeDtypeStruct((NODES, columns), F32), jax.ShapeDtypeStruct((NODES, 128), F32)),
        grid_spec=pltpu.PrefetchScalarGridSpec(
            num_scalar_prefetch=1,
            grid=(groups,),
            in_specs=vocab_specs(blocks, span, columns),
            out_specs=(
                pl.BlockSpec((NODES, columns), lambda i, side: (0, 0)),
                pl.BlockSpec((NODES, 128), lambda i, side: (0, 0)),
            ),
        ),
        compiler_params=pltpu.CompilerParams(vmem_limit_bytes=12 << 20),
        cost_estimate=pl.CostEstimate(
            flops=2 * NODES * groups * span * columns, transcendentals=0, bytes_accessed=10 << 20
        ),
        name="vocab_first",
    )(side, hidden, gain, weight)


def vocab_second(side, hidden, gain, weight, y_first, sq_first, target, copies):
    groups, _, span, columns = weight.shape
    blocks = span // 128

    def kernel(side_ref, h_ref, g_ref, w_ref, y0_ref, sq0_ref, t_ref, o_ref, acc, sq):
        y, squares = vocab_blocks(side_ref, h_ref, g_ref, w_ref, blocks)

        @pl.when(pl.program_id(0) == 0)
        def _():
            acc[...] = y0_ref[...] + y
            sq[...] = sq0_ref[...] + squares

        @pl.when(pl.program_id(0) > 0)
        def _():
            acc[...] += y
            sq[...] += squares

        @pl.when(pl.program_id(0) == groups - 1)
        def _():
            mean = jnp.sum(sq[...], axis=1, keepdims=True) / D
            logits = acc[...] * lax.rsqrt(mean + EPSILON)
            peak = jnp.max(logits, axis=1, keepdims=True)
            total = jnp.sum(jnp.exp(logits - peak), axis=1, keepdims=True)
            lse = peak + jnp.log(total)
            column = lax.broadcasted_iota(jnp.int32, (NODES, columns), 1)
            chosen = jnp.sum(jnp.where(column == t_ref[...], logits, 0.0), axis=1, keepdims=True)
            lane = lax.broadcasted_iota(jnp.int32, (NODES, 128), 1)
            rows = jnp.where(lane == 0, lse, jnp.where(lane == 1, chosen, 0.0)).T
            for i in range(copies):
                o_ref[i] = rows[0:8, :]

    return pl.pallas_call(
        kernel,
        out_shape=jax.ShapeDtypeStruct((copies, 8, NODES), F32),
        grid_spec=pltpu.PrefetchScalarGridSpec(
            num_scalar_prefetch=1,
            grid=(groups,),
            in_specs=vocab_specs(blocks, span, columns)
            + [
                pl.BlockSpec((NODES, columns), lambda i, side: (0, 0)),
                pl.BlockSpec((NODES, 128), lambda i, side: (0, 0)),
                pl.BlockSpec((NODES, 1), lambda i, side: (0, 0)),
            ],
            out_specs=pl.BlockSpec((copies, 8, NODES), lambda i, side: (0, 0, 0)),
            scratch_shapes=[VM((NODES, columns), F32), VM((NODES, 128), F32)],
        ),
        compiler_params=pltpu.CompilerParams(vmem_limit_bytes=12 << 20),
        cost_estimate=pl.CostEstimate(
            flops=2 * NODES * groups * span * columns, transcendentals=1 << 16, bytes_accessed=10 << 20
        ),
        name="vocab_second",
    )(side, hidden, gain, weight, y_first, sq_first, target)


def final_score(stats, amateur):
    def kernel(s_ref, a_ref, o_ref):
        lse = s_ref[:, 0, :]
        chosen = s_ref[:, 1, :]
        best = jnp.max(lse, axis=0, keepdims=True)
        total = jnp.sum(jnp.exp(lse - best), axis=0, keepdims=True)
        picked = jnp.sum(chosen, axis=0, keepdims=True)
        o_ref[...] = picked - (best + jnp.log(total)) - a_ref[...]

    vmem = pl.BlockSpec(memory_space=pltpu.VMEM)
    return pl.pallas_call(
        kernel,
        out_shape=jax.ShapeDtypeStruct((1, NODES), F32),
        in_specs=[vmem, vmem],
        out_specs=vmem,
        compiler_params=pltpu.CompilerParams(vmem_limit_bytes=8 << 20),
        name="final_score",
    )(stats, amateur)


def body(
    queries,
    cache_keys,
    cache_values,
    tree_keys,
    tree_values,
    ancestors,
    filled_extents,
    out_weight,
    residual,
    norm_gain,
    vocab_weight,
    candidates,
    amateur,
):
    positions = cache_keys.shape[1]
    seq_index = lax.axis_index(SEQ)
    head_index = lax.axis_index(HEAD)
    core = lax.axis_index("c")
    seq_size = lax.axis_size(SEQ)
    cores = lax.axis_size("c")
    chips = lax.axis_size(CHIPS)
    devices = chips * cores

    def scalar(x):
        return x.astype(jnp.int32).reshape(1)

    parts = attention(queries, cache_keys, cache_values, filled_extents, scalar(seq_index * positions))
    parts = lax.all_to_all(parts, SEQ, 0, 0, tiled=True)
    tree_sums, tree_stats = tree_part(queries, tree_keys, tree_values, ancestors, scalar(seq_index))
    attended = combine(parts, tree_sums, tree_stats)
    attended = lax.all_to_all(attended, SEQ, 0, 0, tiled=True)
    shares = project(attended, out_weight)
    shares = lax.all_to_all(shares, HEAD, 0, 0, tiled=True)
    hidden, repeated = finish_hidden(shares, residual, scalar(head_index), chips)
    own_side = lax.all_to_all(repeated, CHIPS, 0, 0, tiled=True)
    other_side = lax.ppermute(own_side, "c", [(0, 1), (1, 0)])
    vocab_local = vocab_weight.shape[1]
    groups = seq_size // cores
    span = D // seq_size
    weight = vocab_weight.reshape(groups, cores, span, vocab_local)
    gain = norm_gain.reshape(groups, cores, span // 128, 128)
    y, squares = vocab_first(scalar(core), own_side, gain, weight)
    target = (candidates - lax.axis_index(ALL) * vocab_local).reshape(NODES, 1)
    stats = vocab_second(scalar(1 - core), other_side, gain, weight, y, squares, target, devices)
    stats = lax.all_to_all(stats, ALL, 0, 0, tiled=True)
    contrast = final_score(stats, amateur.reshape(1, NODES))
    return (hidden, contrast.reshape(NODES))


def solution(mesh):
    fine = Mesh(mesh.devices.reshape(2, 4, 2, 4, 2), ALL)
    in_specs = (
        P(None, HEAD),
        P(None, SEQ, HEAD),
        P(None, SEQ, HEAD),
        P(None, HEAD),
        P(None, HEAD),
        P(),
        P(),
        P(HEAD, SEQ),
        P(None, SEQ),
        P(),
        P(None, ALL),
        P(),
        P(),
    )
    out_specs = (P(None, ALL), P())
    return jax.shard_map(body, mesh=fine, in_specs=in_specs, out_specs=out_specs, check_vma=False)
```

```python
import math

import jax
import jax.numpy as jnp
from jax import lax
from jax.experimental import pallas as pl
from jax.experimental.pallas import tpu as pltpu
from jax.sharding import Mesh, PartitionSpec as P

NODES_REQ = 64
NODES = 128
D = 16384
HD = 128
EPSILON = 1e-05
NEG_FILL = -1e30
LOG2E = math.log2(math.e)
SCALE2 = HD ** (-0.5) * LOG2E

SEQ = ("zh", "y", "c")
HEAD = ("x", "zl")
ROWS = ("zh", "y")
CHIPS = ("zh", "y", "x", "zl")
ALL = SEQ + HEAD


F32 = jnp.float32
BF16 = jnp.bfloat16
VM = pltpu.VMEM
STAT_ROWS = 16
BLOCK_ROWS = 256
CHUNK = 1024


def nt_dot(a, b):
    return lax.dot_general(a, b, (((1,), (1,)), ((), ())), preferred_element_type=F32)


def thirds(x):
    hi = x.astype(BF16).astype(F32)
    rest = x - hi
    mid = rest.astype(BF16).astype(F32)
    return hi, mid, rest - mid


def attention(queries, keys, values, extents, place):
    requests, positions, _ = keys.shape
    heads = queries.shape[1] // HD
    per_block = BLOCK_ROWS // NODES_REQ
    blocks_req = heads // per_block
    blocks = requests * blocks_req
    chunks = positions // CHUNK

    half = heads // 2

    def kernel(ext_ref, place_ref, q_hbm, k_hbm, v_hbm, keep, send, q_ref, qs, kv, vv, bias, s_buf, m_buf, l_buf, acc, stat, sem):
        q_copy = pltpu.make_async_copy(q_hbm, q_ref, sem.at[2 * requests])
        q_copy.start()
        core = place_ref[1]
        copies = []
        for b in range(requests):
            copies.append(
                (
                    pltpu.make_async_copy(k_hbm.at[b], kv.at[b], sem.at[2 * b]),
                    pltpu.make_async_copy(v_hbm.at[b], vv.at[b], sem.at[2 * b + 1]),
                )
            )
        for pair in copies:
            for copy in pair:
                copy.start()
        lane = lax.broadcasted_iota(jnp.int32, (8, positions), 1)
        for b in range(requests):
            left = ext_ref[b] - place_ref[0]
            bias[b] = jnp.where(lane < left, 0.0, NEG_FILL).astype(F32)
        stat[...] = jnp.zeros_like(stat)
        q_copy.wait()
        for g in range(heads):
            head = 2 * g + core if g < half else 2 * (g - half) + 1 - core
            at = pl.multiple_of(head * HD, HD)
            for b in range(requests):
                qs[b * blocks_req + g // per_block, (g % per_block) * NODES_REQ : (g % per_block + 1) * NODES_REQ, :] = (
                    q_ref[b * NODES_REQ : (b + 1) * NODES_REQ, pl.ds(at, HD)]
                )

        def scores(block, chunk, slot):
            b = block // blocks_req
            at = pl.multiple_of(chunk * CHUNK, CHUNK)
            s = nt_dot(qs[block], kv[b, pl.ds(at, CHUNK), :])
            best = m_buf[slot]
            for t in range(CHUNK // 128):
                piece = s[:, t * 128 : (t + 1) * 128]
                shift = bias[b, :, pl.ds(pl.multiple_of(at + t * 128, 128), 128)]
                piece = (piece.reshape(BLOCK_ROWS // 8, 8, 128) + shift[None]).reshape(BLOCK_ROWS, 128)
                s_buf[slot, chunk, :, t * 128 : (t + 1) * 128] = piece
                best = jnp.maximum(best, piece)
            m_buf[slot] = best

        def weigh(block, chunk, slot, top):
            b = block // blocks_req
            at = pl.multiple_of(chunk * CHUNK, CHUNK)
            total = l_buf[...]
            pieces = []
            for t in range(CHUNK // 128):
                w = jnp.exp2(s_buf[slot, chunk, :, t * 128 : (t + 1) * 128] * SCALE2 - top)
                total = total + w
                pieces.append(w.astype(BF16))
            l_buf[...] = total
            acc[...] += jnp.dot(
                jnp.concatenate(pieces, axis=1), vv[b, pl.ds(at, CHUNK), :], preferred_element_type=F32
            )

        copies[0][0].wait()
        m_buf[0] = jnp.full((BLOCK_ROWS, 128), NEG_FILL, F32)

        @pl.loop(0, chunks)
        def _(chunk):
            scores(0, chunk, 0)

        def finish(block, best):
            total = jnp.sum(l_buf[...], axis=1, keepdims=True)
            b = block // blocks_req
            j = block % blocks_req
            slots = lax.broadcasted_iota(jnp.int32, (NODES_REQ, 128), 1)
            rows = slice(b * NODES_REQ, (b + 1) * NODES_REQ)
            held = stat[rows, :]
            for i in range(per_block):
                g = j * per_block + i
                part = slice(i * NODES_REQ, (i + 1) * NODES_REQ)
                out = keep if g < half else send
                out[g % half, rows, :] = acc[part, :].astype(BF16)
                for n, column in enumerate(thirds(best[part]) + thirds(total[part])):
                    held = jnp.where(slots == g * 8 + n, column, held)
            stat[rows, :] = held

        for block in range(blocks):
            last = block == blocks - 1
            slot = block % 2
            if block % blocks_req == 0:
                copies[block // blocks_req][1].wait()
            if not last and (block + 1) % blocks_req == 0:
                copies[(block + 1) // blocks_req][0].wait()
            best = jnp.max(m_buf[slot], axis=1, keepdims=True)
            best = jnp.maximum(best, 0.5 * NEG_FILL) * SCALE2
            top = jnp.broadcast_to(best, (BLOCK_ROWS, 128))
            l_buf[...] = jnp.zeros_like(l_buf)
            acc[...] = jnp.zeros_like(acc)
            if not last:
                m_buf[1 - slot] = jnp.full((BLOCK_ROWS, 128), NEG_FILL, F32)

            @pl.loop(0, chunks)
            def _(chunk):
                if not last:
                    scores(block + 1, chunk, 1 - slot)
                weigh(block, chunk, slot, top)

            finish(block, best)

        turned = stat[...].T
        for g in range(heads):
            out = keep if g < half else send
            out[g % half, NODES : NODES + STAT_ROWS, :] = jnp.concatenate(
                [turned[g * 8 : (g + 1) * 8, :], jnp.zeros((STAT_ROWS - 8, NODES), F32)], axis=0
            ).astype(BF16)

    smem = pl.BlockSpec(memory_space=pltpu.SMEM)
    vmem = pl.BlockSpec(memory_space=pltpu.VMEM)
    hbm = pl.BlockSpec(memory_space=pltpu.HBM)
    out = jax.ShapeDtypeStruct((half, NODES + STAT_ROWS, HD), BF16)
    return pl.pallas_call(
        kernel,
        out_shape=(out, out),
        in_specs=[smem, smem, hbm, hbm, hbm],
        out_specs=(vmem, vmem),
        scratch_shapes=[
            VM((NODES, heads * HD), BF16),
            VM((blocks, BLOCK_ROWS, HD), BF16),
            VM((requests, positions, HD), BF16),
            VM((requests, positions, HD), BF16),
            VM((requests, 8, positions), F32),
            VM((2, chunks, BLOCK_ROWS, CHUNK), F32),
            VM((2, BLOCK_ROWS, 128), F32),
            VM((BLOCK_ROWS, 128), F32),
            VM((BLOCK_ROWS, HD), F32),
            VM((NODES, 128), F32),
            pltpu.SemaphoreType.DMA((2 * requests + 1,)),
        ],
        compiler_params=pltpu.CompilerParams(vmem_limit_bytes=32 << 20),
        cost_estimate=pl.CostEstimate(
            flops=4 * NODES * heads * positions * HD, transcendentals=NODES * heads * positions, bytes_accessed=5 << 20
        ),
        name="attention",
    )(extents, place, queries, keys, values)


def tree_part(queries, tree_keys, tree_values, ancestors, head):
    requests = ancestors.shape[0]

    def kernel(head_ref, q_ref, k_ref, v_ref, a_ref, o_ref, st_ref):
        at = pl.multiple_of(head_ref[0] * HD, HD)
        slots = lax.broadcasted_iota(jnp.int32, (NODES_REQ, 128), 1)
        for b in range(requests):
            rows = slice(b * NODES_REQ, (b + 1) * NODES_REQ)
            s = nt_dot(q_ref[rows, pl.ds(at, HD)], k_ref[rows, :])
            live = a_ref[b] > 0
            s = jnp.where(live, s * SCALE2, NEG_FILL)
            top = jnp.max(s, axis=1, keepdims=True)
            w = jnp.where(live, jnp.exp2(s - top), 0.0)
            total = jnp.sum(w, axis=1, keepdims=True)
            o_ref[rows, :] = jnp.dot(w.astype(BF16), v_ref[rows, :], preferred_element_type=F32)
            st_ref[rows, :] = jnp.where(slots == 0, top, jnp.where(slots == 1, total, 0.0))
        st_ref[...] = st_ref[...].T

    vmem = pl.BlockSpec(memory_space=pltpu.VMEM)
    return pl.pallas_call(
        kernel,
        out_shape=(jax.ShapeDtypeStruct((NODES, HD), F32), jax.ShapeDtypeStruct((128, NODES), F32)),
        in_specs=[pl.BlockSpec(memory_space=pltpu.SMEM)] + [vmem] * 4,
        out_specs=(vmem, vmem),
        compiler_params=pltpu.CompilerParams(vmem_limit_bytes=8 << 20),
        cost_estimate=pl.CostEstimate(flops=1 << 22, transcendentals=8192, bytes_accessed=1 << 20),
        name="tree_part",
    )(head, queries, tree_keys, tree_values, ancestors)


def merge(first, second):
    heads = first.shape[0]

    def kernel(a_ref, b_ref, o_ref):
        rows = []
        columns = []
        for g in range(heads):
            a = a_ref[g, NODES : NODES + STAT_ROWS, :].astype(F32)
            b = b_ref[g, NODES : NODES + STAT_ROWS, :].astype(F32)
            top_a = a[0:1] + a[1:2] + a[2:3]
            top_b = b[0:1] + b[1:2] + b[2:3]
            top = jnp.maximum(top_a, top_b)
            fa = jnp.exp2(top_a - top)
            fb = jnp.exp2(top_b - top)
            total = fa * (a[3:4] + a[4:5] + a[5:6]) + fb * (b[3:4] + b[4:5] + b[5:6])
            rows.append(jnp.concatenate(thirds(top) + thirds(total) + (jnp.zeros((STAT_ROWS - 6, NODES), F32),), axis=0))
            columns += [fa, fb]
        columns.append(jnp.zeros((128 - 2 * heads, NODES), F32))
        factor = jnp.concatenate(columns, axis=0).T
        for g in range(heads):
            o_ref[g, 0:NODES, :] = (
                a_ref[g, 0:NODES, :].astype(F32) * factor[:, 2 * g : 2 * g + 1]
                + b_ref[g, 0:NODES, :].astype(F32) * factor[:, 2 * g + 1 : 2 * g + 2]
            ).astype(BF16)
            o_ref[g, NODES : NODES + STAT_ROWS, :] = rows[g].astype(BF16)

    vmem = pl.BlockSpec(memory_space=pltpu.VMEM)
    return pl.pallas_call(
        kernel,
        out_shape=jax.ShapeDtypeStruct(first.shape, BF16),
        in_specs=[vmem] * 2,
        out_specs=vmem,
        compiler_params=pltpu.CompilerParams(vmem_limit_bytes=8 << 20),
        cost_estimate=pl.CostEstimate(flops=1 << 20, transcendentals=4096, bytes_accessed=1 << 20),
        name="merge",
    )(first, second)


def combine(parts, tree_sums, tree_stats):
    sources = parts.shape[0]

    def kernel(p_ref, t_ref, ts_ref, o_ref):
        tops = []
        totals = []
        for s in range(sources):
            st = p_ref[s, NODES : NODES + STAT_ROWS, :].astype(F32)
            tops.append(st[0:1] + st[1:2] + st[2:3])
            totals.append(st[3:4] + st[4:5] + st[5:6])
        tops.append(ts_ref[0:1, :])
        totals.append(ts_ref[1:2, :])
        tops = jnp.concatenate(tops + [jnp.full((24 - sources - 1, NODES), NEG_FILL, F32)], axis=0)
        totals = jnp.concatenate(totals + [jnp.zeros((24 - sources - 1, NODES), F32)], axis=0)
        best = jnp.max(tops, axis=0, keepdims=True)
        factor = jnp.exp2(tops - best)
        factor = factor / jnp.sum(factor * totals, axis=0, keepdims=True)
        factor = jnp.concatenate([factor, jnp.zeros((128 - 24, NODES), F32)], axis=0).T
        out = t_ref[...] * factor[:, sources : sources + 1]
        for s in range(sources):
            out = out + p_ref[s, 0:NODES, :].astype(F32) * factor[:, s : s + 1]
        out = out.astype(BF16)
        for s in range(sources):
            o_ref[s] = out

    vmem = pl.BlockSpec(memory_space=pltpu.VMEM)
    return pl.pallas_call(
        kernel,
        out_shape=jax.ShapeDtypeStruct((sources, NODES, HD), BF16),
        in_specs=[vmem] * 3,
        out_specs=vmem,
        compiler_params=pltpu.CompilerParams(vmem_limit_bytes=8 << 20),
        cost_estimate=pl.CostEstimate(flops=1 << 20, transcendentals=4096, bytes_accessed=1 << 20),
        name="combine",
    )(parts, tree_sums, tree_stats)


def project(side, attended, weight, so_far=None):
    heads = attended.shape[0]
    columns = weight.shape[3]
    width = 256
    rounded = so_far is not None

    def kernel(side_ref, a_ref, w_ref, *rest):
        x = jnp.concatenate([a_ref[g] for g in range(heads)], axis=1)
        y = jnp.dot(x, w_ref[:, 0].reshape(heads * HD, width), preferred_element_type=F32)
        if rounded:
            y = (y + rest[0][...]).astype(BF16)
            for i in range(width // 128):
                rest[1][i] = y[:, i * 128 : (i + 1) * 128]
        else:
            rest[0][...] = y

    wide = pl.BlockSpec((NODES, width), lambda i, side: (0, i))
    return pl.pallas_call(
        kernel,
        out_shape=jax.ShapeDtypeStruct((columns // 128, NODES, 128), BF16)
        if rounded
        else jax.ShapeDtypeStruct((NODES, columns), F32),
        grid_spec=pltpu.PrefetchScalarGridSpec(
            num_scalar_prefetch=1,
            grid=(columns // width,),
            in_specs=[
                pl.BlockSpec((heads, NODES, HD), lambda i, side: (0, 0, 0)),
                pl.BlockSpec((heads, 1, HD, width), lambda i, side: (0, side[0], 0, i)),
            ]
            + ([wide] if rounded else []),
            out_specs=pl.BlockSpec((width // 128, NODES, 128), lambda i, side: (i, 0, 0)) if rounded else wide,
        ),
        compiler_params=pltpu.CompilerParams(vmem_limit_bytes=12 << 20),
        cost_estimate=pl.CostEstimate(flops=2 * NODES * heads * HD * columns, transcendentals=0, bytes_accessed=3 << 20),
        name="project",
    )(side, attended, weight, *((so_far,) if rounded else ()))


def finish_hidden(shares, residual, position, copies):
    sources = shares.shape[0]

    def kernel(pos_ref, s_ref, r_ref, h_ref, o_ref):
        at = pl.multiple_of(pos_ref[0] * 128, 128)
        total = s_ref[0].astype(F32)
        for s in range(1, sources):
            total = total + s_ref[s].astype(F32)
        h = (r_ref[:, pl.ds(at, 128)].astype(F32) + total).astype(BF16)
        h_ref[...] = h
        for i in range(copies):
            o_ref[i] = h

    vmem = pl.BlockSpec(memory_space=pltpu.VMEM)
    return pl.pallas_call(
        kernel,
        out_shape=(
            jax.ShapeDtypeStruct((NODES, 128), BF16),
            jax.ShapeDtypeStruct((copies, NODES, 128), BF16),
        ),
        in_specs=[pl.BlockSpec(memory_space=pltpu.SMEM), vmem, vmem],
        out_specs=(vmem, vmem),
        compiler_params=pltpu.CompilerParams(vmem_limit_bytes=8 << 20),
        cost_estimate=pl.CostEstimate(flops=1 << 18, transcendentals=0, bytes_accessed=3 << 20),
        name="finish_hidden",
    )(position, shares, residual)


def vocab_blocks(side_ref, h_ref, g_ref, w_ref, blocks):
    pieces = []
    squares = jnp.zeros((NODES, 128), F32)
    for i in range(blocks):
        h = h_ref[i].astype(F32)
        squares = squares + h * h
        pieces.append((h * g_ref[0, 0, i : i + 1, :].astype(F32)).astype(BF16))
    x = jnp.concatenate(pieces, axis=1)
    return jnp.dot(x, w_ref[0, 0], preferred_element_type=F32), squares


def vocab_specs(blocks, span, columns):
    return [
        pl.BlockSpec((blocks, NODES, 128), lambda i, side: (i, 0, 0)),
        pl.BlockSpec((1, 1, blocks, 128), lambda i, side: (i, side[0], 0, 0)),
        pl.BlockSpec((1, 1, span, columns), lambda i, side: (i, side[0], 0, 0)),
    ]


def vocab_first(side, hidden, gain, weight):
    groups, _, span, columns = weight.shape
    blocks = span // 128

    def kernel(side_ref, h_ref, g_ref, w_ref, y_ref, sq_ref):
        y, squares = vocab_blocks(side_ref, h_ref, g_ref, w_ref, blocks)

        @pl.when(pl.program_id(0) == 0)
        def _():
            y_ref[...] = y
            sq_ref[...] = squares

        @pl.when(pl.program_id(0) > 0)
        def _():
            y_ref[...] += y
            sq_ref[...] += squares

    return pl.pallas_call(
        kernel,
        out_shape=(jax.ShapeDtypeStruct((NODES, columns), F32), jax.ShapeDtypeStruct((NODES, 128), F32)),
        grid_spec=pltpu.PrefetchScalarGridSpec(
            num_scalar_prefetch=1,
            grid=(groups,),
            in_specs=vocab_specs(blocks, span, columns),
            out_specs=(
                pl.BlockSpec((NODES, columns), lambda i, side: (0, 0)),
                pl.BlockSpec((NODES, 128), lambda i, side: (0, 0)),
            ),
        ),
        compiler_params=pltpu.CompilerParams(vmem_limit_bytes=12 << 20),
        cost_estimate=pl.CostEstimate(
            flops=2 * NODES * groups * span * columns, transcendentals=0, bytes_accessed=10 << 20
        ),
        name="vocab_first",
    )(side, hidden, gain, weight)


def vocab_second(side, hidden, gain, weight, y_first, sq_first, target, copies):
    groups, _, span, columns = weight.shape
    blocks = span // 128

    def kernel(side_ref, h_ref, g_ref, w_ref, y0_ref, sq0_ref, t_ref, o_ref, acc, sq):
        y, squares = vocab_blocks(side_ref, h_ref, g_ref, w_ref, blocks)

        @pl.when(pl.program_id(0) == 0)
        def _():
            acc[...] = y0_ref[...] + y
            sq[...] = sq0_ref[...] + squares

        @pl.when(pl.program_id(0) > 0)
        def _():
            acc[...] += y
            sq[...] += squares

        @pl.when(pl.program_id(0) == groups - 1)
        def _():
            mean = jnp.sum(sq[...], axis=1, keepdims=True) / D
            logits = acc[...] * lax.rsqrt(mean + EPSILON)
            peak = jnp.max(logits, axis=1, keepdims=True)
            total = jnp.sum(jnp.exp(logits - peak), axis=1, keepdims=True)
            lse = peak + jnp.log(total)
            column = lax.broadcasted_iota(jnp.int32, (NODES, columns), 1)
            chosen = jnp.sum(jnp.where(column == t_ref[...], logits, 0.0), axis=1, keepdims=True)
            lane = lax.broadcasted_iota(jnp.int32, (NODES, 128), 1)
            rows = jnp.where(lane == 0, lse, jnp.where(lane == 1, chosen, 0.0)).T
            row = jnp.concatenate([rows[0:1, :], rows[1:2, :]], axis=1)
            for i in range(copies):
                o_ref[i] = row

    return pl.pallas_call(
        kernel,
        out_shape=jax.ShapeDtypeStruct((copies, 1, 2 * NODES), F32),
        grid_spec=pltpu.PrefetchScalarGridSpec(
            num_scalar_prefetch=1,
            grid=(groups,),
            in_specs=vocab_specs(blocks, span, columns)
            + [
                pl.BlockSpec((NODES, columns), lambda i, side: (0, 0)),
                pl.BlockSpec((NODES, 128), lambda i, side: (0, 0)),
                pl.BlockSpec((NODES, 1), lambda i, side: (0, 0)),
            ],
            out_specs=pl.BlockSpec((copies, 1, 2 * NODES), lambda i, side: (0, 0, 0)),
            scratch_shapes=[VM((NODES, columns), F32), VM((NODES, 128), F32)],
        ),
        compiler_params=pltpu.CompilerParams(vmem_limit_bytes=12 << 20),
        cost_estimate=pl.CostEstimate(
            flops=2 * NODES * groups * span * columns, transcendentals=1 << 16, bytes_accessed=10 << 20
        ),
        name="vocab_second",
    )(side, hidden, gain, weight, y_first, sq_first, target)


def final_score(stats, amateur):
    def kernel(s_ref, a_ref, o_ref):
        lse = s_ref[:, 0, 0:NODES]
        chosen = s_ref[:, 0, NODES : 2 * NODES]
        best = jnp.max(lse, axis=0, keepdims=True)
        total = jnp.sum(jnp.exp(lse - best), axis=0, keepdims=True)
        picked = jnp.sum(chosen, axis=0, keepdims=True)
        o_ref[...] = picked - (best + jnp.log(total)) - a_ref[...]

    vmem = pl.BlockSpec(memory_space=pltpu.VMEM)
    return pl.pallas_call(
        kernel,
        out_shape=jax.ShapeDtypeStruct((1, NODES), F32),
        in_specs=[vmem, vmem],
        out_specs=vmem,
        compiler_params=pltpu.CompilerParams(vmem_limit_bytes=8 << 20),
        name="final_score",
    )(stats, amateur)


def body(
    queries,
    cache_keys,
    cache_values,
    tree_keys,
    tree_values,
    ancestors,
    filled_extents,
    out_weight,
    residual,
    norm_gain,
    vocab_weight,
    candidates,
    amateur,
):
    positions = cache_keys.shape[1]
    seq_index = lax.axis_index(SEQ)
    head_index = lax.axis_index(HEAD)
    core = lax.axis_index("c")
    seq_size = lax.axis_size(SEQ)
    cores = lax.axis_size("c")
    chips = lax.axis_size(CHIPS)
    devices = chips * cores

    def scalar(x):
        return x.astype(jnp.int32).reshape(1)

    def swap(x):
        return lax.ppermute(x, "c", [(0, 1), (1, 0)])

    def in_hbm(x):
        return pltpu.with_memory_space_constraint(x, pltpu.HBM)

    own, other = scalar(core), scalar(1 - core)
    place = jnp.stack([seq_index * positions, core]).astype(jnp.int32)
    keep, send = attention(in_hbm(queries), in_hbm(cache_keys), in_hbm(cache_values), in_hbm(filled_extents), place)
    parts = merge(keep, swap(send))
    parts = lax.all_to_all(parts, ROWS, 0, 0, tiled=True)
    tree_sums, tree_stats = tree_part(queries, tree_keys, tree_values, ancestors, scalar(seq_index))
    attended = combine(parts, tree_sums, tree_stats)
    attended = lax.all_to_all(attended, ROWS, 0, 0, tiled=True)
    swapped = swap(attended)
    rows, columns = out_weight.shape
    weight = in_hbm(out_weight.reshape(rows // HD // cores, cores, HD, columns))
    projected = project(own, attended, weight)
    shares = project(other, swapped, weight, projected)
    shares = lax.all_to_all(shares, HEAD, 0, 0, tiled=True)
    hidden, repeated = finish_hidden(shares, residual, scalar(head_index), chips)
    own_side = lax.all_to_all(repeated, CHIPS, 0, 0, tiled=True)
    other_side = swap(own_side)
    vocab_local = vocab_weight.shape[1]
    groups = seq_size // cores
    span = D // seq_size
    weight = in_hbm(vocab_weight.reshape(groups, cores, span, vocab_local))
    gain = norm_gain.reshape(groups, cores, span // 128, 128)
    y, squares = vocab_first(own, own_side, gain, weight)
    target = (candidates - lax.axis_index(ALL) * vocab_local).reshape(NODES, 1)
    stats = vocab_second(other, other_side, gain, weight, y, squares, target, devices)
    stats = lax.all_to_all(stats, ALL, 0, 0, tiled=True)
    contrast = final_score(stats, amateur.reshape(1, NODES))
    return (hidden, contrast.reshape(NODES))


def solution(mesh):
    fine = Mesh(mesh.devices.reshape(2, 4, 2, 4, 2), ALL)
    in_specs = (
        P(None, HEAD),
        P(None, SEQ, HEAD),
        P(None, SEQ, HEAD),
        P(None, HEAD),
        P(None, HEAD),
        P(),
        P(),
        P(HEAD, SEQ),
        P(None, SEQ),
        P(),
        P(None, ALL),
        P(),
        P(),
    )
    out_specs = (P(None, ALL), P())
    return jax.shard_map(body, mesh=fine, in_specs=in_specs, out_specs=out_specs, check_vma=False)
```

```python
import math

import jax
import jax.numpy as jnp
from jax import lax
from jax.experimental import pallas as pl
from jax.experimental.pallas import tpu as pltpu
from jax.sharding import Mesh, PartitionSpec as P

NODES_REQ = 64
NODES = 128
D = 16384
HD = 128
EPSILON = 1e-05
NEG_FILL = -1e30
LOG2E = math.log2(math.e)
SCALE2 = HD ** (-0.5) * LOG2E

SEQ = ("zh", "y", "c")
HEAD = ("x", "zl")
ROWS = ("zh", "y")
CHIPS = ("zh", "y", "x", "zl")
ALL = SEQ + HEAD


F32 = jnp.float32
BF16 = jnp.bfloat16
VM = pltpu.VMEM
STAT_ROWS = 16
BLOCK_ROWS = 256
CHUNK = 2048


def nt_dot(a, b):
    return lax.dot_general(a, b, (((1,), (1,)), ((), ())), preferred_element_type=F32)


def thirds(x):
    hi = x.astype(BF16).astype(F32)
    rest = x - hi
    mid = rest.astype(BF16).astype(F32)
    return hi, mid, rest - mid


def attention(queries, keys, values, extents, place):
    requests, positions, _ = keys.shape
    heads = queries.shape[1] // HD
    per_block = BLOCK_ROWS // NODES_REQ
    blocks_req = heads // per_block
    blocks = requests * blocks_req
    chunks = positions // CHUNK

    half = heads // 2

    def kernel(ext_ref, place_ref, q_hbm, k_hbm, v_hbm, keep, send, q_ref, qs, kv, vv, bias, s_buf, m_buf, acc, stat, sem):
        q_copy = pltpu.make_async_copy(q_hbm, q_ref, sem.at[2 * requests])
        q_copy.start()
        core = place_ref[1]
        copies = []
        for b in range(requests):
            copies.append(
                (
                    pltpu.make_async_copy(k_hbm.at[b], kv.at[b], sem.at[2 * b]),
                    pltpu.make_async_copy(v_hbm.at[b], vv.at[b, :, pl.ds(0, HD)], sem.at[2 * b + 1]),
                )
            )
        for pair in copies:
            for copy in pair:
                copy.start()
        lane = lax.broadcasted_iota(jnp.int32, (8, positions), 1)
        for b in range(requests):
            left = ext_ref[b] - place_ref[0]
            bias[b] = jnp.where(lane < left, 0.0, NEG_FILL).astype(F32)
        for b in range(requests):
            vv[b, :, HD : 2 * HD] = jnp.ones((positions, HD), BF16)
        stat[...] = jnp.zeros_like(stat)
        q_copy.wait()
        for g in range(heads):
            head = 2 * g + core if g < half else 2 * (g - half) + 1 - core
            at = pl.multiple_of(head * HD, HD)
            for b in range(requests):
                qs[b * blocks_req + g // per_block, (g % per_block) * NODES_REQ : (g % per_block + 1) * NODES_REQ, :] = (
                    q_ref[b * NODES_REQ : (b + 1) * NODES_REQ, pl.ds(at, HD)]
                )

        def scores(block, chunk, slot):
            b = block // blocks_req
            at = pl.multiple_of(chunk * CHUNK, CHUNK)
            s = nt_dot(qs[block], kv[b, pl.ds(at, CHUNK), :])
            best = m_buf[slot]
            for t in range(CHUNK // 128):
                piece = s[:, t * 128 : (t + 1) * 128]
                shift = bias[b, :, pl.ds(pl.multiple_of(at + t * 128, 128), 128)]
                piece = (piece.reshape(BLOCK_ROWS // 8, 8, 128) + shift[None]).reshape(BLOCK_ROWS, 128)
                s_buf[slot, chunk, :, t * 128 : (t + 1) * 128] = piece
                best = jnp.maximum(best, piece)
            m_buf[slot] = best

        def weigh(block, chunk, slot, top):
            b = block // blocks_req
            at = pl.multiple_of(chunk * CHUNK, CHUNK)
            pieces = []
            for t in range(CHUNK // 128):
                w = jnp.exp2(s_buf[slot, chunk, :, t * 128 : (t + 1) * 128] * SCALE2 - top)
                pieces.append(w.astype(BF16))
            acc[...] += jnp.dot(
                jnp.concatenate(pieces, axis=1), vv[b, pl.ds(at, CHUNK), :], preferred_element_type=F32
            )

        copies[0][0].wait()
        m_buf[0] = jnp.full((BLOCK_ROWS, 128), NEG_FILL, F32)

        @pl.loop(0, chunks)
        def _(chunk):
            scores(0, chunk, 0)

        def finish(block, best):
            total = acc[:, HD : HD + 1]
            b = block // blocks_req
            j = block % blocks_req
            slots = lax.broadcasted_iota(jnp.int32, (NODES_REQ, 128), 1)
            rows = slice(b * NODES_REQ, (b + 1) * NODES_REQ)
            held = stat[rows, :]
            for i in range(per_block):
                g = j * per_block + i
                part = slice(i * NODES_REQ, (i + 1) * NODES_REQ)
                out = keep if g < half else send
                out[g % half, rows, :] = acc[part, 0:HD].astype(BF16)
                for n, column in enumerate(thirds(best[part]) + thirds(total[part])):
                    held = jnp.where(slots == g * 8 + n, column, held)
            stat[rows, :] = held

        for block in range(blocks):
            last = block == blocks - 1
            slot = block % 2
            if block % blocks_req == 0:
                copies[block // blocks_req][1].wait()
            if not last and (block + 1) % blocks_req == 0:
                copies[(block + 1) // blocks_req][0].wait()
            best = jnp.max(m_buf[slot], axis=1, keepdims=True)
            best = jnp.maximum(best, 0.5 * NEG_FILL) * SCALE2
            top = jnp.broadcast_to(best, (BLOCK_ROWS, 128))
            acc[...] = jnp.zeros_like(acc)
            if not last:
                m_buf[1 - slot] = jnp.full((BLOCK_ROWS, 128), NEG_FILL, F32)

            @pl.loop(0, chunks)
            def _(chunk):
                if not last:
                    scores(block + 1, chunk, 1 - slot)
                weigh(block, chunk, slot, top)

            finish(block, best)

        turned = stat[...].T
        for g in range(heads):
            out = keep if g < half else send
            out[g % half, NODES : NODES + STAT_ROWS, :] = jnp.concatenate(
                [turned[g * 8 : (g + 1) * 8, :], jnp.zeros((STAT_ROWS - 8, NODES), F32)], axis=0
            ).astype(BF16)

    smem = pl.BlockSpec(memory_space=pltpu.SMEM)
    vmem = pl.BlockSpec(memory_space=pltpu.VMEM)
    hbm = pl.BlockSpec(memory_space=pltpu.HBM)
    out = jax.ShapeDtypeStruct((half, NODES + STAT_ROWS, HD), BF16)
    return pl.pallas_call(
        kernel,
        out_shape=(out, out),
        in_specs=[smem, smem, hbm, hbm, hbm],
        out_specs=(vmem, vmem),
        scratch_shapes=[
            VM((NODES, heads * HD), BF16),
            VM((blocks, BLOCK_ROWS, HD), BF16),
            VM((requests, positions, HD), BF16),
            VM((requests, positions, 2 * HD), BF16),
            VM((requests, 8, positions), F32),
            VM((2, chunks, BLOCK_ROWS, CHUNK), F32),
            VM((2, BLOCK_ROWS, 128), F32),
            VM((BLOCK_ROWS, 2 * HD), F32),
            VM((NODES, 128), F32),
            pltpu.SemaphoreType.DMA((2 * requests + 1,)),
        ],
        compiler_params=pltpu.CompilerParams(vmem_limit_bytes=32 << 20),
        cost_estimate=pl.CostEstimate(
            flops=4 * NODES * heads * positions * HD, transcendentals=NODES * heads * positions, bytes_accessed=5 << 20
        ),
        name="attention",
    )(extents, place, queries, keys, values)


def tree_part(queries, tree_keys, tree_values, ancestors, head):
    requests = ancestors.shape[0]

    def kernel(head_ref, q_ref, k_ref, v_ref, a_ref, o_ref, st_ref):
        at = pl.multiple_of(head_ref[0] * HD, HD)
        slots = lax.broadcasted_iota(jnp.int32, (NODES_REQ, 128), 1)
        for b in range(requests):
            rows = slice(b * NODES_REQ, (b + 1) * NODES_REQ)
            s = nt_dot(q_ref[rows, pl.ds(at, HD)], k_ref[rows, :])
            live = a_ref[b] > 0
            s = jnp.where(live, s * SCALE2, NEG_FILL)
            top = jnp.max(s, axis=1, keepdims=True)
            w = jnp.where(live, jnp.exp2(s - top), 0.0)
            total = jnp.sum(w, axis=1, keepdims=True)
            o_ref[rows, :] = jnp.dot(w.astype(BF16), v_ref[rows, :], preferred_element_type=F32)
            st_ref[rows, :] = jnp.where(slots == 0, top, jnp.where(slots == 1, total, 0.0))
        st_ref[...] = st_ref[...].T

    vmem = pl.BlockSpec(memory_space=pltpu.VMEM)
    return pl.pallas_call(
        kernel,
        out_shape=(jax.ShapeDtypeStruct((NODES, HD), F32), jax.ShapeDtypeStruct((128, NODES), F32)),
        in_specs=[pl.BlockSpec(memory_space=pltpu.SMEM)] + [vmem] * 4,
        out_specs=(vmem, vmem),
        compiler_params=pltpu.CompilerParams(vmem_limit_bytes=8 << 20),
        cost_estimate=pl.CostEstimate(flops=1 << 22, transcendentals=8192, bytes_accessed=1 << 20),
        name="tree_part",
    )(head, queries, tree_keys, tree_values, ancestors)


def merge(first, second):
    heads = first.shape[0]

    def kernel(a_ref, b_ref, o_ref):
        rows = []
        columns = []
        for g in range(heads):
            a = a_ref[g, NODES : NODES + STAT_ROWS, :].astype(F32)
            b = b_ref[g, NODES : NODES + STAT_ROWS, :].astype(F32)
            top_a = a[0:1] + a[1:2] + a[2:3]
            top_b = b[0:1] + b[1:2] + b[2:3]
            top = jnp.maximum(top_a, top_b)
            fa = jnp.exp2(top_a - top)
            fb = jnp.exp2(top_b - top)
            total = fa * (a[3:4] + a[4:5] + a[5:6]) + fb * (b[3:4] + b[4:5] + b[5:6])
            rows.append(jnp.concatenate(thirds(top) + thirds(total) + (jnp.zeros((STAT_ROWS - 6, NODES), F32),), axis=0))
            columns += [fa, fb]
        columns.append(jnp.zeros((128 - 2 * heads, NODES), F32))
        factor = jnp.concatenate(columns, axis=0).T
        for g in range(heads):
            o_ref[g, 0:NODES, :] = (
                a_ref[g, 0:NODES, :].astype(F32) * factor[:, 2 * g : 2 * g + 1]
                + b_ref[g, 0:NODES, :].astype(F32) * factor[:, 2 * g + 1 : 2 * g + 2]
            ).astype(BF16)
            o_ref[g, NODES : NODES + STAT_ROWS, :] = rows[g].astype(BF16)

    vmem = pl.BlockSpec(memory_space=pltpu.VMEM)
    return pl.pallas_call(
        kernel,
        out_shape=jax.ShapeDtypeStruct(first.shape, BF16),
        in_specs=[vmem] * 2,
        out_specs=vmem,
        compiler_params=pltpu.CompilerParams(vmem_limit_bytes=8 << 20),
        cost_estimate=pl.CostEstimate(flops=1 << 20, transcendentals=4096, bytes_accessed=1 << 20),
        name="merge",
    )(first, second)


def combine(parts, tree_sums, tree_stats):
    sources = parts.shape[0]

    def kernel(p_ref, t_ref, ts_ref, o_ref):
        tops = []
        totals = []
        for s in range(sources):
            st = p_ref[s, NODES : NODES + STAT_ROWS, :].astype(F32)
            tops.append(st[0:1] + st[1:2] + st[2:3])
            totals.append(st[3:4] + st[4:5] + st[5:6])
        tops.append(ts_ref[0:1, :])
        totals.append(ts_ref[1:2, :])
        tops = jnp.concatenate(tops + [jnp.full((24 - sources - 1, NODES), NEG_FILL, F32)], axis=0)
        totals = jnp.concatenate(totals + [jnp.zeros((24 - sources - 1, NODES), F32)], axis=0)
        best = jnp.max(tops, axis=0, keepdims=True)
        factor = jnp.exp2(tops - best)
        factor = factor / jnp.sum(factor * totals, axis=0, keepdims=True)
        factor = jnp.concatenate([factor, jnp.zeros((128 - 24, NODES), F32)], axis=0).T
        out = t_ref[...] * factor[:, sources : sources + 1]
        for s in range(sources):
            out = out + p_ref[s, 0:NODES, :].astype(F32) * factor[:, s : s + 1]
        out = out.astype(BF16)
        for s in range(sources):
            o_ref[s] = out

    vmem = pl.BlockSpec(memory_space=pltpu.VMEM)
    return pl.pallas_call(
        kernel,
        out_shape=jax.ShapeDtypeStruct((sources, NODES, HD), BF16),
        in_specs=[vmem] * 3,
        out_specs=vmem,
        compiler_params=pltpu.CompilerParams(vmem_limit_bytes=8 << 20),
        cost_estimate=pl.CostEstimate(flops=1 << 20, transcendentals=4096, bytes_accessed=1 << 20),
        name="combine",
    )(parts, tree_sums, tree_stats)


def project(side, attended, weight, so_far=None):
    heads = attended.shape[0]
    columns = weight.shape[3]
    rounded = so_far is not None
    step = 2

    def kernel(side_ref, a_ref, w_hbm, *rest):
        w, sem = rest[-2:]
        copies = [pltpu.make_async_copy(w_hbm.at[g, side_ref[0]], w.at[g], sem.at[g]) for g in range(heads)]
        for copy in copies:
            copy.start()
        y = rest[0][...] if rounded else jnp.zeros((NODES, columns), F32)
        for g in range(0, heads, step):
            x = jnp.concatenate([a_ref[g + i] for i in range(step)], axis=1)
            for i in range(step):
                copies[g + i].wait()
            y = y + jnp.dot(x, w[g : g + step].reshape(step * HD, columns), preferred_element_type=F32)
        if rounded:
            y = y.astype(BF16)
            for i in range(columns // 128):
                rest[1][i] = y[:, i * 128 : (i + 1) * 128]
        else:
            rest[0][...] = y

    vmem = pl.BlockSpec(memory_space=pltpu.VMEM)
    return pl.pallas_call(
        kernel,
        out_shape=jax.ShapeDtypeStruct((columns // 128, NODES, 128), BF16)
        if rounded
        else jax.ShapeDtypeStruct((NODES, columns), F32),
        in_specs=[pl.BlockSpec(memory_space=pltpu.SMEM), vmem, pl.BlockSpec(memory_space=pltpu.HBM)]
        + ([vmem] if rounded else []),
        out_specs=vmem,
        scratch_shapes=[VM((heads, HD, columns), BF16), pltpu.SemaphoreType.DMA((heads,))],
        compiler_params=pltpu.CompilerParams(vmem_limit_bytes=12 << 20),
        cost_estimate=pl.CostEstimate(flops=2 * NODES * heads * HD * columns, transcendentals=0, bytes_accessed=3 << 20),
        name="project",
    )(side, attended, weight, *((so_far,) if rounded else ()))


def finish_hidden(shares, residual, position, copies):
    sources = shares.shape[0]

    def kernel(pos_ref, s_ref, r_ref, h_ref, o_ref):
        at = pl.multiple_of(pos_ref[0] * 128, 128)
        total = s_ref[0].astype(F32)
        for s in range(1, sources):
            total = total + s_ref[s].astype(F32)
        h = (r_ref[:, pl.ds(at, 128)].astype(F32) + total).astype(BF16)
        h_ref[...] = h
        for i in range(copies):
            o_ref[i] = h

    vmem = pl.BlockSpec(memory_space=pltpu.VMEM)
    return pl.pallas_call(
        kernel,
        out_shape=(
            jax.ShapeDtypeStruct((NODES, 128), BF16),
            jax.ShapeDtypeStruct((copies, NODES, 128), BF16),
        ),
        in_specs=[pl.BlockSpec(memory_space=pltpu.SMEM), vmem, vmem],
        out_specs=(vmem, vmem),
        compiler_params=pltpu.CompilerParams(vmem_limit_bytes=8 << 20),
        cost_estimate=pl.CostEstimate(flops=1 << 18, transcendentals=0, bytes_accessed=3 << 20),
        name="finish_hidden",
    )(position, shares, residual)


def vocab_sum(side_ref, h_any, g_ref, w_hbm, y_ref, sq_ref, h_buf, w_buf, sem):
    groups, _, span, _ = w_hbm.shape
    blocks = span // 128
    side = side_ref[0]

    def copies(group):
        at = pl.ds(group * blocks, blocks)
        return (
            pltpu.make_async_copy(h_any.at[at], h_buf.at[at], sem.at[2 * group]),
            pltpu.make_async_copy(w_hbm.at[group, side], w_buf.at[group], sem.at[2 * group + 1]),
        )

    for group in range(groups):
        for copy in copies(group):
            copy.start()

    @pl.loop(0, groups)
    def _(group):
        for copy in copies(group):
            copy.wait()
        pieces = []
        squares = sq_ref[...]
        for i in range(blocks):
            h = h_buf[group * blocks + i].astype(F32)
            squares = squares + h * h
            pieces.append((h * g_ref[group, side, i : i + 1, :].astype(F32)).astype(BF16))
        sq_ref[...] = squares
        x = jnp.concatenate(pieces, axis=1)
        y_ref[...] += jnp.dot(x, w_buf[group], preferred_element_type=F32)


def vocab_scratch(hidden, weight):
    groups, _, span, columns = weight.shape
    return [
        VM(hidden.shape, BF16),
        VM((groups, span, columns), BF16),
        pltpu.SemaphoreType.DMA((2 * groups,)),
    ]


def vocab_first(side, hidden, gain, weight):
    groups, _, span, columns = weight.shape

    def kernel(side_ref, h_any, g_ref, w_hbm, y_ref, sq_ref, *scratch):
        y_ref[...] = jnp.zeros_like(y_ref)
        sq_ref[...] = jnp.zeros_like(sq_ref)
        vocab_sum(side_ref, h_any, g_ref, w_hbm, y_ref, sq_ref, *scratch)

    vmem = pl.BlockSpec(memory_space=pltpu.VMEM)
    anywhere = pl.BlockSpec(memory_space=pl.ANY)
    return pl.pallas_call(
        kernel,
        out_shape=(jax.ShapeDtypeStruct((NODES, columns), F32), jax.ShapeDtypeStruct((NODES, 128), F32)),
        in_specs=[pl.BlockSpec(memory_space=pltpu.SMEM), anywhere, vmem, pl.BlockSpec(memory_space=pltpu.HBM)],
        out_specs=(vmem, vmem),
        scratch_shapes=vocab_scratch(hidden, weight),
        compiler_params=pltpu.CompilerParams(vmem_limit_bytes=24 << 20),
        cost_estimate=pl.CostEstimate(
            flops=2 * NODES * groups * span * columns, transcendentals=0, bytes_accessed=10 << 20
        ),
        name="vocab_first",
    )(side, hidden, gain, weight)


def vocab_second(side, hidden, gain, weight, y_first, sq_first, target, copies):
    groups, _, span, columns = weight.shape

    def kernel(side_ref, h_any, g_ref, w_hbm, y0_ref, sq0_ref, t_ref, o_ref, acc, sq, *scratch):
        acc[...] = y0_ref[...]
        sq[...] = sq0_ref[...]
        vocab_sum(side_ref, h_any, g_ref, w_hbm, acc, sq, *scratch)
        mean = jnp.sum(sq[...], axis=1, keepdims=True) / D
        logits = acc[...] * lax.rsqrt(mean + EPSILON)
        peak = jnp.max(logits, axis=1, keepdims=True)
        total = jnp.sum(jnp.exp(logits - peak), axis=1, keepdims=True)
        lse = peak + jnp.log(total)
        column = lax.broadcasted_iota(jnp.int32, (NODES, columns), 1)
        chosen = jnp.sum(jnp.where(column == t_ref[...], logits, 0.0), axis=1, keepdims=True)
        lane = lax.broadcasted_iota(jnp.int32, (NODES, 128), 1)
        rows = jnp.where(lane == 0, lse, jnp.where(lane == 1, chosen, 0.0)).T
        row = jnp.concatenate([rows[0:1, :], rows[1:2, :]], axis=1)
        for i in range(copies):
            o_ref[i] = row

    vmem = pl.BlockSpec(memory_space=pltpu.VMEM)
    anywhere = pl.BlockSpec(memory_space=pl.ANY)
    return pl.pallas_call(
        kernel,
        out_shape=jax.ShapeDtypeStruct((copies, 1, 2 * NODES), F32),
        in_specs=[pl.BlockSpec(memory_space=pltpu.SMEM), anywhere, vmem, pl.BlockSpec(memory_space=pltpu.HBM)] + [vmem] * 3,
        out_specs=vmem,
        scratch_shapes=[VM((NODES, columns), F32), VM((NODES, 128), F32)] + vocab_scratch(hidden, weight),
        compiler_params=pltpu.CompilerParams(vmem_limit_bytes=24 << 20),
        cost_estimate=pl.CostEstimate(
            flops=2 * NODES * groups * span * columns, transcendentals=1 << 16, bytes_accessed=10 << 20
        ),
        name="vocab_second",
    )(side, hidden, gain, weight, y_first, sq_first, target)


def final_score(stats, amateur):
    def kernel(s_ref, a_ref, o_ref):
        lse = s_ref[:, 0, 0:NODES]
        chosen = s_ref[:, 0, NODES : 2 * NODES]
        best = jnp.max(lse, axis=0, keepdims=True)
        total = jnp.sum(jnp.exp(lse - best), axis=0, keepdims=True)
        picked = jnp.sum(chosen, axis=0, keepdims=True)
        o_ref[...] = picked - (best + jnp.log(total)) - a_ref[...]

    vmem = pl.BlockSpec(memory_space=pltpu.VMEM)
    return pl.pallas_call(
        kernel,
        out_shape=jax.ShapeDtypeStruct((1, NODES), F32),
        in_specs=[vmem, vmem],
        out_specs=vmem,
        compiler_params=pltpu.CompilerParams(vmem_limit_bytes=8 << 20),
        name="final_score",
    )(stats, amateur)


def body(
    queries,
    cache_keys,
    cache_values,
    tree_keys,
    tree_values,
    ancestors,
    filled_extents,
    out_weight,
    residual,
    norm_gain,
    vocab_weight,
    candidates,
    amateur,
):
    positions = cache_keys.shape[1]
    seq_index = lax.axis_index(SEQ)
    head_index = lax.axis_index(HEAD)
    core = lax.axis_index("c")
    seq_size = lax.axis_size(SEQ)
    cores = lax.axis_size("c")
    chips = lax.axis_size(CHIPS)
    devices = chips * cores

    def scalar(x):
        return x.astype(jnp.int32).reshape(1)

    def swap(x):
        return lax.ppermute(x, "c", [(0, 1), (1, 0)])

    def in_hbm(x):
        return pltpu.with_memory_space_constraint(x, pltpu.HBM)

    own, other = scalar(core), scalar(1 - core)
    place = jnp.stack([seq_index * positions, core]).astype(jnp.int32)
    keep, send = attention(in_hbm(queries), in_hbm(cache_keys), in_hbm(cache_values), in_hbm(filled_extents), place)
    parts = merge(keep, swap(send))
    parts = lax.all_to_all(parts, ROWS, 0, 0, tiled=True)
    tree_sums, tree_stats = tree_part(queries, tree_keys, tree_values, ancestors, scalar(seq_index))
    attended = combine(parts, tree_sums, tree_stats)
    rows, columns = out_weight.shape
    weight = in_hbm(out_weight.reshape(rows // HD // cores, cores, HD, columns))
    attended = lax.all_to_all(attended, ROWS, 0, 0, tiled=True)
    swapped = swap(attended)
    projected = project(own, attended, weight)
    shares = project(other, swapped, weight, projected)
    shares = lax.all_to_all(shares, HEAD, 0, 0, tiled=True)
    hidden, repeated = finish_hidden(shares, residual, scalar(head_index), chips)
    own_side = lax.all_to_all(repeated, CHIPS, 0, 0, tiled=True)
    vocab_local = vocab_weight.shape[1]
    groups = seq_size // cores
    span = D // seq_size
    weight = in_hbm(vocab_weight.reshape(groups, cores, span, vocab_local))
    other_side = swap(own_side)
    gain = norm_gain.reshape(groups, cores, span // 128, 128)
    y, squares = vocab_first(own, own_side, gain, weight)
    target = (candidates - lax.axis_index(ALL) * vocab_local).reshape(NODES, 1)
    stats = vocab_second(other, other_side, gain, weight, y, squares, target, devices)
    stats = lax.all_to_all(stats, ALL, 0, 0, tiled=True)
    contrast = final_score(stats, amateur.reshape(1, NODES))
    return (hidden, contrast.reshape(NODES))


def solution(mesh):
    fine = Mesh(mesh.devices.reshape(2, 4, 2, 4, 2), ALL)
    in_specs = (
        P(None, HEAD),
        P(None, SEQ, HEAD),
        P(None, SEQ, HEAD),
        P(None, HEAD),
        P(None, HEAD),
        P(),
        P(),
        P(HEAD, SEQ),
        P(None, SEQ),
        P(),
        P(None, ALL),
        P(),
        P(),
    )
    out_specs = (P(None, ALL), P())
    return jax.shard_map(body, mesh=fine, in_specs=in_specs, out_specs=out_specs, check_vma=False)
```

```python
import math

import jax
import jax.numpy as jnp
from jax import lax
from jax.experimental import pallas as pl
from jax.experimental.pallas import tpu as pltpu
from jax.sharding import Mesh, PartitionSpec as P

NODES_REQ = 64
NODES = 128
D = 16384
HD = 128
EPSILON = 1e-05
NEG_FILL = -1e30
LOG2E = math.log2(math.e)
SCALE2 = HD ** (-0.5) * LOG2E

SEQ = ("zh", "y", "c")
HEAD = ("x", "zl")
ROWS = ("zh", "y")
CHIPS = ("zh", "y", "x", "zl")
ALL = SEQ + HEAD


F32 = jnp.float32
BF16 = jnp.bfloat16
VM = pltpu.VMEM
STAT_ROWS = 16
BLOCK_ROWS = 256
CHUNK = 2048


def nt_dot(a, b):
    return lax.dot_general(a, b, (((1,), (1,)), ((), ())), preferred_element_type=F32)


def thirds(x):
    hi = x.astype(BF16).astype(F32)
    rest = x - hi
    mid = rest.astype(BF16).astype(F32)
    return hi, mid, rest - mid


def attention(queries, keys, values, extents, first, side):
    requests, positions, _ = keys.shape
    heads = queries.shape[1] // HD
    per_block = BLOCK_ROWS // NODES_REQ
    blocks_req = heads // per_block
    blocks = requests * blocks_req
    chunks = positions // CHUNK

    half = heads // 2

    def kernel(ext_ref, first_ref, side_ref, q_hbm, k_hbm, v_hbm, keep, send, q_ref, qs, kv, vv, bias, s_buf, m_buf, acc, stat, sem):
        q_copy = pltpu.make_async_copy(q_hbm, q_ref, sem.at[2 * requests])
        q_copy.start()
        core = side_ref[0]
        copies = []
        for b in range(requests):
            copies.append(
                (
                    pltpu.make_async_copy(k_hbm.at[b], kv.at[b], sem.at[2 * b]),
                    pltpu.make_async_copy(v_hbm.at[b], vv.at[b, :, pl.ds(0, HD)], sem.at[2 * b + 1]),
                )
            )
        for pair in copies:
            for copy in pair:
                copy.start()
        lane = lax.broadcasted_iota(jnp.int32, (8, positions), 1)
        for b in range(requests):
            left = ext_ref[b] - first_ref[0]
            bias[b] = jnp.where(lane < left, 0.0, NEG_FILL).astype(F32)
        for b in range(requests):
            vv[b, :, HD : 2 * HD] = jnp.ones((positions, HD), BF16)
        stat[...] = jnp.zeros_like(stat)
        q_copy.wait()
        for g in range(heads):
            head = 2 * g + core if g < half else 2 * (g - half) + 1 - core
            at = pl.multiple_of(head * HD, HD)
            for b in range(requests):
                qs[b * blocks_req + g // per_block, (g % per_block) * NODES_REQ : (g % per_block + 1) * NODES_REQ, :] = (
                    q_ref[b * NODES_REQ : (b + 1) * NODES_REQ, pl.ds(at, HD)]
                )

        def scores(block, chunk, slot):
            b = block // blocks_req
            at = pl.multiple_of(chunk * CHUNK, CHUNK)
            s = nt_dot(qs[block], kv[b, pl.ds(at, CHUNK), :])
            best = m_buf[slot]
            for t in range(CHUNK // 128):
                piece = s[:, t * 128 : (t + 1) * 128]
                shift = bias[b, :, pl.ds(pl.multiple_of(at + t * 128, 128), 128)]
                piece = (piece.reshape(BLOCK_ROWS // 8, 8, 128) + shift[None]).reshape(BLOCK_ROWS, 128)
                s_buf[slot, chunk, :, t * 128 : (t + 1) * 128] = piece
                best = jnp.maximum(best, piece)
            m_buf[slot] = best

        def weigh(block, chunk, slot, top):
            b = block // blocks_req
            at = pl.multiple_of(chunk * CHUNK, CHUNK)
            pieces = []
            for t in range(CHUNK // 128):
                w = jnp.exp2(s_buf[slot, chunk, :, t * 128 : (t + 1) * 128] * SCALE2 - top)
                pieces.append(w.astype(BF16))
            acc[...] += jnp.dot(
                jnp.concatenate(pieces, axis=1), vv[b, pl.ds(at, CHUNK), :], preferred_element_type=F32
            )

        copies[0][0].wait()
        m_buf[0] = jnp.full((BLOCK_ROWS, 128), NEG_FILL, F32)

        @pl.loop(0, chunks)
        def _(chunk):
            scores(0, chunk, 0)

        def finish(block, best):
            total = acc[:, HD : HD + 1]
            b = block // blocks_req
            j = block % blocks_req
            slots = lax.broadcasted_iota(jnp.int32, (NODES_REQ, 128), 1)
            rows = slice(b * NODES_REQ, (b + 1) * NODES_REQ)
            held = stat[rows, :]
            for i in range(per_block):
                g = j * per_block + i
                part = slice(i * NODES_REQ, (i + 1) * NODES_REQ)
                out = keep if g < half else send
                out[g % half, rows, :] = acc[part, 0:HD].astype(BF16)
                for n, column in enumerate(thirds(best[part]) + thirds(total[part])):
                    held = jnp.where(slots == g * 8 + n, column, held)
            stat[rows, :] = held

        for block in range(blocks):
            last = block == blocks - 1
            slot = block % 2
            if block % blocks_req == 0:
                copies[block // blocks_req][1].wait()
            if not last and (block + 1) % blocks_req == 0:
                copies[(block + 1) // blocks_req][0].wait()
            best = jnp.max(m_buf[slot], axis=1, keepdims=True)
            best = jnp.maximum(best, 0.5 * NEG_FILL) * SCALE2
            top = jnp.broadcast_to(best, (BLOCK_ROWS, 128))
            acc[...] = jnp.zeros_like(acc)
            if not last:
                m_buf[1 - slot] = jnp.full((BLOCK_ROWS, 128), NEG_FILL, F32)

            @pl.loop(0, chunks)
            def _(chunk):
                if not last:
                    scores(block + 1, chunk, 1 - slot)
                weigh(block, chunk, slot, top)

            finish(block, best)

        turned = stat[...].T
        for g in range(heads):
            out = keep if g < half else send
            out[g % half, NODES : NODES + STAT_ROWS, :] = jnp.concatenate(
                [turned[g * 8 : (g + 1) * 8, :], jnp.zeros((STAT_ROWS - 8, NODES), F32)], axis=0
            ).astype(BF16)

    smem = pl.BlockSpec(memory_space=pltpu.SMEM)
    vmem = pl.BlockSpec(memory_space=pltpu.VMEM)
    hbm = pl.BlockSpec(memory_space=pltpu.HBM)
    out = jax.ShapeDtypeStruct((half, NODES + STAT_ROWS, HD), BF16)
    return pl.pallas_call(
        kernel,
        out_shape=(out, out),
        in_specs=[smem, smem, smem, hbm, hbm, hbm],
        out_specs=(vmem, vmem),
        scratch_shapes=[
            VM((NODES, heads * HD), BF16),
            VM((blocks, BLOCK_ROWS, HD), BF16),
            VM((requests, positions, HD), BF16),
            VM((requests, positions, 2 * HD), BF16),
            VM((requests, 8, positions), F32),
            VM((2, chunks, BLOCK_ROWS, CHUNK), F32),
            VM((2, BLOCK_ROWS, 128), F32),
            VM((BLOCK_ROWS, 2 * HD), F32),
            VM((NODES, 128), F32),
            pltpu.SemaphoreType.DMA((2 * requests + 1,)),
        ],
        compiler_params=pltpu.CompilerParams(vmem_limit_bytes=32 << 20),
        cost_estimate=pl.CostEstimate(
            flops=4 * NODES * heads * positions * HD, transcendentals=NODES * heads * positions, bytes_accessed=5 << 20
        ),
        name="attention",
    )(extents, first, side, queries, keys, values)


def tree_part(queries, tree_keys, tree_values, ancestors, head):
    requests = ancestors.shape[0]

    def kernel(head_ref, q_ref, k_ref, v_ref, a_ref, o_ref, st_ref):
        at = pl.multiple_of(head_ref[0] * HD, HD)
        slots = lax.broadcasted_iota(jnp.int32, (NODES_REQ, 128), 1)
        for b in range(requests):
            rows = slice(b * NODES_REQ, (b + 1) * NODES_REQ)
            s = nt_dot(q_ref[rows, pl.ds(at, HD)], k_ref[rows, :])
            live = a_ref[b] > 0
            s = jnp.where(live, s * SCALE2, NEG_FILL)
            top = jnp.max(s, axis=1, keepdims=True)
            w = jnp.where(live, jnp.exp2(s - top), 0.0)
            total = jnp.sum(w, axis=1, keepdims=True)
            o_ref[rows, :] = jnp.dot(w.astype(BF16), v_ref[rows, :], preferred_element_type=F32)
            st_ref[rows, :] = jnp.where(slots == 0, top, jnp.where(slots == 1, total, 0.0))
        st_ref[...] = st_ref[...].T

    vmem = pl.BlockSpec(memory_space=pltpu.VMEM)
    return pl.pallas_call(
        kernel,
        out_shape=(jax.ShapeDtypeStruct((NODES, HD), F32), jax.ShapeDtypeStruct((128, NODES), F32)),
        in_specs=[pl.BlockSpec(memory_space=pltpu.SMEM)] + [vmem] * 4,
        out_specs=(vmem, vmem),
        compiler_params=pltpu.CompilerParams(vmem_limit_bytes=8 << 20),
        cost_estimate=pl.CostEstimate(flops=1 << 22, transcendentals=8192, bytes_accessed=1 << 20),
        name="tree_part",
    )(head, queries, tree_keys, tree_values, ancestors)


def merge(first, second):
    heads = first.shape[0]

    def kernel(a_ref, b_ref, o_ref):
        rows = []
        columns = []
        for g in range(heads):
            a = a_ref[g, NODES : NODES + STAT_ROWS, :].astype(F32)
            b = b_ref[g, NODES : NODES + STAT_ROWS, :].astype(F32)
            top_a = a[0:1] + a[1:2] + a[2:3]
            top_b = b[0:1] + b[1:2] + b[2:3]
            top = jnp.maximum(top_a, top_b)
            fa = jnp.exp2(top_a - top)
            fb = jnp.exp2(top_b - top)
            total = fa * (a[3:4] + a[4:5] + a[5:6]) + fb * (b[3:4] + b[4:5] + b[5:6])
            rows.append(jnp.concatenate(thirds(top) + thirds(total) + (jnp.zeros((STAT_ROWS - 6, NODES), F32),), axis=0))
            columns += [fa, fb]
        columns.append(jnp.zeros((128 - 2 * heads, NODES), F32))
        factor = jnp.concatenate(columns, axis=0).T
        for g in range(heads):
            o_ref[g, 0:NODES, :] = (
                a_ref[g, 0:NODES, :].astype(F32) * factor[:, 2 * g : 2 * g + 1]
                + b_ref[g, 0:NODES, :].astype(F32) * factor[:, 2 * g + 1 : 2 * g + 2]
            ).astype(BF16)
            o_ref[g, NODES : NODES + STAT_ROWS, :] = rows[g].astype(BF16)

    vmem = pl.BlockSpec(memory_space=pltpu.VMEM)
    return pl.pallas_call(
        kernel,
        out_shape=jax.ShapeDtypeStruct(first.shape, BF16),
        in_specs=[vmem] * 2,
        out_specs=vmem,
        compiler_params=pltpu.CompilerParams(vmem_limit_bytes=8 << 20),
        cost_estimate=pl.CostEstimate(flops=1 << 20, transcendentals=4096, bytes_accessed=1 << 20),
        name="merge",
    )(first, second)


def combine(parts, tree_sums, tree_stats):
    sources = parts.shape[0]

    def kernel(p_ref, t_ref, ts_ref, o_ref):
        tops = []
        totals = []
        for s in range(sources):
            st = p_ref[s, NODES : NODES + STAT_ROWS, :].astype(F32)
            tops.append(st[0:1] + st[1:2] + st[2:3])
            totals.append(st[3:4] + st[4:5] + st[5:6])
        tops.append(ts_ref[0:1, :])
        totals.append(ts_ref[1:2, :])
        tops = jnp.concatenate(tops + [jnp.full((24 - sources - 1, NODES), NEG_FILL, F32)], axis=0)
        totals = jnp.concatenate(totals + [jnp.zeros((24 - sources - 1, NODES), F32)], axis=0)
        best = jnp.max(tops, axis=0, keepdims=True)
        factor = jnp.exp2(tops - best)
        factor = factor / jnp.sum(factor * totals, axis=0, keepdims=True)
        factor = jnp.concatenate([factor, jnp.zeros((128 - 24, NODES), F32)], axis=0).T
        out = t_ref[...] * factor[:, sources : sources + 1]
        for s in range(sources):
            out = out + p_ref[s, 0:NODES, :].astype(F32) * factor[:, s : s + 1]
        out = out.astype(BF16)
        for s in range(sources):
            o_ref[s] = out

    vmem = pl.BlockSpec(memory_space=pltpu.VMEM)
    return pl.pallas_call(
        kernel,
        out_shape=jax.ShapeDtypeStruct((sources, NODES, HD), BF16),
        in_specs=[vmem] * 3,
        out_specs=vmem,
        compiler_params=pltpu.CompilerParams(vmem_limit_bytes=8 << 20),
        cost_estimate=pl.CostEstimate(flops=1 << 20, transcendentals=4096, bytes_accessed=1 << 20),
        name="combine",
    )(parts, tree_sums, tree_stats)


def project(side, attended, weight, so_far=None):
    heads = attended.shape[0]
    columns = weight.shape[3]
    rounded = so_far is not None
    step = 2

    def kernel(side_ref, a_ref, w_hbm, *rest):
        w, sem = rest[-2:]
        copies = [pltpu.make_async_copy(w_hbm.at[g, side_ref[0]], w.at[g], sem.at[g]) for g in range(heads)]
        for copy in copies:
            copy.start()
        y = rest[0][...] if rounded else jnp.zeros((NODES, columns), F32)
        for g in range(0, heads, step):
            x = jnp.concatenate([a_ref[g + i] for i in range(step)], axis=1)
            for i in range(step):
                copies[g + i].wait()
            y = y + jnp.dot(x, w[g : g + step].reshape(step * HD, columns), preferred_element_type=F32)
        if rounded:
            y = y.astype(BF16)
            for i in range(columns // 128):
                rest[1][i] = y[:, i * 128 : (i + 1) * 128]
        else:
            rest[0][...] = y

    vmem = pl.BlockSpec(memory_space=pltpu.VMEM)
    return pl.pallas_call(
        kernel,
        out_shape=jax.ShapeDtypeStruct((columns // 128, NODES, 128), BF16)
        if rounded
        else jax.ShapeDtypeStruct((NODES, columns), F32),
        in_specs=[pl.BlockSpec(memory_space=pltpu.SMEM), vmem, pl.BlockSpec(memory_space=pltpu.HBM)]
        + ([vmem] if rounded else []),
        out_specs=vmem,
        scratch_shapes=[VM((heads, HD, columns), BF16), pltpu.SemaphoreType.DMA((heads,))],
        compiler_params=pltpu.CompilerParams(vmem_limit_bytes=12 << 20),
        cost_estimate=pl.CostEstimate(flops=2 * NODES * heads * HD * columns, transcendentals=0, bytes_accessed=3 << 20),
        name="project",
    )(side, attended, weight, *((so_far,) if rounded else ()))


def finish_hidden(shares, residual, position, copies):
    sources = shares.shape[0]

    def kernel(pos_ref, s_ref, r_ref, h_ref, o_ref):
        at = pl.multiple_of(pos_ref[0] * 128, 128)
        total = s_ref[0].astype(F32)
        for s in range(1, sources):
            total = total + s_ref[s].astype(F32)
        h = (r_ref[:, pl.ds(at, 128)].astype(F32) + total).astype(BF16)
        h_ref[...] = h
        for i in range(copies):
            o_ref[i] = h

    vmem = pl.BlockSpec(memory_space=pltpu.VMEM)
    return pl.pallas_call(
        kernel,
        out_shape=(
            jax.ShapeDtypeStruct((NODES, 128), BF16),
            jax.ShapeDtypeStruct((copies, NODES, 128), BF16),
        ),
        in_specs=[pl.BlockSpec(memory_space=pltpu.SMEM), vmem, vmem],
        out_specs=(vmem, vmem),
        compiler_params=pltpu.CompilerParams(vmem_limit_bytes=8 << 20),
        cost_estimate=pl.CostEstimate(flops=1 << 18, transcendentals=0, bytes_accessed=3 << 20),
        name="finish_hidden",
    )(position, shares, residual)


def vocab_part(side, colour, hidden, gain, weight, so_far=None, target=None, copies=0):
    groups, _, pairs, _, _, span, columns = weight.shape
    blocks = 2 * pairs
    sizes = [part.shape[0] for part in hidden]
    ends = target is not None
    continues = so_far is not None

    def kernel(side_ref, colour_ref, *rest):
        rest = list(rest)
        h_refs = [rest.pop(0) for _ in sizes]
        g_ref, w_hbm = rest.pop(0), rest.pop(0)
        before = [rest.pop(0) for _ in range(2)] if continues else None
        t_ref = rest.pop(0) if ends else None
        o_ref = rest.pop(0) if ends else None
        acc, sq, h_buf, w_buf, h_sem, w_sem = rest
        side, colour = side_ref[0], colour_ref[0]

        def fetches(group):
            low = (colour + group) % 2
            return (
                pltpu.make_async_copy(w_hbm.at[group, side, :, 0, low], w_buf.at[group, 0], w_sem.at[2 * group]),
                pltpu.make_async_copy(w_hbm.at[group, side, :, 1, 1 - low], w_buf.at[group, 1], w_sem.at[2 * group + 1]),
            )

        arrivals = []
        at = 0
        for n, size in enumerate(sizes):
            arrivals.append(pltpu.make_async_copy(h_refs[n], h_buf.at[pl.ds(at, size)], h_sem.at[n]))
            at += size
        for copy in arrivals:
            copy.start()
        for group in range(groups):
            for fetch in fetches(group):
                fetch.start()
        acc[...] = before[0][...] if continues else jnp.zeros(acc.shape, F32)
        sq[...] = before[1][...] if continues else jnp.zeros(sq.shape, F32)
        for copy in arrivals:
            copy.wait()

        @pl.loop(0, groups)
        def _(group):
            low = (colour + group) % 2
            for fetch in fetches(group):
                fetch.wait()
            pieces = []
            squares = sq[...]
            for odd in range(2):
                for pair in range(pairs):
                    x = 2 * pair + odd
                    h = h_buf[group * blocks + x].astype(F32)
                    squares = squares + h * h
                    upper = (low + odd) % 2 == 1
                    scale = jnp.where(upper, g_ref[group, side, 2 * x + 1 : 2 * x + 2, :], g_ref[group, side, 2 * x : 2 * x + 1, :])
                    pieces.append((h * scale.astype(F32)).astype(BF16))
            sq[...] = squares
            x = jnp.concatenate(pieces, axis=1)
            acc[...] += jnp.dot(x, w_buf[group].reshape(blocks * span, columns), preferred_element_type=F32)

        if ends:
            mean = jnp.sum(sq[...], axis=1, keepdims=True) / D
            logits = acc[...] * lax.rsqrt(mean + EPSILON)
            peak = jnp.max(logits, axis=1, keepdims=True)
            total = jnp.sum(jnp.exp(logits - peak), axis=1, keepdims=True)
            lse = peak + jnp.log(total)
            column = lax.broadcasted_iota(jnp.int32, (NODES, columns), 1)
            chosen = jnp.sum(jnp.where(column == t_ref[...], logits, 0.0), axis=1, keepdims=True)
            lane = lax.broadcasted_iota(jnp.int32, (NODES, 128), 1)
            rows = jnp.where(lane == 0, lse, jnp.where(lane == 1, chosen, 0.0)).T
            row = jnp.concatenate([rows[0:1, :], rows[1:2, :]], axis=1)
            for i in range(copies):
                o_ref[i] = row

    vmem = pl.BlockSpec(memory_space=pltpu.VMEM)
    anywhere = pl.BlockSpec(memory_space=pl.ANY)
    sums = [((NODES, columns), F32), ((NODES, 128), F32)]
    return pl.pallas_call(
        kernel,
        out_shape=jax.ShapeDtypeStruct((copies, 1, 2 * NODES), F32)
        if ends
        else tuple(jax.ShapeDtypeStruct(*kind) for kind in sums),
        in_specs=[pl.BlockSpec(memory_space=pltpu.SMEM)] * 2
        + [anywhere] * len(sizes)
        + [vmem, pl.BlockSpec(memory_space=pltpu.HBM)]
        + [vmem] * (2 * continues + ends),
        out_specs=vmem if ends else (vmem, vmem),
        scratch_shapes=([VM(*kind) for kind in sums] if ends else [])
        + [
            VM((sum(sizes), NODES, 128), BF16),
            VM((groups, 2, pairs, span, columns), BF16),
            pltpu.SemaphoreType.DMA((len(sizes),)),
            pltpu.SemaphoreType.DMA((2 * groups,)),
        ],
        compiler_params=pltpu.CompilerParams(vmem_limit_bytes=16 << 20),
        cost_estimate=pl.CostEstimate(
            flops=2 * NODES * groups * blocks * span * columns, transcendentals=0, bytes_accessed=6 << 20
        ),
        name="vocab_part",
    )(side, colour, *hidden, gain, weight, *(so_far or ()), *((target,) if ends else ()))


def colours(sizes):
    zhs, ys, cs, xs, zls = sizes
    tori = (xs, ys, zhs * zls)
    groups = [[] for _ in range(2 * cs)]
    swaps = [[] for _ in range(6)]
    for index in range(math.prod(sizes)):
        rest, zl = divmod(index, zls)
        rest, x = divmod(rest, xs)
        rest, c = divmod(rest, cs)
        zh, y = divmod(rest, ys)
        spot = (x, y, zh * zls + zl)
        colour = sum(spot) % 2
        groups[colour * cs + c].append(index)
        for k in range(6):
            axis, sign = k // 2, 1 - 2 * (k % 2)
            to = list(spot)
            to[axis] = (to[axis] + (sign if colour == 0 else -sign)) % tori[axis]
            high, low = divmod(to[2], zls)
            swaps[k].append((index, (((high * ys + to[1]) * cs + c) * xs + to[0]) * zls + low))
    return groups, swaps


def final_score(stats, amateur):
    def kernel(s_ref, a_ref, o_ref):
        lse = s_ref[:, 0, 0:NODES]
        chosen = s_ref[:, 0, NODES : 2 * NODES]
        best = jnp.max(lse, axis=0, keepdims=True)
        total = jnp.sum(jnp.exp(lse - best), axis=0, keepdims=True)
        picked = jnp.sum(chosen, axis=0, keepdims=True)
        o_ref[...] = picked - (best + jnp.log(total)) - a_ref[...]

    vmem = pl.BlockSpec(memory_space=pltpu.VMEM)
    return pl.pallas_call(
        kernel,
        out_shape=jax.ShapeDtypeStruct((1, NODES), F32),
        in_specs=[vmem, vmem],
        out_specs=vmem,
        compiler_params=pltpu.CompilerParams(vmem_limit_bytes=8 << 20),
        name="final_score",
    )(stats, amateur)


def body(
    queries,
    cache_keys,
    cache_values,
    tree_keys,
    tree_values,
    ancestors,
    filled_extents,
    out_weight,
    residual,
    norm_gain,
    vocab_weight,
    candidates,
    amateur,
):
    positions = cache_keys.shape[1]
    seq_index = lax.axis_index(SEQ)
    head_index = lax.axis_index(HEAD)
    core = lax.axis_index("c")
    seq_size = lax.axis_size(SEQ)
    cores = lax.axis_size("c")
    chips = lax.axis_size(CHIPS)
    devices = chips * cores

    def scalar(x):
        return x.astype(jnp.int32).reshape(1)

    def swap(x):
        return lax.ppermute(x, "c", [(0, 1), (1, 0)])

    def in_hbm(x):
        return pltpu.with_memory_space_constraint(x, pltpu.HBM)

    own, other = scalar(core), scalar(1 - core)
    keep, send = attention(
        in_hbm(queries), in_hbm(cache_keys), in_hbm(cache_values), in_hbm(filled_extents), scalar(seq_index * positions), own
    )
    parts = merge(keep, swap(send))
    parts = lax.all_to_all(parts, ROWS, 0, 0, tiled=True)
    tree_sums, tree_stats = tree_part(queries, tree_keys, tree_values, ancestors, scalar(seq_index))
    attended = combine(parts, tree_sums, tree_stats)
    rows, columns = out_weight.shape
    weight = in_hbm(out_weight.reshape(rows // HD // cores, cores, HD, columns))
    attended = lax.all_to_all(attended, ROWS, 0, 0, tiled=True)
    swapped = swap(attended)
    projected = project(own, attended, weight)
    shares = project(other, swapped, weight, projected)
    shares = lax.all_to_all(shares, HEAD, 0, 0, tiled=True)
    same, swaps = colours([lax.axis_size(name) for name in ALL])
    count = len(same[0])
    hidden, repeated = finish_hidden(shares, residual, scalar(head_index), count)
    near = lax.all_to_all(repeated, ALL, 0, 0, axis_index_groups=same, tiled=True)
    cuts = [count * k // 6 for k in range(7)]
    near_other = swap(near)
    far = []
    for k in range(6):
        far.append(lax.ppermute(near[cuts[k] : cuts[k + 1]], ALL, swaps[k]))
    far_other = [swap(part) for part in far]
    vocab_local = vocab_weight.shape[1]
    groups = seq_size // cores
    span = D // devices
    xs, zls = lax.axis_size("x"), lax.axis_size("zl")
    weight = in_hbm(vocab_weight.reshape(groups, cores, xs // 2, 2, zls, span, vocab_local))
    gain = norm_gain.reshape(groups, cores, xs * zls, span)
    target = (candidates - lax.axis_index(ALL) * vocab_local).reshape(NODES, 1)
    colour = (lax.axis_index("x") + lax.axis_index("y") + lax.axis_index("zl")) % 2

    tint, other_tint = scalar(colour), scalar(1 - colour)
    sums = vocab_part(own, tint, [near], gain, weight)
    sums = vocab_part(other, tint, [near_other], gain, weight, sums)
    sums = vocab_part(own, other_tint, far, gain, weight, sums)
    stats = vocab_part(other, other_tint, far_other, gain, weight, sums, target, devices)
    stats = lax.all_to_all(stats, ALL, 0, 0, tiled=True)
    contrast = final_score(stats, amateur.reshape(1, NODES))
    return (hidden, contrast.reshape(NODES))


def solution(mesh):
    fine = Mesh(mesh.devices.reshape(2, 4, 2, 4, 2), ALL)
    in_specs = (
        P(None, HEAD),
        P(None, SEQ, HEAD),
        P(None, SEQ, HEAD),
        P(None, HEAD),
        P(None, HEAD),
        P(),
        P(),
        P(HEAD, SEQ),
        P(None, SEQ),
        P(),
        P(None, ALL),
        P(),
        P(),
    )
    out_specs = (P(None, ALL), P())

    return jax.shard_map(body, mesh=fine, in_specs=in_specs, out_specs=out_specs, check_vma=False)
```

```python
import math

import jax
import jax.numpy as jnp
from jax import lax
from jax.experimental import pallas as pl
from jax.experimental.pallas import tpu as pltpu
from jax.sharding import Mesh, PartitionSpec as P

NODES_REQ = 64
NODES = 128
D = 16384
HD = 128
EPSILON = 1e-05
NEG_FILL = -1e30
LOG2E = math.log2(math.e)
SCALE2 = HD ** (-0.5) * LOG2E

SEQ = ("zh", "y", "c")
HEAD = ("x", "zl")
ROWS = ("zh", "y")
CHIPS = ("zh", "y", "x", "zl")
ALL = SEQ + HEAD


F32 = jnp.float32
BF16 = jnp.bfloat16
VM = pltpu.VMEM
STAT_ROWS = 16
BLOCK_ROWS = 512
CHUNK = 2048


def nt_dot(a, b):
    return lax.dot_general(a, b, (((1,), (1,)), ((), ())), preferred_element_type=F32)


def thirds(x):
    hi = x.astype(BF16).astype(F32)
    rest = x - hi
    mid = rest.astype(BF16).astype(F32)
    return hi, mid, rest - mid


def attention(queries, keys, values, extents, place):
    requests, positions, _ = keys.shape
    heads = queries.shape[1] // HD
    per_block = BLOCK_ROWS // NODES_REQ
    blocks_req = heads // per_block
    blocks = requests * blocks_req
    chunks = positions // CHUNK

    half = heads // 2

    def kernel(ext_ref, place_ref, q_hbm, k_hbm, v_hbm, keep, send, q_ref, qs, kv, vv, turned, bias, s_buf, m_buf, acc, stat, sem):
        q_copy = pltpu.make_async_copy(q_hbm, q_ref, sem.at[2 * requests])
        q_copy.start()
        core = place_ref[1]
        copies = []
        for b in range(requests):
            copies.append(
                (
                    pltpu.make_async_copy(k_hbm.at[b], kv.at[b], sem.at[2 * b]),
                    pltpu.make_async_copy(v_hbm.at[b], vv.at[b], sem.at[2 * b + 1]),
                )
            )
        for pair in copies:
            for copy in pair:
                copy.start()
        index = lax.broadcasted_iota(jnp.int32, (positions, 128), 0)
        for b in range(requests):
            left = ext_ref[b] - place_ref[0]
            bias[b] = jnp.where(index < left, 0.0, NEG_FILL).astype(F32)
            turned[b, HD:, :] = jnp.ones((STAT_ROWS, positions), BF16)
        q_copy.wait()
        for g in range(heads):
            head = 2 * g + core if g < half else 2 * (g - half) + 1 - core
            at = pl.multiple_of(head * HD, HD)
            for b in range(requests):
                qs[b * blocks_req + g // per_block, (g % per_block) * NODES_REQ : (g % per_block + 1) * NODES_REQ, :] = (
                    q_ref[b * NODES_REQ : (b + 1) * NODES_REQ, pl.ds(at, HD)]
                )

        def scores(block, chunk, slot):
            b = block // blocks_req
            rows = pl.ds(pl.multiple_of(chunk * CHUNK, CHUNK), CHUNK)
            s = nt_dot(kv[b, rows, :], qs[block])
            shift = bias[b, rows, :]
            for t in range(BLOCK_ROWS // 128):
                lanes = slice(t * 128, (t + 1) * 128)
                piece = s[:, lanes] + shift
                s_buf[slot, chunk, :, lanes] = piece
                m_buf[slot, :, lanes] = jnp.maximum(m_buf[slot, :, lanes], jnp.max(piece.reshape(CHUNK // 8, 8, 128), axis=0))

        def weigh(block, chunk, slot, top):
            b = block // blocks_req
            columns = pl.ds(pl.multiple_of(chunk * CHUNK, CHUNK), CHUNK)
            pieces = []
            for t in range(BLOCK_ROWS // 128):
                lanes = slice(t * 128, (t + 1) * 128)
                scaled = s_buf[slot, chunk, :, lanes].reshape(CHUNK // 8, 8, 128) * SCALE2 - top[:, lanes][None]
                pieces.append(jnp.exp2(scaled).reshape(CHUNK, 128).astype(BF16))
            acc[...] += jnp.dot(turned[b, :, columns], jnp.concatenate(pieces, axis=1), preferred_element_type=F32)

        copies[0][0].wait()
        m_buf[0] = jnp.full((8, BLOCK_ROWS), NEG_FILL, F32)

        @pl.loop(0, chunks)
        def _(chunk):
            scores(0, chunk, 0)

        def finish(block, best):
            total = acc[HD : HD + 1, :]
            b = block // blocks_req
            j = block % blocks_req
            rows = slice(b * NODES_REQ, (b + 1) * NODES_REQ)
            lane = lax.broadcasted_iota(jnp.int32, (8, NODES), 1)
            mine = (lane // NODES_REQ) == b
            for t in range(BLOCK_ROWS // 128):
                lanes = slice(t * 128, (t + 1) * 128)
                sums = acc[0:HD, lanes].T.astype(BF16)
                facts = jnp.concatenate(
                    thirds(best[:, lanes]) + thirds(total[:, lanes]) + (jnp.zeros((2, 128), F32),), axis=0
                )
                swapped = pltpu.roll(facts, NODES_REQ, 1)
                for i in range(2):
                    g = j * per_block + 2 * t + i
                    out = keep if g < half else send
                    out[g % half, rows, :] = sums[i * NODES_REQ : (i + 1) * NODES_REQ, :]
                    row = facts if i == b else swapped
                    stat[g] = row if b == 0 else jnp.where(mine, row, stat[g])

        for block in range(blocks):
            last = block == blocks - 1
            slot = block % 2
            b = block // blocks_req
            if block % blocks_req == 0:
                copies[b][1].wait()

                @pl.loop(0, positions // 512)
                def _(i):
                    at = pl.multiple_of(i * 512, 512)
                    turned[b, 0:HD, pl.ds(at, 512)] = vv[b, pl.ds(at, 512), :].T

            if not last and (block + 1) % blocks_req == 0:
                copies[(block + 1) // blocks_req][0].wait()
            best = jnp.max(m_buf[slot], axis=0, keepdims=True)
            best = jnp.maximum(best, 0.5 * NEG_FILL) * SCALE2
            top = jnp.broadcast_to(best, (8, BLOCK_ROWS))
            acc[...] = jnp.zeros_like(acc)
            if not last:
                m_buf[1 - slot] = jnp.full((8, BLOCK_ROWS), NEG_FILL, F32)

            @pl.loop(0, chunks)
            def _(chunk):
                if not last:
                    scores(block + 1, chunk, 1 - slot)
                weigh(block, chunk, slot, top)

            finish(block, best)

        for g in range(heads):
            out = keep if g < half else send
            out[g % half, NODES : NODES + STAT_ROWS, :] = jnp.concatenate(
                [stat[g], jnp.zeros((STAT_ROWS - 8, NODES), F32)], axis=0
            ).astype(BF16)

    smem = pl.BlockSpec(memory_space=pltpu.SMEM)
    vmem = pl.BlockSpec(memory_space=pltpu.VMEM)
    hbm = pl.BlockSpec(memory_space=pltpu.HBM)
    out = jax.ShapeDtypeStruct((half, NODES + STAT_ROWS, HD), BF16)
    return pl.pallas_call(
        kernel,
        out_shape=(out, out),
        in_specs=[smem, smem, hbm, hbm, hbm],
        out_specs=(vmem, vmem),
        scratch_shapes=[
            VM((NODES, heads * HD), BF16),
            VM((blocks, BLOCK_ROWS, HD), BF16),
            VM((requests, positions, HD), BF16),
            VM((requests, positions, HD), BF16),
            VM((requests, HD + STAT_ROWS, positions), BF16),
            VM((requests, positions, 128), F32),
            VM((2, chunks, CHUNK, BLOCK_ROWS), F32),
            VM((2, 8, BLOCK_ROWS), F32),
            VM((HD + STAT_ROWS, BLOCK_ROWS), F32),
            VM((heads, 8, NODES), F32),
            pltpu.SemaphoreType.DMA((2 * requests + 1,)),
        ],
        compiler_params=pltpu.CompilerParams(vmem_limit_bytes=48 << 20),
        cost_estimate=pl.CostEstimate(
            flops=4 * NODES * heads * positions * HD, transcendentals=NODES * heads * positions, bytes_accessed=5 << 20
        ),
        name="attention",
    )(extents, place, queries, keys, values)


def tree_part(queries, tree_keys, tree_values, ancestors, head):
    requests = ancestors.shape[0]

    def kernel(head_ref, q_ref, k_ref, v_ref, a_ref, o_ref, st_ref):
        at = pl.multiple_of(head_ref[0] * HD, HD)
        slots = lax.broadcasted_iota(jnp.int32, (NODES_REQ, 128), 1)
        for b in range(requests):
            rows = slice(b * NODES_REQ, (b + 1) * NODES_REQ)
            s = nt_dot(q_ref[rows, pl.ds(at, HD)], k_ref[rows, :])
            live = a_ref[b] > 0
            s = jnp.where(live, s * SCALE2, NEG_FILL)
            top = jnp.max(s, axis=1, keepdims=True)
            w = jnp.where(live, jnp.exp2(s - top), 0.0)
            total = jnp.sum(w, axis=1, keepdims=True)
            o_ref[rows, :] = jnp.dot(w.astype(BF16), v_ref[rows, :], preferred_element_type=F32)
            st_ref[rows, :] = jnp.where(slots == 0, top, jnp.where(slots == 1, total, 0.0))
        st_ref[...] = st_ref[...].T

    vmem = pl.BlockSpec(memory_space=pltpu.VMEM)
    return pl.pallas_call(
        kernel,
        out_shape=(jax.ShapeDtypeStruct((NODES, HD), F32), jax.ShapeDtypeStruct((128, NODES), F32)),
        in_specs=[pl.BlockSpec(memory_space=pltpu.SMEM)] + [vmem] * 4,
        out_specs=(vmem, vmem),
        compiler_params=pltpu.CompilerParams(vmem_limit_bytes=8 << 20),
        cost_estimate=pl.CostEstimate(flops=1 << 22, transcendentals=8192, bytes_accessed=1 << 20),
        name="tree_part",
    )(head, queries, tree_keys, tree_values, ancestors)


def merge(first, second):
    heads = first.shape[0]

    def kernel(a_ref, b_ref, o_ref):
        rows = []
        columns = []
        for g in range(heads):
            a = a_ref[g, NODES : NODES + STAT_ROWS, :].astype(F32)
            b = b_ref[g, NODES : NODES + STAT_ROWS, :].astype(F32)
            top_a = a[0:1] + a[1:2] + a[2:3]
            top_b = b[0:1] + b[1:2] + b[2:3]
            top = jnp.maximum(top_a, top_b)
            fa = jnp.exp2(top_a - top)
            fb = jnp.exp2(top_b - top)
            total = fa * (a[3:4] + a[4:5] + a[5:6]) + fb * (b[3:4] + b[4:5] + b[5:6])
            rows.append(jnp.concatenate(thirds(top) + thirds(total) + (jnp.zeros((STAT_ROWS - 6, NODES), F32),), axis=0))
            columns += [fa, fb]
        columns.append(jnp.zeros((128 - 2 * heads, NODES), F32))
        factor = jnp.concatenate(columns, axis=0).T
        for g in range(heads):
            o_ref[g, 0:NODES, :] = (
                a_ref[g, 0:NODES, :].astype(F32) * factor[:, 2 * g : 2 * g + 1]
                + b_ref[g, 0:NODES, :].astype(F32) * factor[:, 2 * g + 1 : 2 * g + 2]
            ).astype(BF16)
            o_ref[g, NODES : NODES + STAT_ROWS, :] = rows[g].astype(BF16)

    vmem = pl.BlockSpec(memory_space=pltpu.VMEM)
    return pl.pallas_call(
        kernel,
        out_shape=jax.ShapeDtypeStruct(first.shape, BF16),
        in_specs=[vmem] * 2,
        out_specs=vmem,
        compiler_params=pltpu.CompilerParams(vmem_limit_bytes=8 << 20),
        cost_estimate=pl.CostEstimate(flops=1 << 20, transcendentals=4096, bytes_accessed=1 << 20),
        name="merge",
    )(first, second)


def combine(parts, tree_sums, tree_stats):
    sources = parts.shape[0]

    def kernel(p_ref, t_ref, ts_ref, o_ref):
        tops = []
        totals = []
        for s in range(sources):
            st = p_ref[s, NODES : NODES + STAT_ROWS, :].astype(F32)
            tops.append(st[0:1] + st[1:2] + st[2:3])
            totals.append(st[3:4] + st[4:5] + st[5:6])
        tops.append(ts_ref[0:1, :])
        totals.append(ts_ref[1:2, :])
        tops = jnp.concatenate(tops + [jnp.full((24 - sources - 1, NODES), NEG_FILL, F32)], axis=0)
        totals = jnp.concatenate(totals + [jnp.zeros((24 - sources - 1, NODES), F32)], axis=0)
        best = jnp.max(tops, axis=0, keepdims=True)
        factor = jnp.exp2(tops - best)
        factor = factor / jnp.sum(factor * totals, axis=0, keepdims=True)
        factor = jnp.concatenate([factor, jnp.zeros((128 - 24, NODES), F32)], axis=0).T
        out = t_ref[...] * factor[:, sources : sources + 1]
        for s in range(sources):
            out = out + p_ref[s, 0:NODES, :].astype(F32) * factor[:, s : s + 1]
        out = out.astype(BF16)
        for s in range(sources):
            o_ref[s] = out

    vmem = pl.BlockSpec(memory_space=pltpu.VMEM)
    return pl.pallas_call(
        kernel,
        out_shape=jax.ShapeDtypeStruct((sources, NODES, HD), BF16),
        in_specs=[vmem] * 3,
        out_specs=vmem,
        compiler_params=pltpu.CompilerParams(vmem_limit_bytes=8 << 20),
        cost_estimate=pl.CostEstimate(flops=1 << 20, transcendentals=4096, bytes_accessed=1 << 20),
        name="combine",
    )(parts, tree_sums, tree_stats)


def project(side, attended, weight, so_far=None):
    heads = attended.shape[0]
    columns = weight.shape[3]
    rounded = so_far is not None
    step = 2

    def kernel(side_ref, a_ref, w_hbm, *rest):
        w, sem = rest[-2:]
        copies = [pltpu.make_async_copy(w_hbm.at[g, side_ref[0]], w.at[g], sem.at[g]) for g in range(heads)]
        for copy in copies:
            copy.start()
        y = rest[0][...] if rounded else jnp.zeros((NODES, columns), F32)
        for g in range(0, heads, step):
            x = jnp.concatenate([a_ref[g + i] for i in range(step)], axis=1)
            for i in range(step):
                copies[g + i].wait()
            y = y + jnp.dot(x, w[g : g + step].reshape(step * HD, columns), preferred_element_type=F32)
        if rounded:
            y = y.astype(BF16)
            for i in range(columns // 128):
                rest[1][i] = y[:, i * 128 : (i + 1) * 128]
        else:
            rest[0][...] = y

    vmem = pl.BlockSpec(memory_space=pltpu.VMEM)
    return pl.pallas_call(
        kernel,
        out_shape=jax.ShapeDtypeStruct((columns // 128, NODES, 128), BF16)
        if rounded
        else jax.ShapeDtypeStruct((NODES, columns), F32),
        in_specs=[pl.BlockSpec(memory_space=pltpu.SMEM), vmem, pl.BlockSpec(memory_space=pltpu.HBM)]
        + ([vmem] if rounded else []),
        out_specs=vmem,
        scratch_shapes=[VM((heads, HD, columns), BF16), pltpu.SemaphoreType.DMA((heads,))],
        compiler_params=pltpu.CompilerParams(vmem_limit_bytes=12 << 20),
        cost_estimate=pl.CostEstimate(flops=2 * NODES * heads * HD * columns, transcendentals=0, bytes_accessed=3 << 20),
        name="project",
    )(side, attended, weight, *((so_far,) if rounded else ()))


def finish_hidden(shares, residual, position, copies):
    sources = shares.shape[0]

    def kernel(pos_ref, s_ref, r_ref, h_ref, o_ref):
        at = pl.multiple_of(pos_ref[0] * 128, 128)
        total = s_ref[0].astype(F32)
        for s in range(1, sources):
            total = total + s_ref[s].astype(F32)
        h = (r_ref[:, pl.ds(at, 128)].astype(F32) + total).astype(BF16)
        h_ref[...] = h
        for i in range(copies):
            o_ref[i] = h

    vmem = pl.BlockSpec(memory_space=pltpu.VMEM)
    return pl.pallas_call(
        kernel,
        out_shape=(
            jax.ShapeDtypeStruct((NODES, 128), BF16),
            jax.ShapeDtypeStruct((copies, NODES, 128), BF16),
        ),
        in_specs=[pl.BlockSpec(memory_space=pltpu.SMEM), vmem, vmem],
        out_specs=(vmem, vmem),
        compiler_params=pltpu.CompilerParams(vmem_limit_bytes=8 << 20),
        cost_estimate=pl.CostEstimate(flops=1 << 18, transcendentals=0, bytes_accessed=3 << 20),
        name="finish_hidden",
    )(position, shares, residual)


def vocab_sum(side_ref, h_any, g_ref, w_hbm, y_ref, sq_ref, h_buf, w_buf, sem):
    groups, _, span, _ = w_hbm.shape
    blocks = span // 128
    side = side_ref[0]

    def copies(group):
        at = pl.ds(group * blocks, blocks)
        return (
            pltpu.make_async_copy(h_any.at[at], h_buf.at[at], sem.at[2 * group]),
            pltpu.make_async_copy(w_hbm.at[group, side], w_buf.at[group], sem.at[2 * group + 1]),
        )

    for group in range(groups):
        for copy in copies(group):
            copy.start()

    @pl.loop(0, groups)
    def _(group):
        for copy in copies(group):
            copy.wait()
        pieces = []
        squares = sq_ref[...]
        for i in range(blocks):
            h = h_buf[group * blocks + i].astype(F32)
            squares = squares + h * h
            pieces.append((h * g_ref[group, side, i : i + 1, :].astype(F32)).astype(BF16))
        sq_ref[...] = squares
        x = jnp.concatenate(pieces, axis=1)
        y_ref[...] += jnp.dot(x, w_buf[group], preferred_element_type=F32)


def vocab_scratch(hidden, weight):
    groups, _, span, columns = weight.shape
    return [
        VM(hidden.shape, BF16),
        VM((groups, span, columns), BF16),
        pltpu.SemaphoreType.DMA((2 * groups,)),
    ]


def vocab_first(side, hidden, gain, weight):
    groups, _, span, columns = weight.shape

    def kernel(side_ref, h_any, g_ref, w_hbm, y_ref, sq_ref, *scratch):
        y_ref[...] = jnp.zeros_like(y_ref)
        sq_ref[...] = jnp.zeros_like(sq_ref)
        vocab_sum(side_ref, h_any, g_ref, w_hbm, y_ref, sq_ref, *scratch)

    vmem = pl.BlockSpec(memory_space=pltpu.VMEM)
    anywhere = pl.BlockSpec(memory_space=pl.ANY)
    return pl.pallas_call(
        kernel,
        out_shape=(jax.ShapeDtypeStruct((NODES, columns), F32), jax.ShapeDtypeStruct((NODES, 128), F32)),
        in_specs=[pl.BlockSpec(memory_space=pltpu.SMEM), anywhere, vmem, pl.BlockSpec(memory_space=pltpu.HBM)],
        out_specs=(vmem, vmem),
        scratch_shapes=vocab_scratch(hidden, weight),
        compiler_params=pltpu.CompilerParams(vmem_limit_bytes=24 << 20),
        cost_estimate=pl.CostEstimate(
            flops=2 * NODES * groups * span * columns, transcendentals=0, bytes_accessed=10 << 20
        ),
        name="vocab_first",
    )(side, hidden, gain, weight)


def vocab_second(side, hidden, gain, weight, y_first, sq_first, target, copies):
    groups, _, span, columns = weight.shape

    def kernel(side_ref, h_any, g_ref, w_hbm, y0_ref, sq0_ref, t_ref, o_ref, acc, sq, *scratch):
        acc[...] = y0_ref[...]
        sq[...] = sq0_ref[...]
        vocab_sum(side_ref, h_any, g_ref, w_hbm, acc, sq, *scratch)
        mean = jnp.sum(sq[...], axis=1, keepdims=True) / D
        logits = acc[...] * lax.rsqrt(mean + EPSILON)
        peak = jnp.max(logits, axis=1, keepdims=True)
        total = jnp.sum(jnp.exp(logits - peak), axis=1, keepdims=True)
        lse = peak + jnp.log(total)
        column = lax.broadcasted_iota(jnp.int32, (NODES, columns), 1)
        chosen = jnp.sum(jnp.where(column == t_ref[...], logits, 0.0), axis=1, keepdims=True)
        lane = lax.broadcasted_iota(jnp.int32, (NODES, 128), 1)
        rows = jnp.where(lane == 0, lse, jnp.where(lane == 1, chosen, 0.0)).T
        row = jnp.concatenate([rows[0:1, :], rows[1:2, :]], axis=1)
        for i in range(copies):
            o_ref[i] = row

    vmem = pl.BlockSpec(memory_space=pltpu.VMEM)
    anywhere = pl.BlockSpec(memory_space=pl.ANY)
    return pl.pallas_call(
        kernel,
        out_shape=jax.ShapeDtypeStruct((copies, 1, 2 * NODES), F32),
        in_specs=[pl.BlockSpec(memory_space=pltpu.SMEM), anywhere, vmem, pl.BlockSpec(memory_space=pltpu.HBM)] + [vmem] * 3,
        out_specs=vmem,
        scratch_shapes=[VM((NODES, columns), F32), VM((NODES, 128), F32)] + vocab_scratch(hidden, weight),
        compiler_params=pltpu.CompilerParams(vmem_limit_bytes=24 << 20),
        cost_estimate=pl.CostEstimate(
            flops=2 * NODES * groups * span * columns, transcendentals=1 << 16, bytes_accessed=10 << 20
        ),
        name="vocab_second",
    )(side, hidden, gain, weight, y_first, sq_first, target)


def final_score(stats, amateur):
    def kernel(s_ref, a_ref, o_ref):
        lse = s_ref[:, 0, 0:NODES]
        chosen = s_ref[:, 0, NODES : 2 * NODES]
        best = jnp.max(lse, axis=0, keepdims=True)
        total = jnp.sum(jnp.exp(lse - best), axis=0, keepdims=True)
        picked = jnp.sum(chosen, axis=0, keepdims=True)
        o_ref[...] = picked - (best + jnp.log(total)) - a_ref[...]

    vmem = pl.BlockSpec(memory_space=pltpu.VMEM)
    return pl.pallas_call(
        kernel,
        out_shape=jax.ShapeDtypeStruct((1, NODES), F32),
        in_specs=[vmem, vmem],
        out_specs=vmem,
        compiler_params=pltpu.CompilerParams(vmem_limit_bytes=8 << 20),
        name="final_score",
    )(stats, amateur)


def body(
    queries,
    cache_keys,
    cache_values,
    tree_keys,
    tree_values,
    ancestors,
    filled_extents,
    out_weight,
    residual,
    norm_gain,
    vocab_weight,
    candidates,
    amateur,
):
    positions = cache_keys.shape[1]
    seq_index = lax.axis_index(SEQ)
    head_index = lax.axis_index(HEAD)
    core = lax.axis_index("c")
    seq_size = lax.axis_size(SEQ)
    cores = lax.axis_size("c")
    chips = lax.axis_size(CHIPS)
    devices = chips * cores

    def scalar(x):
        return x.astype(jnp.int32).reshape(1)

    def swap(x):
        return lax.ppermute(x, "c", [(0, 1), (1, 0)])

    def in_hbm(x):
        return pltpu.with_memory_space_constraint(x, pltpu.HBM)

    own, other = scalar(core), scalar(1 - core)
    place = jnp.stack([seq_index * positions, core]).astype(jnp.int32)
    keep, send = attention(in_hbm(queries), in_hbm(cache_keys), in_hbm(cache_values), in_hbm(filled_extents), place)
    parts = merge(keep, swap(send))
    parts = lax.all_to_all(parts, ROWS, 0, 0, tiled=True)
    tree_sums, tree_stats = tree_part(queries, tree_keys, tree_values, ancestors, scalar(seq_index))
    attended = combine(parts, tree_sums, tree_stats)
    rows, columns = out_weight.shape
    weight = in_hbm(out_weight.reshape(rows // HD // cores, cores, HD, columns))
    attended = lax.all_to_all(attended, ROWS, 0, 0, tiled=True)
    swapped = swap(attended)
    projected = project(own, attended, weight)
    shares = project(other, swapped, weight, projected)
    shares = lax.all_to_all(shares, HEAD, 0, 0, tiled=True)
    hidden, repeated = finish_hidden(shares, residual, scalar(head_index), chips)
    own_side = lax.all_to_all(repeated, CHIPS, 0, 0, tiled=True)
    vocab_local = vocab_weight.shape[1]
    groups = seq_size // cores
    span = D // seq_size
    weight = in_hbm(vocab_weight.reshape(groups, cores, span, vocab_local))
    other_side = swap(own_side)
    gain = norm_gain.reshape(groups, cores, span // 128, 128)
    y, squares = vocab_first(own, own_side, gain, weight)
    target = (candidates - lax.axis_index(ALL) * vocab_local).reshape(NODES, 1)
    stats = vocab_second(other, other_side, gain, weight, y, squares, target, devices)
    stats = lax.all_to_all(stats, ALL, 0, 0, tiled=True)
    contrast = final_score(stats, amateur.reshape(1, NODES))
    return (hidden, contrast.reshape(NODES))


def solution(mesh):
    fine = Mesh(mesh.devices.reshape(2, 4, 2, 4, 2), ALL)
    in_specs = (
        P(None, HEAD),
        P(None, SEQ, HEAD),
        P(None, SEQ, HEAD),
        P(None, HEAD),
        P(None, HEAD),
        P(),
        P(),
        P(HEAD, SEQ),
        P(None, SEQ),
        P(),
        P(None, ALL),
        P(),
        P(),
    )
    out_specs = (P(None, ALL), P())
    return jax.shard_map(body, mesh=fine, in_specs=in_specs, out_specs=out_specs, check_vma=False)
```

```python
import math

import jax
import jax.numpy as jnp
from jax import lax
from jax.experimental import pallas as pl
from jax.experimental.pallas import tpu as pltpu
from jax.sharding import Mesh, PartitionSpec as P

NODES_REQ = 64
NODES = 128
D = 16384
HD = 128
EPSILON = 1e-05
NEG_FILL = -1e30
LOG2E = math.log2(math.e)
SCALE2 = HD ** (-0.5) * LOG2E

SEQ = ("zh", "y", "c")
HEAD = ("x", "zl")
ROWS = ("zh", "y")
CHIPS = ("zh", "y", "x", "zl")
ALL = SEQ + HEAD


F32 = jnp.float32
BF16 = jnp.bfloat16
VM = pltpu.VMEM
STAT_ROWS = 16
BLOCK_ROWS = 512
CHUNK = 2048


def nt_dot(a, b):
    return lax.dot_general(a, b, (((1,), (1,)), ((), ())), preferred_element_type=F32)


def thirds(x):
    hi = x.astype(BF16).astype(F32)
    rest = x - hi
    mid = rest.astype(BF16).astype(F32)
    return hi, mid, rest - mid


def attention(queries, keys, values, extents, place):
    requests, positions, _ = keys.shape
    heads = queries.shape[1] // HD
    per_block = BLOCK_ROWS // NODES_REQ
    blocks_req = heads // per_block
    blocks = requests * blocks_req
    chunks = positions // CHUNK

    half = heads // 2

    def kernel(ext_ref, place_ref, q_hbm, k_hbm, v_hbm, keep, send, q_ref, qs, kv, vv, turned, bias, s_buf, m_buf, acc, stat, sem):
        q_copy = pltpu.make_async_copy(q_hbm, q_ref, sem.at[2 * requests])
        q_copy.start()
        core = place_ref[1]
        copies = []
        for b in range(requests):
            copies.append(
                (
                    pltpu.make_async_copy(k_hbm.at[b], kv.at[b], sem.at[2 * b]),
                    pltpu.make_async_copy(v_hbm.at[b], vv.at[b], sem.at[2 * b + 1]),
                )
            )
        for pair in copies:
            for copy in pair:
                copy.start()
        index = lax.broadcasted_iota(jnp.int32, (positions, 128), 0)
        for b in range(requests):
            left = ext_ref[b] - place_ref[0]
            bias[b] = jnp.where(index < left, 0.0, NEG_FILL).astype(F32)
            turned[b, HD:, :] = jnp.ones((STAT_ROWS, positions), BF16)
        q_copy.wait()
        for g in range(heads):
            head = 2 * g + core if g < half else 2 * (g - half) + 1 - core
            at = pl.multiple_of(head * HD, HD)
            for b in range(requests):
                qs[b * blocks_req + g // per_block, (g % per_block) * NODES_REQ : (g % per_block + 1) * NODES_REQ, :] = (
                    q_ref[b * NODES_REQ : (b + 1) * NODES_REQ, pl.ds(at, HD)]
                )

        def scores(block, chunk, slot):
            b = block // blocks_req
            rows = pl.ds(pl.multiple_of(chunk * CHUNK, CHUNK), CHUNK)
            s = nt_dot(kv[b, rows, :], qs[block])
            shift = bias[b, rows, :]
            for t in range(BLOCK_ROWS // 128):
                lanes = slice(t * 128, (t + 1) * 128)
                piece = s[:, lanes] + shift
                s_buf[slot, chunk, :, lanes] = piece
                m_buf[slot, :, lanes] = jnp.maximum(m_buf[slot, :, lanes], jnp.max(piece.reshape(CHUNK // 8, 8, 128), axis=0))

        def weigh(block, chunk, slot, top):
            b = block // blocks_req
            columns = pl.ds(pl.multiple_of(chunk * CHUNK, CHUNK), CHUNK)
            pieces = []
            for t in range(BLOCK_ROWS // 128):
                lanes = slice(t * 128, (t + 1) * 128)
                scaled = s_buf[slot, chunk, :, lanes].reshape(CHUNK // 8, 8, 128) * SCALE2 - top[:, lanes][None]
                pieces.append(jnp.exp2(scaled).reshape(CHUNK, 128).astype(BF16))
            acc[...] += jnp.dot(turned[b, :, columns], jnp.concatenate(pieces, axis=1), preferred_element_type=F32)

        copies[0][0].wait()
        m_buf[0] = jnp.full((8, BLOCK_ROWS), NEG_FILL, F32)

        @pl.loop(0, chunks)
        def _(chunk):
            scores(0, chunk, 0)

        def finish(block, best):
            total = acc[HD : HD + 1, :]
            b = block // blocks_req
            j = block % blocks_req
            rows = slice(b * NODES_REQ, (b + 1) * NODES_REQ)
            lane = lax.broadcasted_iota(jnp.int32, (8, NODES), 1)
            mine = (lane // NODES_REQ) == b
            for t in range(BLOCK_ROWS // 128):
                lanes = slice(t * 128, (t + 1) * 128)
                sums = acc[0:HD, lanes].T.astype(BF16)
                facts = jnp.concatenate(
                    thirds(best[:, lanes]) + thirds(total[:, lanes]) + (jnp.zeros((2, 128), F32),), axis=0
                )
                swapped = pltpu.roll(facts, NODES_REQ, 1)
                for i in range(2):
                    g = j * per_block + 2 * t + i
                    out = keep if g < half else send
                    out[g % half, rows, :] = sums[i * NODES_REQ : (i + 1) * NODES_REQ, :]
                    row = facts if i == b else swapped
                    stat[g] = row if b == 0 else jnp.where(mine, row, stat[g])

        for block in range(blocks):
            last = block == blocks - 1
            slot = block % 2
            b = block // blocks_req
            if block % blocks_req == 0:
                copies[b][1].wait()

                @pl.loop(0, positions // 512)
                def _(i):
                    at = pl.multiple_of(i * 512, 512)
                    turned[b, 0:HD, pl.ds(at, 512)] = vv[b, pl.ds(at, 512), :].T

            if not last and (block + 1) % blocks_req == 0:
                copies[(block + 1) // blocks_req][0].wait()
            best = jnp.max(m_buf[slot], axis=0, keepdims=True)
            best = jnp.maximum(best, 0.5 * NEG_FILL) * SCALE2
            top = jnp.broadcast_to(best, (8, BLOCK_ROWS))
            acc[...] = jnp.zeros_like(acc)
            if not last:
                m_buf[1 - slot] = jnp.full((8, BLOCK_ROWS), NEG_FILL, F32)

            @pl.loop(0, chunks)
            def _(chunk):
                if not last:
                    scores(block + 1, chunk, 1 - slot)
                weigh(block, chunk, slot, top)

            finish(block, best)

        for g in range(heads):
            out = keep if g < half else send
            out[g % half, NODES : NODES + STAT_ROWS, :] = jnp.concatenate(
                [stat[g], jnp.zeros((STAT_ROWS - 8, NODES), F32)], axis=0
            ).astype(BF16)

    smem = pl.BlockSpec(memory_space=pltpu.SMEM)
    vmem = pl.BlockSpec(memory_space=pltpu.VMEM)
    hbm = pl.BlockSpec(memory_space=pltpu.HBM)
    out = jax.ShapeDtypeStruct((half, NODES + STAT_ROWS, HD), BF16)
    return pl.pallas_call(
        kernel,
        out_shape=(out, out),
        in_specs=[smem, smem, hbm, hbm, hbm],
        out_specs=(vmem, vmem),
        scratch_shapes=[
            VM((NODES, heads * HD), BF16),
            VM((blocks, BLOCK_ROWS, HD), BF16),
            VM((requests, positions, HD), BF16),
            VM((requests, positions, HD), BF16),
            VM((requests, HD + STAT_ROWS, positions), BF16),
            VM((requests, positions, 128), F32),
            VM((2, chunks, CHUNK, BLOCK_ROWS), F32),
            VM((2, 8, BLOCK_ROWS), F32),
            VM((HD + STAT_ROWS, BLOCK_ROWS), F32),
            VM((heads, 8, NODES), F32),
            pltpu.SemaphoreType.DMA((2 * requests + 1,)),
        ],
        compiler_params=pltpu.CompilerParams(vmem_limit_bytes=48 << 20),
        cost_estimate=pl.CostEstimate(
            flops=4 * NODES * heads * positions * HD, transcendentals=NODES * heads * positions, bytes_accessed=5 << 20
        ),
        name="attention",
    )(extents, place, queries, keys, values)


def tree_part(queries, tree_keys, tree_values, ancestors, head):
    requests = ancestors.shape[0]

    def kernel(head_ref, q_ref, k_ref, v_ref, a_ref, o_ref, st_ref):
        at = pl.multiple_of(head_ref[0] * HD, HD)
        slots = lax.broadcasted_iota(jnp.int32, (NODES_REQ, 128), 1)
        for b in range(requests):
            rows = slice(b * NODES_REQ, (b + 1) * NODES_REQ)
            s = nt_dot(q_ref[rows, pl.ds(at, HD)], k_ref[rows, :])
            live = a_ref[b] > 0
            s = jnp.where(live, s * SCALE2, NEG_FILL)
            top = jnp.max(s, axis=1, keepdims=True)
            w = jnp.where(live, jnp.exp2(s - top), 0.0)
            total = jnp.sum(w, axis=1, keepdims=True)
            o_ref[rows, :] = jnp.dot(w.astype(BF16), v_ref[rows, :], preferred_element_type=F32)
            st_ref[rows, :] = jnp.where(slots == 0, top, jnp.where(slots == 1, total, 0.0))
        st_ref[...] = st_ref[...].T

    vmem = pl.BlockSpec(memory_space=pltpu.VMEM)
    return pl.pallas_call(
        kernel,
        out_shape=(jax.ShapeDtypeStruct((NODES, HD), F32), jax.ShapeDtypeStruct((128, NODES), F32)),
        in_specs=[pl.BlockSpec(memory_space=pltpu.SMEM)] + [vmem] * 4,
        out_specs=(vmem, vmem),
        compiler_params=pltpu.CompilerParams(vmem_limit_bytes=8 << 20),
        cost_estimate=pl.CostEstimate(flops=1 << 22, transcendentals=8192, bytes_accessed=1 << 20),
        name="tree_part",
    )(head, queries, tree_keys, tree_values, ancestors)


def merge(first, second):
    heads = first.shape[0]

    def kernel(a_ref, b_ref, o_ref):
        rows = []
        columns = []
        for g in range(heads):
            a = a_ref[g, NODES : NODES + STAT_ROWS, :].astype(F32)
            b = b_ref[g, NODES : NODES + STAT_ROWS, :].astype(F32)
            top_a = a[0:1] + a[1:2] + a[2:3]
            top_b = b[0:1] + b[1:2] + b[2:3]
            top = jnp.maximum(top_a, top_b)
            fa = jnp.exp2(top_a - top)
            fb = jnp.exp2(top_b - top)
            total = fa * (a[3:4] + a[4:5] + a[5:6]) + fb * (b[3:4] + b[4:5] + b[5:6])
            rows.append(jnp.concatenate(thirds(top) + thirds(total) + (jnp.zeros((STAT_ROWS - 6, NODES), F32),), axis=0))
            columns += [fa, fb]
        columns.append(jnp.zeros((128 - 2 * heads, NODES), F32))
        factor = jnp.concatenate(columns, axis=0).T
        for g in range(heads):
            o_ref[g, 0:NODES, :] = (
                a_ref[g, 0:NODES, :].astype(F32) * factor[:, 2 * g : 2 * g + 1]
                + b_ref[g, 0:NODES, :].astype(F32) * factor[:, 2 * g + 1 : 2 * g + 2]
            ).astype(BF16)
            o_ref[g, NODES : NODES + STAT_ROWS, :] = rows[g].astype(BF16)

    vmem = pl.BlockSpec(memory_space=pltpu.VMEM)
    return pl.pallas_call(
        kernel,
        out_shape=jax.ShapeDtypeStruct(first.shape, BF16),
        in_specs=[vmem] * 2,
        out_specs=vmem,
        compiler_params=pltpu.CompilerParams(vmem_limit_bytes=8 << 20),
        cost_estimate=pl.CostEstimate(flops=1 << 20, transcendentals=4096, bytes_accessed=1 << 20),
        name="merge",
    )(first, second)


def combine(parts, tree_sums, tree_stats):
    sources = parts.shape[0]

    def kernel(p_ref, t_ref, ts_ref, o_ref):
        tops = []
        totals = []
        for s in range(sources):
            st = p_ref[s, NODES : NODES + STAT_ROWS, :].astype(F32)
            tops.append(st[0:1] + st[1:2] + st[2:3])
            totals.append(st[3:4] + st[4:5] + st[5:6])
        tops.append(ts_ref[0:1, :])
        totals.append(ts_ref[1:2, :])
        tops = jnp.concatenate(tops + [jnp.full((24 - sources - 1, NODES), NEG_FILL, F32)], axis=0)
        totals = jnp.concatenate(totals + [jnp.zeros((24 - sources - 1, NODES), F32)], axis=0)
        best = jnp.max(tops, axis=0, keepdims=True)
        factor = jnp.exp2(tops - best)
        factor = factor / jnp.sum(factor * totals, axis=0, keepdims=True)
        factor = jnp.concatenate([factor, jnp.zeros((128 - 24, NODES), F32)], axis=0).T
        out = t_ref[...] * factor[:, sources : sources + 1]
        for s in range(sources):
            out = out + p_ref[s, 0:NODES, :].astype(F32) * factor[:, s : s + 1]
        out = out.astype(BF16)
        for s in range(sources):
            o_ref[s] = out

    vmem = pl.BlockSpec(memory_space=pltpu.VMEM)
    return pl.pallas_call(
        kernel,
        out_shape=jax.ShapeDtypeStruct((sources, NODES, HD), BF16),
        in_specs=[vmem] * 3,
        out_specs=vmem,
        compiler_params=pltpu.CompilerParams(vmem_limit_bytes=8 << 20),
        cost_estimate=pl.CostEstimate(flops=1 << 20, transcendentals=4096, bytes_accessed=1 << 20),
        name="combine",
    )(parts, tree_sums, tree_stats)


def bring(side, weight, after):
    heads, _, span, columns = weight.shape

    def kernel(side_ref, w_hbm, after_ref, o_ref, sem):
        copies = [pltpu.make_async_copy(w_hbm.at[g, side_ref[0]], o_ref.at[g], sem.at[g]) for g in range(heads)]
        for copy in copies:
            copy.start()
        for copy in copies:
            copy.wait()

    anywhere = pl.BlockSpec(memory_space=pl.ANY)
    held = pl.pallas_call(
        kernel,
        out_shape=jax.ShapeDtypeStruct((heads, span, columns), BF16),
        in_specs=[pl.BlockSpec(memory_space=pltpu.SMEM), pl.BlockSpec(memory_space=pltpu.HBM), anywhere],
        out_specs=anywhere,
        scratch_shapes=[pltpu.SemaphoreType.DMA((heads,))],
        compiler_params=pltpu.CompilerParams(vmem_limit_bytes=1 << 20),
        cost_estimate=pl.CostEstimate(flops=0, transcendentals=0, bytes_accessed=4 << 20),
        name="bring",
    )(side, weight, after)
    return pltpu.with_memory_space_constraint(held, pltpu.VMEM)


def own_rows(attended, w_ref):
    heads, span, columns = w_ref.shape
    x = jnp.concatenate([attended[g] for g in range(heads)], axis=1)
    return jnp.dot(x, w_ref[...].reshape(heads * span, columns), preferred_element_type=F32)


def project_own(other, attended, held, weight):
    heads, span, columns = held.shape

    def kernel(other_ref, a_ref, h_ref, w_hbm, y_ref, o_ref, sem):
        copies = [pltpu.make_async_copy(w_hbm.at[g, other_ref[0]], o_ref.at[g], sem.at[g]) for g in range(heads)]
        for copy in copies:
            copy.start()
        y_ref[...] = own_rows(a_ref, h_ref)
        for copy in copies:
            copy.wait()

    vmem = pl.BlockSpec(memory_space=pltpu.VMEM)
    y, fetched = pl.pallas_call(
        kernel,
        out_shape=(jax.ShapeDtypeStruct((NODES, columns), F32), jax.ShapeDtypeStruct(held.shape, BF16)),
        in_specs=[pl.BlockSpec(memory_space=pltpu.SMEM), vmem, vmem, pl.BlockSpec(memory_space=pltpu.HBM)],
        out_specs=(vmem, pl.BlockSpec(memory_space=pl.ANY)),
        scratch_shapes=[pltpu.SemaphoreType.DMA((heads,))],
        compiler_params=pltpu.CompilerParams(vmem_limit_bytes=8 << 20),
        cost_estimate=pl.CostEstimate(flops=2 * NODES * heads * span * columns, transcendentals=0, bytes_accessed=4 << 20),
        name="project_own",
    )(other, attended, held, weight)
    return y, pltpu.with_memory_space_constraint(fetched, pltpu.VMEM)


def project_other(attended, fetched, so_far):
    columns = fetched.shape[2]

    def kernel(a_ref, w_ref, y_ref, o_ref):
        y = (y_ref[...] + own_rows(a_ref, w_ref)).astype(BF16)
        for i in range(columns // 128):
            o_ref[i] = y[:, i * 128 : (i + 1) * 128]

    vmem = pl.BlockSpec(memory_space=pltpu.VMEM)
    return pl.pallas_call(
        kernel,
        out_shape=jax.ShapeDtypeStruct((columns // 128, NODES, 128), BF16),
        in_specs=[vmem] * 3,
        out_specs=vmem,
        compiler_params=pltpu.CompilerParams(vmem_limit_bytes=8 << 20),
        cost_estimate=pl.CostEstimate(flops=2 * NODES * fetched.size, transcendentals=0, bytes_accessed=1 << 20),
        name="project_other",
    )(attended, fetched, so_far)


def finish_hidden(shares, residual, position, copies):
    sources = shares.shape[0]

    def kernel(pos_ref, s_ref, r_ref, h_ref, o_ref):
        at = pl.multiple_of(pos_ref[0] * 128, 128)
        total = s_ref[0].astype(F32)
        for s in range(1, sources):
            total = total + s_ref[s].astype(F32)
        h = (r_ref[:, pl.ds(at, 128)].astype(F32) + total).astype(BF16)
        h_ref[...] = h
        for i in range(copies):
            o_ref[i] = h

    vmem = pl.BlockSpec(memory_space=pltpu.VMEM)
    return pl.pallas_call(
        kernel,
        out_shape=(
            jax.ShapeDtypeStruct((NODES, 128), BF16),
            jax.ShapeDtypeStruct((copies, NODES, 128), BF16),
        ),
        in_specs=[pl.BlockSpec(memory_space=pltpu.SMEM), vmem, vmem],
        out_specs=(vmem, vmem),
        compiler_params=pltpu.CompilerParams(vmem_limit_bytes=8 << 20),
        cost_estimate=pl.CostEstimate(flops=1 << 18, transcendentals=0, bytes_accessed=3 << 20),
        name="finish_hidden",
    )(position, shares, residual)


def vocab_sum(side_ref, h_any, g_ref, w_hbm, y_ref, sq_ref, h_buf, w_buf, sem):
    groups, _, span, _ = w_hbm.shape
    blocks = span // 128
    side = side_ref[0]

    def copies(group):
        at = pl.ds(group * blocks, blocks)
        return (
            pltpu.make_async_copy(h_any.at[at], h_buf.at[at], sem.at[2 * group]),
            pltpu.make_async_copy(w_hbm.at[group, side], w_buf.at[group], sem.at[2 * group + 1]),
        )

    for group in range(groups):
        for copy in copies(group):
            copy.start()

    @pl.loop(0, groups)
    def _(group):
        for copy in copies(group):
            copy.wait()
        pieces = []
        squares = sq_ref[...]
        for i in range(blocks):
            h = h_buf[group * blocks + i].astype(F32)
            squares = squares + h * h
            pieces.append((h * g_ref[group, side, i : i + 1, :].astype(F32)).astype(BF16))
        sq_ref[...] = squares
        x = jnp.concatenate(pieces, axis=1)
        y_ref[...] += jnp.dot(x, w_buf[group], preferred_element_type=F32)


def vocab_scratch(hidden, weight):
    groups, _, span, columns = weight.shape
    return [
        VM(hidden.shape, BF16),
        VM((groups, span, columns), BF16),
        pltpu.SemaphoreType.DMA((2 * groups,)),
    ]


def vocab_first(side, hidden, gain, weight):
    groups, _, span, columns = weight.shape

    def kernel(side_ref, h_any, g_ref, w_hbm, y_ref, sq_ref, *scratch):
        y_ref[...] = jnp.zeros_like(y_ref)
        sq_ref[...] = jnp.zeros_like(sq_ref)
        vocab_sum(side_ref, h_any, g_ref, w_hbm, y_ref, sq_ref, *scratch)

    vmem = pl.BlockSpec(memory_space=pltpu.VMEM)
    anywhere = pl.BlockSpec(memory_space=pl.ANY)
    return pl.pallas_call(
        kernel,
        out_shape=(jax.ShapeDtypeStruct((NODES, columns), F32), jax.ShapeDtypeStruct((NODES, 128), F32)),
        in_specs=[pl.BlockSpec(memory_space=pltpu.SMEM), anywhere, vmem, pl.BlockSpec(memory_space=pltpu.HBM)],
        out_specs=(vmem, vmem),
        scratch_shapes=vocab_scratch(hidden, weight),
        compiler_params=pltpu.CompilerParams(vmem_limit_bytes=24 << 20),
        cost_estimate=pl.CostEstimate(
            flops=2 * NODES * groups * span * columns, transcendentals=0, bytes_accessed=10 << 20
        ),
        name="vocab_first",
    )(side, hidden, gain, weight)


def vocab_second(side, hidden, gain, weight, y_first, sq_first, target, copies):
    groups, _, span, columns = weight.shape

    def kernel(side_ref, h_any, g_ref, w_hbm, y0_ref, sq0_ref, t_ref, o_ref, acc, sq, *scratch):
        acc[...] = y0_ref[...]
        sq[...] = sq0_ref[...]
        vocab_sum(side_ref, h_any, g_ref, w_hbm, acc, sq, *scratch)
        mean = jnp.sum(sq[...], axis=1, keepdims=True) / D
        logits = acc[...] * lax.rsqrt(mean + EPSILON)
        peak = jnp.max(logits, axis=1, keepdims=True)
        total = jnp.sum(jnp.exp(logits - peak), axis=1, keepdims=True)
        lse = peak + jnp.log(total)
        column = lax.broadcasted_iota(jnp.int32, (NODES, columns), 1)
        chosen = jnp.sum(jnp.where(column == t_ref[...], logits, 0.0), axis=1, keepdims=True)
        lane = lax.broadcasted_iota(jnp.int32, (NODES, 128), 1)
        rows = jnp.where(lane == 0, lse, jnp.where(lane == 1, chosen, 0.0)).T
        row = jnp.concatenate([rows[0:1, :], rows[1:2, :]], axis=1)
        for i in range(copies):
            o_ref[i] = row

    vmem = pl.BlockSpec(memory_space=pltpu.VMEM)
    anywhere = pl.BlockSpec(memory_space=pl.ANY)
    return pl.pallas_call(
        kernel,
        out_shape=jax.ShapeDtypeStruct((copies, 1, 2 * NODES), F32),
        in_specs=[pl.BlockSpec(memory_space=pltpu.SMEM), anywhere, vmem, pl.BlockSpec(memory_space=pltpu.HBM)] + [vmem] * 3,
        out_specs=vmem,
        scratch_shapes=[VM((NODES, columns), F32), VM((NODES, 128), F32)] + vocab_scratch(hidden, weight),
        compiler_params=pltpu.CompilerParams(vmem_limit_bytes=24 << 20),
        cost_estimate=pl.CostEstimate(
            flops=2 * NODES * groups * span * columns, transcendentals=1 << 16, bytes_accessed=10 << 20
        ),
        name="vocab_second",
    )(side, hidden, gain, weight, y_first, sq_first, target)


def final_score(stats, amateur):
    def kernel(s_ref, a_ref, o_ref):
        lse = s_ref[:, 0, 0:NODES]
        chosen = s_ref[:, 0, NODES : 2 * NODES]
        best = jnp.max(lse, axis=0, keepdims=True)
        total = jnp.sum(jnp.exp(lse - best), axis=0, keepdims=True)
        picked = jnp.sum(chosen, axis=0, keepdims=True)
        o_ref[...] = picked - (best + jnp.log(total)) - a_ref[...]

    vmem = pl.BlockSpec(memory_space=pltpu.VMEM)
    return pl.pallas_call(
        kernel,
        out_shape=jax.ShapeDtypeStruct((1, NODES), F32),
        in_specs=[vmem, vmem],
        out_specs=vmem,
        compiler_params=pltpu.CompilerParams(vmem_limit_bytes=8 << 20),
        name="final_score",
    )(stats, amateur)


def body(
    queries,
    cache_keys,
    cache_values,
    tree_keys,
    tree_values,
    ancestors,
    filled_extents,
    out_weight,
    residual,
    norm_gain,
    vocab_weight,
    candidates,
    amateur,
):
    positions = cache_keys.shape[1]
    seq_index = lax.axis_index(SEQ)
    head_index = lax.axis_index(HEAD)
    core = lax.axis_index("c")
    seq_size = lax.axis_size(SEQ)
    cores = lax.axis_size("c")
    chips = lax.axis_size(CHIPS)
    devices = chips * cores

    def scalar(x):
        return x.astype(jnp.int32).reshape(1)

    def swap(x):
        return lax.ppermute(x, "c", [(0, 1), (1, 0)])

    def in_hbm(x):
        return pltpu.with_memory_space_constraint(x, pltpu.HBM)

    own, other = scalar(core), scalar(1 - core)
    place = jnp.stack([seq_index * positions, core]).astype(jnp.int32)
    keep, send = attention(in_hbm(queries), in_hbm(cache_keys), in_hbm(cache_values), in_hbm(filled_extents), place)
    parts = merge(keep, swap(send))
    parts = lax.all_to_all(parts, ROWS, 0, 0, tiled=True)
    tree_sums, tree_stats = tree_part(queries, tree_keys, tree_values, ancestors, scalar(seq_index))
    attended = combine(parts, tree_sums, tree_stats)
    rows, columns = out_weight.shape
    weight = in_hbm(out_weight.reshape(rows // HD // cores, cores, HD, columns))
    held = bring(own, weight, attended)
    attended = lax.all_to_all(attended, ROWS, 0, 0, tiled=True)
    swapped = swap(attended)
    projected, fetched = project_own(other, attended, held, weight)
    shares = project_other(swapped, fetched, projected)
    shares = lax.all_to_all(shares, HEAD, 0, 0, tiled=True)
    hidden, repeated = finish_hidden(shares, residual, scalar(head_index), chips)
    own_side = lax.all_to_all(repeated, CHIPS, 0, 0, tiled=True)
    vocab_local = vocab_weight.shape[1]
    groups = seq_size // cores
    span = D // seq_size
    weight = in_hbm(vocab_weight.reshape(groups, cores, span, vocab_local))
    other_side = swap(own_side)
    gain = norm_gain.reshape(groups, cores, span // 128, 128)
    y, squares = vocab_first(own, own_side, gain, weight)
    target = (candidates - lax.axis_index(ALL) * vocab_local).reshape(NODES, 1)
    stats = vocab_second(other, other_side, gain, weight, y, squares, target, devices)
    stats = lax.all_to_all(stats, ALL, 0, 0, tiled=True)
    contrast = final_score(stats, amateur.reshape(1, NODES))
    return (hidden, contrast.reshape(NODES))


def solution(mesh):
    fine = Mesh(mesh.devices.reshape(2, 4, 2, 4, 2), ALL)
    in_specs = (
        P(None, HEAD),
        P(None, SEQ, HEAD),
        P(None, SEQ, HEAD),
        P(None, HEAD),
        P(None, HEAD),
        P(),
        P(),
        P(HEAD, SEQ),
        P(None, SEQ),
        P(),
        P(None, ALL),
        P(),
        P(),
    )
    out_specs = (P(None, ALL), P())

    return jax.shard_map(body, mesh=fine, in_specs=in_specs, out_specs=out_specs, check_vma=False)
```

```python
import math

import jax
import jax.numpy as jnp
from jax import lax
from jax.experimental import pallas as pl
from jax.experimental.pallas import tpu as pltpu
from jax.sharding import Mesh, PartitionSpec as P

NODES_REQ = 64
NODES = 128
D = 16384
HD = 128
EPSILON = 1e-05
NEG_FILL = -1e30
LOG2E = math.log2(math.e)
SCALE2 = HD ** (-0.5) * LOG2E

SEQ = ("zh", "y", "c")
HEAD = ("x", "zl")
ROWS = ("zh", "y")
CHIPS = ("zh", "y", "x", "zl")
ALL = SEQ + HEAD


F32 = jnp.float32
BF16 = jnp.bfloat16
VM = pltpu.VMEM
STAT_ROWS = 16
BLOCK_ROWS = 512
CHUNK = 2048


def nt_dot(a, b):
    return lax.dot_general(a, b, (((1,), (1,)), ((), ())), preferred_element_type=F32)


def thirds(x):
    hi = x.astype(BF16).astype(F32)
    rest = x - hi
    mid = rest.astype(BF16).astype(F32)
    return hi, mid, rest - mid


def attention(queries, keys, values, extents, place):
    requests, positions, _ = keys.shape
    heads = queries.shape[1] // HD
    per_block = BLOCK_ROWS // NODES_REQ
    blocks_req = heads // per_block
    blocks = requests * blocks_req
    chunks = positions // CHUNK

    half = heads // 2

    def kernel(ext_ref, place_ref, q_hbm, k_hbm, v_hbm, keep, send, q_ref, qs, kv, vv, turned, bias, s_buf, m_buf, acc, stat, sem):
        q_copy = pltpu.make_async_copy(q_hbm, q_ref, sem.at[2 * requests])
        q_copy.start()
        core = place_ref[1]
        copies = []
        for b in range(requests):
            copies.append(
                (
                    pltpu.make_async_copy(k_hbm.at[b], kv.at[b], sem.at[2 * b]),
                    pltpu.make_async_copy(v_hbm.at[b], vv.at[b], sem.at[2 * b + 1]),
                )
            )
        for pair in copies:
            for copy in pair:
                copy.start()
        index = lax.broadcasted_iota(jnp.int32, (positions, 128), 0)
        for b in range(requests):
            left = ext_ref[b] - place_ref[0]
            bias[b] = jnp.where(index < left, 0.0, NEG_FILL).astype(F32)
            turned[b, HD:, :] = jnp.ones((STAT_ROWS, positions), BF16)
        q_copy.wait()
        for g in range(heads):
            head = 2 * g + core if g < half else 2 * (g - half) + 1 - core
            at = pl.multiple_of(head * HD, HD)
            for b in range(requests):
                qs[b * blocks_req + g // per_block, (g % per_block) * NODES_REQ : (g % per_block + 1) * NODES_REQ, :] = (
                    q_ref[b * NODES_REQ : (b + 1) * NODES_REQ, pl.ds(at, HD)]
                )

        def scores(block, chunk, slot):
            b = block // blocks_req
            rows = pl.ds(pl.multiple_of(chunk * CHUNK, CHUNK), CHUNK)
            s = nt_dot(kv[b, rows, :], qs[block])
            shift = bias[b, rows, :]
            for t in range(BLOCK_ROWS // 128):
                lanes = slice(t * 128, (t + 1) * 128)
                piece = s[:, lanes] + shift
                s_buf[slot, chunk, :, lanes] = piece
                m_buf[slot, :, lanes] = jnp.maximum(m_buf[slot, :, lanes], jnp.max(piece.reshape(CHUNK // 8, 8, 128), axis=0))

        def weigh(block, chunk, slot, top):
            b = block // blocks_req
            columns = pl.ds(pl.multiple_of(chunk * CHUNK, CHUNK), CHUNK)
            pieces = []
            for t in range(BLOCK_ROWS // 128):
                lanes = slice(t * 128, (t + 1) * 128)
                scaled = s_buf[slot, chunk, :, lanes].reshape(CHUNK // 8, 8, 128) * SCALE2 - top[:, lanes][None]
                pieces.append(jnp.exp2(scaled).reshape(CHUNK, 128).astype(BF16))
            acc[...] += jnp.dot(turned[b, :, columns], jnp.concatenate(pieces, axis=1), preferred_element_type=F32)

        copies[0][0].wait()
        m_buf[0] = jnp.full((8, BLOCK_ROWS), NEG_FILL, F32)

        @pl.loop(0, chunks)
        def _(chunk):
            scores(0, chunk, 0)

        def finish(block, best):
            total = acc[HD : HD + 1, :]
            b = block // blocks_req
            j = block % blocks_req
            rows = slice(b * NODES_REQ, (b + 1) * NODES_REQ)
            lane = lax.broadcasted_iota(jnp.int32, (8, NODES), 1)
            mine = (lane // NODES_REQ) == b
            for t in range(BLOCK_ROWS // 128):
                lanes = slice(t * 128, (t + 1) * 128)
                sums = acc[0:HD, lanes].T.astype(BF16)
                facts = jnp.concatenate(
                    thirds(best[:, lanes]) + thirds(total[:, lanes]) + (jnp.zeros((2, 128), F32),), axis=0
                )
                swapped = pltpu.roll(facts, NODES_REQ, 1)
                for i in range(2):
                    g = j * per_block + 2 * t + i
                    out = keep if g < half else send
                    out[g % half, rows, :] = sums[i * NODES_REQ : (i + 1) * NODES_REQ, :]
                    row = facts if i == b else swapped
                    stat[g] = row if b == 0 else jnp.where(mine, row, stat[g])

        for block in range(blocks):
            last = block == blocks - 1
            slot = block % 2
            b = block // blocks_req
            if block % blocks_req == 0:
                copies[b][1].wait()

                @pl.loop(0, positions // 512)
                def _(i):
                    at = pl.multiple_of(i * 512, 512)
                    turned[b, 0:HD, pl.ds(at, 512)] = vv[b, pl.ds(at, 512), :].T

            if not last and (block + 1) % blocks_req == 0:
                copies[(block + 1) // blocks_req][0].wait()
            best = jnp.max(m_buf[slot], axis=0, keepdims=True)
            best = jnp.maximum(best, 0.5 * NEG_FILL) * SCALE2
            top = jnp.broadcast_to(best, (8, BLOCK_ROWS))
            acc[...] = jnp.zeros_like(acc)
            if not last:
                m_buf[1 - slot] = jnp.full((8, BLOCK_ROWS), NEG_FILL, F32)

            @pl.loop(0, chunks)
            def _(chunk):
                if not last:
                    scores(block + 1, chunk, 1 - slot)
                weigh(block, chunk, slot, top)

            finish(block, best)

        for g in range(heads):
            out = keep if g < half else send
            out[g % half, NODES : NODES + STAT_ROWS, :] = jnp.concatenate(
                [stat[g], jnp.zeros((STAT_ROWS - 8, NODES), F32)], axis=0
            ).astype(BF16)

    smem = pl.BlockSpec(memory_space=pltpu.SMEM)
    vmem = pl.BlockSpec(memory_space=pltpu.VMEM)
    hbm = pl.BlockSpec(memory_space=pltpu.HBM)
    out = jax.ShapeDtypeStruct((half, NODES + STAT_ROWS, HD), BF16)
    return pl.pallas_call(
        kernel,
        out_shape=(out, out),
        in_specs=[smem, smem, hbm, hbm, hbm],
        out_specs=(vmem, vmem),
        scratch_shapes=[
            VM((NODES, heads * HD), BF16),
            VM((blocks, BLOCK_ROWS, HD), BF16),
            VM((requests, positions, HD), BF16),
            VM((requests, positions, HD), BF16),
            VM((requests, HD + STAT_ROWS, positions), BF16),
            VM((requests, positions, 128), F32),
            VM((2, chunks, CHUNK, BLOCK_ROWS), F32),
            VM((2, 8, BLOCK_ROWS), F32),
            VM((HD + STAT_ROWS, BLOCK_ROWS), F32),
            VM((heads, 8, NODES), F32),
            pltpu.SemaphoreType.DMA((2 * requests + 1,)),
        ],
        compiler_params=pltpu.CompilerParams(vmem_limit_bytes=48 << 20),
        cost_estimate=pl.CostEstimate(
            flops=4 * NODES * heads * positions * HD, transcendentals=NODES * heads * positions, bytes_accessed=5 << 20
        ),
        name="attention",
    )(extents, place, queries, keys, values)


def tree_part(queries, tree_keys, tree_values, ancestors, head):
    requests = ancestors.shape[0]

    def kernel(head_ref, q_ref, k_ref, v_ref, a_ref, o_ref, st_ref):
        at = pl.multiple_of(head_ref[0] * HD, HD)
        slots = lax.broadcasted_iota(jnp.int32, (NODES_REQ, 128), 1)
        for b in range(requests):
            rows = slice(b * NODES_REQ, (b + 1) * NODES_REQ)
            s = nt_dot(q_ref[rows, pl.ds(at, HD)], k_ref[rows, :])
            live = a_ref[b] > 0
            s = jnp.where(live, s * SCALE2, NEG_FILL)
            top = jnp.max(s, axis=1, keepdims=True)
            w = jnp.where(live, jnp.exp2(s - top), 0.0)
            total = jnp.sum(w, axis=1, keepdims=True)
            o_ref[rows, :] = jnp.dot(w.astype(BF16), v_ref[rows, :], preferred_element_type=F32)
            st_ref[rows, :] = jnp.where(slots == 0, top, jnp.where(slots == 1, total, 0.0))
        st_ref[...] = st_ref[...].T

    vmem = pl.BlockSpec(memory_space=pltpu.VMEM)
    return pl.pallas_call(
        kernel,
        out_shape=(jax.ShapeDtypeStruct((NODES, HD), F32), jax.ShapeDtypeStruct((128, NODES), F32)),
        in_specs=[pl.BlockSpec(memory_space=pltpu.SMEM)] + [vmem] * 4,
        out_specs=(vmem, vmem),
        compiler_params=pltpu.CompilerParams(vmem_limit_bytes=8 << 20),
        cost_estimate=pl.CostEstimate(flops=1 << 22, transcendentals=8192, bytes_accessed=1 << 20),
        name="tree_part",
    )(head, queries, tree_keys, tree_values, ancestors)


def merge(first, second):
    heads = first.shape[0]

    def kernel(a_ref, b_ref, o_ref):
        rows = []
        columns = []
        for g in range(heads):
            a = a_ref[g, NODES : NODES + STAT_ROWS, :].astype(F32)
            b = b_ref[g, NODES : NODES + STAT_ROWS, :].astype(F32)
            top_a = a[0:1] + a[1:2] + a[2:3]
            top_b = b[0:1] + b[1:2] + b[2:3]
            top = jnp.maximum(top_a, top_b)
            fa = jnp.exp2(top_a - top)
            fb = jnp.exp2(top_b - top)
            total = fa * (a[3:4] + a[4:5] + a[5:6]) + fb * (b[3:4] + b[4:5] + b[5:6])
            rows.append(jnp.concatenate(thirds(top) + thirds(total) + (jnp.zeros((STAT_ROWS - 6, NODES), F32),), axis=0))
            columns += [fa, fb]
        columns.append(jnp.zeros((128 - 2 * heads, NODES), F32))
        factor = jnp.concatenate(columns, axis=0).T
        for g in range(heads):
            o_ref[g, 0:NODES, :] = (
                a_ref[g, 0:NODES, :].astype(F32) * factor[:, 2 * g : 2 * g + 1]
                + b_ref[g, 0:NODES, :].astype(F32) * factor[:, 2 * g + 1 : 2 * g + 2]
            ).astype(BF16)
            o_ref[g, NODES : NODES + STAT_ROWS, :] = rows[g].astype(BF16)

    vmem = pl.BlockSpec(memory_space=pltpu.VMEM)
    return pl.pallas_call(
        kernel,
        out_shape=jax.ShapeDtypeStruct(first.shape, BF16),
        in_specs=[vmem] * 2,
        out_specs=vmem,
        compiler_params=pltpu.CompilerParams(vmem_limit_bytes=8 << 20),
        cost_estimate=pl.CostEstimate(flops=1 << 20, transcendentals=4096, bytes_accessed=1 << 20),
        name="merge",
    )(first, second)


def combine(parts, tree_sums, tree_stats):
    sources = parts.shape[0]

    def kernel(p_ref, t_ref, ts_ref, o_ref):
        tops = []
        totals = []
        for s in range(sources):
            st = p_ref[s, NODES : NODES + STAT_ROWS, :].astype(F32)
            tops.append(st[0:1] + st[1:2] + st[2:3])
            totals.append(st[3:4] + st[4:5] + st[5:6])
        tops.append(ts_ref[0:1, :])
        totals.append(ts_ref[1:2, :])
        tops = jnp.concatenate(tops + [jnp.full((24 - sources - 1, NODES), NEG_FILL, F32)], axis=0)
        totals = jnp.concatenate(totals + [jnp.zeros((24 - sources - 1, NODES), F32)], axis=0)
        best = jnp.max(tops, axis=0, keepdims=True)
        factor = jnp.exp2(tops - best)
        factor = factor / jnp.sum(factor * totals, axis=0, keepdims=True)
        factor = jnp.concatenate([factor, jnp.zeros((128 - 24, NODES), F32)], axis=0).T
        out = t_ref[...] * factor[:, sources : sources + 1]
        for s in range(sources):
            out = out + p_ref[s, 0:NODES, :].astype(F32) * factor[:, s : s + 1]
        out = out.astype(BF16)
        for s in range(sources):
            o_ref[s] = out

    vmem = pl.BlockSpec(memory_space=pltpu.VMEM)
    return pl.pallas_call(
        kernel,
        out_shape=jax.ShapeDtypeStruct((sources, NODES, HD), BF16),
        in_specs=[vmem] * 3,
        out_specs=vmem,
        compiler_params=pltpu.CompilerParams(vmem_limit_bytes=8 << 20),
        cost_estimate=pl.CostEstimate(flops=1 << 20, transcendentals=4096, bytes_accessed=1 << 20),
        name="combine",
    )(parts, tree_sums, tree_stats)


def own_rows(attended, w):
    heads, span, columns = w.shape
    x = jnp.concatenate([attended[g] for g in range(heads)], axis=1)
    return jnp.dot(x, w[...].reshape(heads * span, columns), preferred_element_type=F32)


def project_own(side, attended, weight):
    heads, _, span, columns = weight.shape

    def kernel(side_ref, a_ref, w_hbm, y_ref, o_ref, w, sem):
        own = side_ref[0]
        mine = [pltpu.make_async_copy(w_hbm.at[g, own], w.at[g], sem.at[g]) for g in range(heads)]
        others = [pltpu.make_async_copy(w_hbm.at[g, 1 - own], o_ref.at[g], sem.at[heads + g]) for g in range(heads)]
        for copy in mine + others:
            copy.start()
        for copy in mine:
            copy.wait()
        y_ref[...] = own_rows(a_ref, w)
        for copy in others:
            copy.wait()

    vmem = pl.BlockSpec(memory_space=pltpu.VMEM)
    rows = (heads, span, columns)
    y, fetched = pl.pallas_call(
        kernel,
        out_shape=(jax.ShapeDtypeStruct((NODES, columns), F32), jax.ShapeDtypeStruct(rows, BF16)),
        in_specs=[pl.BlockSpec(memory_space=pltpu.SMEM), vmem, pl.BlockSpec(memory_space=pltpu.HBM)],
        out_specs=(vmem, pl.BlockSpec(memory_space=pl.ANY)),
        scratch_shapes=[VM(rows, BF16), pltpu.SemaphoreType.DMA((2 * heads,))],
        compiler_params=pltpu.CompilerParams(vmem_limit_bytes=8 << 20),
        cost_estimate=pl.CostEstimate(flops=2 * NODES * heads * span * columns, transcendentals=0, bytes_accessed=6 << 20),
        name="project_own",
    )(side, attended, weight)
    return y, pltpu.with_memory_space_constraint(fetched, pltpu.VMEM)


def project_other(attended, fetched, so_far):
    columns = fetched.shape[2]

    def kernel(a_ref, w_ref, y_ref, o_ref):
        y = (y_ref[...] + own_rows(a_ref, w_ref)).astype(BF16)
        for i in range(columns // 128):
            o_ref[i] = y[:, i * 128 : (i + 1) * 128]

    vmem = pl.BlockSpec(memory_space=pltpu.VMEM)
    return pl.pallas_call(
        kernel,
        out_shape=jax.ShapeDtypeStruct((columns // 128, NODES, 128), BF16),
        in_specs=[vmem] * 3,
        out_specs=vmem,
        compiler_params=pltpu.CompilerParams(vmem_limit_bytes=8 << 20),
        cost_estimate=pl.CostEstimate(flops=2 * NODES * fetched.size, transcendentals=0, bytes_accessed=1 << 20),
        name="project_other",
    )(attended, fetched, so_far)


def finish_hidden(shares, residual, position, copies):
    sources = shares.shape[0]

    def kernel(pos_ref, s_ref, r_ref, h_ref, o_ref):
        at = pl.multiple_of(pos_ref[0] * 128, 128)
        total = s_ref[0].astype(F32)
        for s in range(1, sources):
            total = total + s_ref[s].astype(F32)
        h = (r_ref[:, pl.ds(at, 128)].astype(F32) + total).astype(BF16)
        h_ref[...] = h
        for i in range(copies):
            o_ref[i] = h

    vmem = pl.BlockSpec(memory_space=pltpu.VMEM)
    return pl.pallas_call(
        kernel,
        out_shape=(
            jax.ShapeDtypeStruct((NODES, 128), BF16),
            jax.ShapeDtypeStruct((copies, NODES, 128), BF16),
        ),
        in_specs=[pl.BlockSpec(memory_space=pltpu.SMEM), vmem, vmem],
        out_specs=(vmem, vmem),
        compiler_params=pltpu.CompilerParams(vmem_limit_bytes=8 << 20),
        cost_estimate=pl.CostEstimate(flops=1 << 18, transcendentals=0, bytes_accessed=3 << 20),
        name="finish_hidden",
    )(position, shares, residual)


HANDED = 4


def vocab_sum(side, h_any, g_ref, w_hbm, y_ref, sq_ref, h_buf, w_buf, sem, held=None, handed=None):
    groups, _, span, _ = w_hbm.shape
    blocks = span // 128
    ready = 0 if held is None else HANDED

    def arrival(group):
        at = pl.ds(group * blocks, blocks)
        return pltpu.make_async_copy(h_any.at[at], h_buf.at[at], sem.at[2 * group])

    def fetch(group):
        return pltpu.make_async_copy(w_hbm.at[group, side], w_buf.at[group - ready], sem.at[2 * group + 1])

    for group in range(groups):
        arrival(group).start()
        if group >= ready:
            fetch(group).start()
    extra = []
    if handed is not None:
        for group in range(HANDED):
            extra.append(pltpu.make_async_copy(w_hbm.at[group, 1 - side], handed.at[group], sem.at[2 * groups + group]))
            extra[-1].start()

    def add(group, rows):
        pieces = []
        squares = sq_ref[...]
        for i in range(blocks):
            h = h_buf[group * blocks + i].astype(F32)
            squares = squares + h * h
            pieces.append((h * g_ref[group, side, i : i + 1, :].astype(F32)).astype(BF16))
        sq_ref[...] = squares
        x = jnp.concatenate(pieces, axis=1)
        y_ref[...] += jnp.dot(x, rows, preferred_element_type=F32)

    if ready:

        @pl.loop(0, ready)
        def _(group):
            arrival(group).wait()
            add(group, held[group])

    @pl.loop(ready, groups)
    def _(group):
        arrival(group).wait()
        fetch(group).wait()
        add(group, w_buf[group - ready])

    for copy in extra:
        copy.wait()


def vocab_scratch(hidden, weight, ready):
    groups, _, span, columns = weight.shape
    return [
        VM(hidden.shape, BF16),
        VM((groups - ready, span, columns), BF16),
        pltpu.SemaphoreType.DMA((2 * groups + HANDED,)),
    ]


def vocab_first(side, hidden, gain, weight):
    groups, _, span, columns = weight.shape

    def kernel(side_ref, h_any, g_ref, w_hbm, y_ref, sq_ref, handed, *scratch):
        y_ref[...] = jnp.zeros_like(y_ref)
        sq_ref[...] = jnp.zeros_like(sq_ref)
        vocab_sum(side_ref[0], h_any, g_ref, w_hbm, y_ref, sq_ref, *scratch, handed=handed)

    vmem = pl.BlockSpec(memory_space=pltpu.VMEM)
    anywhere = pl.BlockSpec(memory_space=pl.ANY)
    y, squares, handed = pl.pallas_call(
        kernel,
        out_shape=(
            jax.ShapeDtypeStruct((NODES, columns), F32),
            jax.ShapeDtypeStruct((NODES, 128), F32),
            jax.ShapeDtypeStruct((HANDED, span, columns), BF16),
        ),
        in_specs=[pl.BlockSpec(memory_space=pltpu.SMEM), anywhere, vmem, pl.BlockSpec(memory_space=pltpu.HBM)],
        out_specs=(vmem, vmem, anywhere),
        scratch_shapes=vocab_scratch(hidden, weight, 0),
        compiler_params=pltpu.CompilerParams(vmem_limit_bytes=24 << 20),
        cost_estimate=pl.CostEstimate(
            flops=2 * NODES * groups * span * columns, transcendentals=0, bytes_accessed=10 << 20
        ),
        name="vocab_first",
    )(side, hidden, gain, weight)
    return y, squares, pltpu.with_memory_space_constraint(handed, pltpu.VMEM)


def vocab_second(side, hidden, gain, weight, y_first, sq_first, held, target, copies):
    groups, _, span, columns = weight.shape

    def kernel(side_ref, h_any, g_ref, w_hbm, y0_ref, sq0_ref, held_ref, t_ref, o_ref, acc, sq, *scratch):
        acc[...] = y0_ref[...]
        sq[...] = sq0_ref[...]
        vocab_sum(side_ref[0], h_any, g_ref, w_hbm, acc, sq, *scratch, held=held_ref)
        mean = jnp.sum(sq[...], axis=1, keepdims=True) / D
        logits = acc[...] * lax.rsqrt(mean + EPSILON)
        peak = jnp.max(logits, axis=1, keepdims=True)
        total = jnp.sum(jnp.exp(logits - peak), axis=1, keepdims=True)
        lse = peak + jnp.log(total)
        column = lax.broadcasted_iota(jnp.int32, (NODES, columns), 1)
        chosen = jnp.sum(jnp.where(column == t_ref[...], logits, 0.0), axis=1, keepdims=True)
        lane = lax.broadcasted_iota(jnp.int32, (NODES, 128), 1)
        rows = jnp.where(lane == 0, lse, jnp.where(lane == 1, chosen, 0.0)).T
        row = jnp.concatenate([rows[0:1, :], rows[1:2, :]], axis=1)
        for i in range(copies):
            o_ref[i] = row

    vmem = pl.BlockSpec(memory_space=pltpu.VMEM)
    anywhere = pl.BlockSpec(memory_space=pl.ANY)
    return pl.pallas_call(
        kernel,
        out_shape=jax.ShapeDtypeStruct((copies, 1, 2 * NODES), F32),
        in_specs=[pl.BlockSpec(memory_space=pltpu.SMEM), anywhere, vmem, pl.BlockSpec(memory_space=pltpu.HBM)] + [vmem] * 4,
        out_specs=vmem,
        scratch_shapes=[VM((NODES, columns), F32), VM((NODES, 128), F32)] + vocab_scratch(hidden, weight, HANDED),
        compiler_params=pltpu.CompilerParams(vmem_limit_bytes=24 << 20),
        cost_estimate=pl.CostEstimate(
            flops=2 * NODES * groups * span * columns, transcendentals=1 << 16, bytes_accessed=10 << 20
        ),
        name="vocab_second",
    )(side, hidden, gain, weight, y_first, sq_first, held, target)


def final_score(stats, amateur):
    def kernel(s_ref, a_ref, o_ref):
        lse = s_ref[:, 0, 0:NODES]
        chosen = s_ref[:, 0, NODES : 2 * NODES]
        best = jnp.max(lse, axis=0, keepdims=True)
        total = jnp.sum(jnp.exp(lse - best), axis=0, keepdims=True)
        picked = jnp.sum(chosen, axis=0, keepdims=True)
        o_ref[...] = picked - (best + jnp.log(total)) - a_ref[...]

    vmem = pl.BlockSpec(memory_space=pltpu.VMEM)
    return pl.pallas_call(
        kernel,
        out_shape=jax.ShapeDtypeStruct((1, NODES), F32),
        in_specs=[vmem, vmem],
        out_specs=vmem,
        compiler_params=pltpu.CompilerParams(vmem_limit_bytes=8 << 20),
        name="final_score",
    )(stats, amateur)


def body(
    queries,
    cache_keys,
    cache_values,
    tree_keys,
    tree_values,
    ancestors,
    filled_extents,
    out_weight,
    residual,
    norm_gain,
    vocab_weight,
    candidates,
    amateur,
):
    positions = cache_keys.shape[1]
    seq_index = lax.axis_index(SEQ)
    head_index = lax.axis_index(HEAD)
    core = lax.axis_index("c")
    seq_size = lax.axis_size(SEQ)
    cores = lax.axis_size("c")
    chips = lax.axis_size(CHIPS)
    devices = chips * cores

    def scalar(x):
        return x.astype(jnp.int32).reshape(1)

    def swap(x):
        return lax.ppermute(x, "c", [(0, 1), (1, 0)])

    def in_hbm(x):
        return pltpu.with_memory_space_constraint(x, pltpu.HBM)

    own, other = scalar(core), scalar(1 - core)
    place = jnp.stack([seq_index * positions, core]).astype(jnp.int32)
    keep, send = attention(in_hbm(queries), in_hbm(cache_keys), in_hbm(cache_values), in_hbm(filled_extents), place)
    parts = merge(keep, swap(send))
    parts = lax.all_to_all(parts, ROWS, 0, 0, tiled=True)
    tree_sums, tree_stats = tree_part(queries, tree_keys, tree_values, ancestors, scalar(seq_index))
    attended = combine(parts, tree_sums, tree_stats)
    rows, columns = out_weight.shape
    weight = in_hbm(out_weight.reshape(rows // HD // cores, cores, HD, columns))
    attended = lax.all_to_all(attended, ROWS, 0, 0, tiled=True)
    swapped = swap(attended)
    projected, fetched = project_own(own, attended, weight)
    shares = project_other(swapped, fetched, projected)
    shares = lax.all_to_all(shares, HEAD, 0, 0, tiled=True)
    hidden, repeated = finish_hidden(shares, residual, scalar(head_index), chips)
    own_side = lax.all_to_all(repeated, CHIPS, 0, 0, tiled=True)
    vocab_local = vocab_weight.shape[1]
    groups = seq_size // cores
    span = D // seq_size
    weight = in_hbm(vocab_weight.reshape(groups, cores, span, vocab_local))
    other_side = swap(own_side)
    gain = norm_gain.reshape(groups, cores, span // 128, 128)
    y, squares, handed = vocab_first(own, own_side, gain, weight)
    target = (candidates - lax.axis_index(ALL) * vocab_local).reshape(NODES, 1)
    stats = vocab_second(other, other_side, gain, weight, y, squares, handed, target, devices)
    stats = lax.all_to_all(stats, ALL, 0, 0, tiled=True)
    contrast = final_score(stats, amateur.reshape(1, NODES))
    return (hidden, contrast.reshape(NODES))


def solution(mesh):
    fine = Mesh(mesh.devices.reshape(2, 4, 2, 4, 2), ALL)
    in_specs = (
        P(None, HEAD),
        P(None, SEQ, HEAD),
        P(None, SEQ, HEAD),
        P(None, HEAD),
        P(None, HEAD),
        P(),
        P(),
        P(HEAD, SEQ),
        P(None, SEQ),
        P(),
        P(None, ALL),
        P(),
        P(),
    )
    out_specs = (P(None, ALL), P())
    return jax.shard_map(body, mesh=fine, in_specs=in_specs, out_specs=out_specs, check_vma=False)
```

```python
import math

import jax
import jax.numpy as jnp
from jax import lax
from jax.experimental import pallas as pl
from jax.experimental.pallas import tpu as pltpu
from jax.sharding import Mesh, PartitionSpec as P

NODES_REQ = 64
NODES = 128
D = 16384
HD = 128
EPSILON = 1e-05
NEG_FILL = -1e30
LOG2E = math.log2(math.e)
SCALE2 = HD ** (-0.5) * LOG2E

SEQ = ("zh", "y", "c")
HEAD = ("x", "zl")
ROWS = ("zh", "y")
CHIPS = ("zh", "y", "x", "zl")
ALL = SEQ + HEAD


F32 = jnp.float32
BF16 = jnp.bfloat16
VM = pltpu.VMEM
STAT_ROWS = 16
BLOCK_ROWS = 512
CHUNK = 2048


def nt_dot(a, b):
    return lax.dot_general(a, b, (((1,), (1,)), ((), ())), preferred_element_type=F32)


def thirds(x):
    hi = x.astype(BF16).astype(F32)
    rest = x - hi
    mid = rest.astype(BF16).astype(F32)
    return hi, mid, rest - mid


def attention(queries, keys, values, extents, place):
    requests, positions, _ = keys.shape
    heads = queries.shape[1] // HD
    per_block = BLOCK_ROWS // NODES_REQ
    blocks_req = heads // per_block
    blocks = requests * blocks_req
    chunks = positions // CHUNK

    half = heads // 2

    def kernel(ext_ref, place_ref, q_hbm, k_hbm, v_hbm, keep, send, q_ref, qs, kv, vv, bias, s_buf, m_buf, acc, stat, sem):
        q_copy = pltpu.make_async_copy(q_hbm, q_ref, sem.at[2 * requests])
        q_copy.start()
        core = place_ref[1]
        copies = []
        for b in range(requests):
            copies.append(
                (
                    pltpu.make_async_copy(k_hbm.at[b], kv.at[b], sem.at[2 * b]),
                    pltpu.make_async_copy(v_hbm.at[b], vv.at[b, :, pl.ds(0, HD)], sem.at[2 * b + 1]),
                )
            )
        for pair in copies:
            for copy in pair:
                copy.start()
        lane = lax.broadcasted_iota(jnp.int32, (8, positions), 1)
        for b in range(requests):
            left = ext_ref[b] - place_ref[0]
            bias[b] = jnp.where(lane < left, 0.0, NEG_FILL).astype(F32)
        for b in range(requests):
            vv[b, :, HD : 2 * HD] = jnp.ones((positions, HD), BF16)
        stat[...] = jnp.zeros_like(stat)
        q_copy.wait()
        for g in range(heads):
            head = 2 * g + core if g < half else 2 * (g - half) + 1 - core
            at = pl.multiple_of(head * HD, HD)
            for b in range(requests):
                qs[b * blocks_req + g // per_block, (g % per_block) * NODES_REQ : (g % per_block + 1) * NODES_REQ, :] = (
                    q_ref[b * NODES_REQ : (b + 1) * NODES_REQ, pl.ds(at, HD)]
                )

        def scores(block, chunk, slot):
            b = block // blocks_req
            at = pl.multiple_of(chunk * CHUNK, CHUNK)
            s = nt_dot(qs[block], kv[b, pl.ds(at, CHUNK), :])
            best = m_buf[slot]
            for t in range(CHUNK // 128):
                piece = s[:, t * 128 : (t + 1) * 128]
                shift = bias[b, :, pl.ds(pl.multiple_of(at + t * 128, 128), 128)]
                piece = (piece.reshape(BLOCK_ROWS // 8, 8, 128) + shift[None]).reshape(BLOCK_ROWS, 128)
                s_buf[slot, chunk, :, t * 128 : (t + 1) * 128] = piece
                best = jnp.maximum(best, piece)
            m_buf[slot] = best

        def weigh(block, chunk, slot, top):
            b = block // blocks_req
            at = pl.multiple_of(chunk * CHUNK, CHUNK)
            pieces = []
            for t in range(CHUNK // 128):
                w = jnp.exp2(s_buf[slot, chunk, :, t * 128 : (t + 1) * 128] * SCALE2 - top)
                pieces.append(w.astype(BF16))
            acc[...] += jnp.dot(
                jnp.concatenate(pieces, axis=1), vv[b, pl.ds(at, CHUNK), :], preferred_element_type=F32
            )

        copies[0][0].wait()
        m_buf[0] = jnp.full((BLOCK_ROWS, 128), NEG_FILL, F32)

        @pl.loop(0, chunks)
        def _(chunk):
            scores(0, chunk, 0)

        def finish(block, best):
            total = acc[:, HD : HD + 1]
            b = block // blocks_req
            j = block % blocks_req
            slots = lax.broadcasted_iota(jnp.int32, (NODES_REQ, 128), 1)
            rows = slice(b * NODES_REQ, (b + 1) * NODES_REQ)
            held = stat[rows, :]
            for i in range(per_block):
                g = j * per_block + i
                part = slice(i * NODES_REQ, (i + 1) * NODES_REQ)
                out = keep if g < half else send
                out[g % half, rows, :] = acc[part, 0:HD].astype(BF16)
                for n, column in enumerate(thirds(best[part]) + thirds(total[part])):
                    held = jnp.where(slots == g * 8 + n, column, held)
            stat[rows, :] = held

        for block in range(blocks):
            last = block == blocks - 1
            slot = block % 2
            if block % blocks_req == 0:
                copies[block // blocks_req][1].wait()
            if not last and (block + 1) % blocks_req == 0:
                copies[(block + 1) // blocks_req][0].wait()
            best = jnp.max(m_buf[slot], axis=1, keepdims=True)
            best = jnp.maximum(best, 0.5 * NEG_FILL) * SCALE2
            top = jnp.broadcast_to(best, (BLOCK_ROWS, 128))
            acc[...] = jnp.zeros_like(acc)
            if not last:
                m_buf[1 - slot] = jnp.full((BLOCK_ROWS, 128), NEG_FILL, F32)

            @pl.loop(0, chunks)
            def _(chunk):
                if not last:
                    scores(block + 1, chunk, 1 - slot)
                weigh(block, chunk, slot, top)

            finish(block, best)

        turned = stat[...].T
        for g in range(heads):
            out = keep if g < half else send
            out[g % half, NODES : NODES + STAT_ROWS, :] = jnp.concatenate(
                [turned[g * 8 : (g + 1) * 8, :], jnp.zeros((STAT_ROWS - 8, NODES), F32)], axis=0
            ).astype(BF16)

    smem = pl.BlockSpec(memory_space=pltpu.SMEM)
    vmem = pl.BlockSpec(memory_space=pltpu.VMEM)
    hbm = pl.BlockSpec(memory_space=pltpu.HBM)
    out = jax.ShapeDtypeStruct((half, NODES + STAT_ROWS, HD), BF16)
    return pl.pallas_call(
        kernel,
        out_shape=(out, out),
        in_specs=[smem, smem, hbm, hbm, hbm],
        out_specs=(vmem, vmem),
        scratch_shapes=[
            VM((NODES, heads * HD), BF16),
            VM((blocks, BLOCK_ROWS, HD), BF16),
            VM((requests, positions, HD), BF16),
            VM((requests, positions, 2 * HD), BF16),
            VM((requests, 8, positions), F32),
            VM((2, chunks, BLOCK_ROWS, CHUNK), F32),
            VM((2, BLOCK_ROWS, 128), F32),
            VM((BLOCK_ROWS, 2 * HD), F32),
            VM((NODES, 128), F32),
            pltpu.SemaphoreType.DMA((2 * requests + 1,)),
        ],
        compiler_params=pltpu.CompilerParams(vmem_limit_bytes=48 << 20),
        cost_estimate=pl.CostEstimate(
            flops=4 * NODES * heads * positions * HD, transcendentals=NODES * heads * positions, bytes_accessed=5 << 20
        ),
        name="attention",
    )(extents, place, queries, keys, values)


def tree_part(queries, tree_keys, tree_values, ancestors, head):
    requests = ancestors.shape[0]

    def kernel(head_ref, q_ref, k_ref, v_ref, a_ref, o_ref, st_ref):
        at = pl.multiple_of(head_ref[0] * HD, HD)
        slots = lax.broadcasted_iota(jnp.int32, (NODES_REQ, 128), 1)
        for b in range(requests):
            rows = slice(b * NODES_REQ, (b + 1) * NODES_REQ)
            s = nt_dot(q_ref[rows, pl.ds(at, HD)], k_ref[rows, :])
            live = a_ref[b] > 0
            s = jnp.where(live, s * SCALE2, NEG_FILL)
            top = jnp.max(s, axis=1, keepdims=True)
            w = jnp.where(live, jnp.exp2(s - top), 0.0)
            total = jnp.sum(w, axis=1, keepdims=True)
            o_ref[rows, :] = jnp.dot(w.astype(BF16), v_ref[rows, :], preferred_element_type=F32)
            st_ref[rows, :] = jnp.where(slots == 0, top, jnp.where(slots == 1, total, 0.0))
        st_ref[...] = st_ref[...].T

    vmem = pl.BlockSpec(memory_space=pltpu.VMEM)
    return pl.pallas_call(
        kernel,
        out_shape=(jax.ShapeDtypeStruct((NODES, HD), F32), jax.ShapeDtypeStruct((128, NODES), F32)),
        in_specs=[pl.BlockSpec(memory_space=pltpu.SMEM)] + [vmem] * 4,
        out_specs=(vmem, vmem),
        compiler_params=pltpu.CompilerParams(vmem_limit_bytes=8 << 20),
        cost_estimate=pl.CostEstimate(flops=1 << 22, transcendentals=8192, bytes_accessed=1 << 20),
        name="tree_part",
    )(head, queries, tree_keys, tree_values, ancestors)


def merge(first, second):
    heads = first.shape[0]

    def kernel(a_ref, b_ref, o_ref):
        rows = []
        columns = []
        for g in range(heads):
            a = a_ref[g, NODES : NODES + STAT_ROWS, :].astype(F32)
            b = b_ref[g, NODES : NODES + STAT_ROWS, :].astype(F32)
            top_a = a[0:1] + a[1:2] + a[2:3]
            top_b = b[0:1] + b[1:2] + b[2:3]
            top = jnp.maximum(top_a, top_b)
            fa = jnp.exp2(top_a - top)
            fb = jnp.exp2(top_b - top)
            total = fa * (a[3:4] + a[4:5] + a[5:6]) + fb * (b[3:4] + b[4:5] + b[5:6])
            rows.append(jnp.concatenate(thirds(top) + thirds(total) + (jnp.zeros((STAT_ROWS - 6, NODES), F32),), axis=0))
            columns += [fa, fb]
        columns.append(jnp.zeros((128 - 2 * heads, NODES), F32))
        factor = jnp.concatenate(columns, axis=0).T
        for g in range(heads):
            o_ref[g, 0:NODES, :] = (
                a_ref[g, 0:NODES, :].astype(F32) * factor[:, 2 * g : 2 * g + 1]
                + b_ref[g, 0:NODES, :].astype(F32) * factor[:, 2 * g + 1 : 2 * g + 2]
            ).astype(BF16)
            o_ref[g, NODES : NODES + STAT_ROWS, :] = rows[g].astype(BF16)

    vmem = pl.BlockSpec(memory_space=pltpu.VMEM)
    return pl.pallas_call(
        kernel,
        out_shape=jax.ShapeDtypeStruct(first.shape, BF16),
        in_specs=[vmem] * 2,
        out_specs=vmem,
        compiler_params=pltpu.CompilerParams(vmem_limit_bytes=8 << 20),
        cost_estimate=pl.CostEstimate(flops=1 << 20, transcendentals=4096, bytes_accessed=1 << 20),
        name="merge",
    )(first, second)


def combine(parts, tree_sums, tree_stats):
    sources = parts.shape[0]

    def kernel(p_ref, t_ref, ts_ref, o_ref):
        tops = []
        totals = []
        for s in range(sources):
            st = p_ref[s, NODES : NODES + STAT_ROWS, :].astype(F32)
            tops.append(st[0:1] + st[1:2] + st[2:3])
            totals.append(st[3:4] + st[4:5] + st[5:6])
        tops.append(ts_ref[0:1, :])
        totals.append(ts_ref[1:2, :])
        tops = jnp.concatenate(tops + [jnp.full((24 - sources - 1, NODES), NEG_FILL, F32)], axis=0)
        totals = jnp.concatenate(totals + [jnp.zeros((24 - sources - 1, NODES), F32)], axis=0)
        best = jnp.max(tops, axis=0, keepdims=True)
        factor = jnp.exp2(tops - best)
        factor = factor / jnp.sum(factor * totals, axis=0, keepdims=True)
        factor = jnp.concatenate([factor, jnp.zeros((128 - 24, NODES), F32)], axis=0).T
        out = t_ref[...] * factor[:, sources : sources + 1]
        for s in range(sources):
            out = out + p_ref[s, 0:NODES, :].astype(F32) * factor[:, s : s + 1]
        out = out.astype(BF16)
        for s in range(sources):
            o_ref[s] = out

    vmem = pl.BlockSpec(memory_space=pltpu.VMEM)
    return pl.pallas_call(
        kernel,
        out_shape=jax.ShapeDtypeStruct((sources, NODES, HD), BF16),
        in_specs=[vmem] * 3,
        out_specs=vmem,
        compiler_params=pltpu.CompilerParams(vmem_limit_bytes=8 << 20),
        cost_estimate=pl.CostEstimate(flops=1 << 20, transcendentals=4096, bytes_accessed=1 << 20),
        name="combine",
    )(parts, tree_sums, tree_stats)


def own_rows(attended, w):
    heads, span, columns = w.shape
    x = jnp.concatenate([attended[g] for g in range(heads)], axis=1)
    return jnp.dot(x, w[...].reshape(heads * span, columns), preferred_element_type=F32)


def project_own(side, attended, weight):
    heads, _, span, columns = weight.shape

    def kernel(side_ref, a_ref, w_hbm, y_ref, o_ref, w, sem):
        own = side_ref[0]
        mine = [pltpu.make_async_copy(w_hbm.at[g, own], w.at[g], sem.at[g]) for g in range(heads)]
        others = [pltpu.make_async_copy(w_hbm.at[g, 1 - own], o_ref.at[g], sem.at[heads + g]) for g in range(heads)]
        for copy in mine + others:
            copy.start()
        for copy in mine:
            copy.wait()
        y_ref[...] = own_rows(a_ref, w)
        for copy in others:
            copy.wait()

    vmem = pl.BlockSpec(memory_space=pltpu.VMEM)
    rows = (heads, span, columns)
    y, fetched = pl.pallas_call(
        kernel,
        out_shape=(jax.ShapeDtypeStruct((NODES, columns), F32), jax.ShapeDtypeStruct(rows, BF16)),
        in_specs=[pl.BlockSpec(memory_space=pltpu.SMEM), vmem, pl.BlockSpec(memory_space=pltpu.HBM)],
        out_specs=(vmem, pl.BlockSpec(memory_space=pl.ANY)),
        scratch_shapes=[VM(rows, BF16), pltpu.SemaphoreType.DMA((2 * heads,))],
        compiler_params=pltpu.CompilerParams(vmem_limit_bytes=8 << 20),
        cost_estimate=pl.CostEstimate(flops=2 * NODES * heads * span * columns, transcendentals=0, bytes_accessed=6 << 20),
        name="project_own",
    )(side, attended, weight)
    return y, pltpu.with_memory_space_constraint(fetched, pltpu.VMEM)


def project_other(attended, fetched, so_far):
    columns = fetched.shape[2]

    def kernel(a_ref, w_ref, y_ref, o_ref):
        y = (y_ref[...] + own_rows(a_ref, w_ref)).astype(BF16)
        for i in range(columns // 128):
            o_ref[i] = y[:, i * 128 : (i + 1) * 128]

    vmem = pl.BlockSpec(memory_space=pltpu.VMEM)
    return pl.pallas_call(
        kernel,
        out_shape=jax.ShapeDtypeStruct((columns // 128, NODES, 128), BF16),
        in_specs=[vmem] * 3,
        out_specs=vmem,
        compiler_params=pltpu.CompilerParams(vmem_limit_bytes=8 << 20),
        cost_estimate=pl.CostEstimate(flops=2 * NODES * fetched.size, transcendentals=0, bytes_accessed=1 << 20),
        name="project_other",
    )(attended, fetched, so_far)


def finish_hidden(shares, residual, position, copies):
    sources = shares.shape[0]

    def kernel(pos_ref, s_ref, r_ref, h_ref, o_ref):
        at = pl.multiple_of(pos_ref[0] * 128, 128)
        total = s_ref[0].astype(F32)
        for s in range(1, sources):
            total = total + s_ref[s].astype(F32)
        h = (r_ref[:, pl.ds(at, 128)].astype(F32) + total).astype(BF16)
        h_ref[...] = h
        for i in range(copies):
            o_ref[i] = h

    vmem = pl.BlockSpec(memory_space=pltpu.VMEM)
    return pl.pallas_call(
        kernel,
        out_shape=(
            jax.ShapeDtypeStruct((NODES, 128), BF16),
            jax.ShapeDtypeStruct((copies, NODES, 128), BF16),
        ),
        in_specs=[pl.BlockSpec(memory_space=pltpu.SMEM), vmem, vmem],
        out_specs=(vmem, vmem),
        compiler_params=pltpu.CompilerParams(vmem_limit_bytes=8 << 20),
        cost_estimate=pl.CostEstimate(flops=1 << 18, transcendentals=0, bytes_accessed=3 << 20),
        name="finish_hidden",
    )(position, shares, residual)


HANDED = 4


def vocab_sum(side, h_any, g_ref, w_hbm, y_ref, sq_ref, h_buf, w_buf, sem, held=None, handed=None):
    groups, _, span, _ = w_hbm.shape
    blocks = span // 128
    ready = 0 if held is None else HANDED

    def arrival(group):
        at = pl.ds(group * blocks, blocks)
        return pltpu.make_async_copy(h_any.at[at], h_buf.at[at], sem.at[2 * group])

    def fetch(group):
        return pltpu.make_async_copy(w_hbm.at[group, side], w_buf.at[group - ready], sem.at[2 * group + 1])

    for group in range(groups):
        arrival(group).start()
        if group >= ready:
            fetch(group).start()
    extra = []
    if handed is not None:
        for group in range(HANDED):
            extra.append(pltpu.make_async_copy(w_hbm.at[group, 1 - side], handed.at[group], sem.at[2 * groups + group]))
            extra[-1].start()

    def add(group, rows):
        pieces = []
        squares = sq_ref[...]
        for i in range(blocks):
            h = h_buf[group * blocks + i].astype(F32)
            squares = squares + h * h
            pieces.append((h * g_ref[group, side, i : i + 1, :].astype(F32)).astype(BF16))
        sq_ref[...] = squares
        x = jnp.concatenate(pieces, axis=1)
        y_ref[...] += jnp.dot(x, rows, preferred_element_type=F32)

    if ready:

        @pl.loop(0, ready)
        def _(group):
            arrival(group).wait()
            add(group, held[group])

    @pl.loop(ready, groups)
    def _(group):
        arrival(group).wait()
        fetch(group).wait()
        add(group, w_buf[group - ready])

    for copy in extra:
        copy.wait()


def vocab_scratch(hidden, weight, ready):
    groups, _, span, columns = weight.shape
    return [
        VM(hidden.shape, BF16),
        VM((groups - ready, span, columns), BF16),
        pltpu.SemaphoreType.DMA((2 * groups + HANDED,)),
    ]


def vocab_first(side, hidden, gain, weight):
    groups, _, span, columns = weight.shape

    def kernel(side_ref, h_any, g_ref, w_hbm, y_ref, sq_ref, handed, *scratch):
        y_ref[...] = jnp.zeros_like(y_ref)
        sq_ref[...] = jnp.zeros_like(sq_ref)
        vocab_sum(side_ref[0], h_any, g_ref, w_hbm, y_ref, sq_ref, *scratch, handed=handed)

    vmem = pl.BlockSpec(memory_space=pltpu.VMEM)
    anywhere = pl.BlockSpec(memory_space=pl.ANY)
    y, squares, handed = pl.pallas_call(
        kernel,
        out_shape=(
            jax.ShapeDtypeStruct((NODES, columns), F32),
            jax.ShapeDtypeStruct((NODES, 128), F32),
            jax.ShapeDtypeStruct((HANDED, span, columns), BF16),
        ),
        in_specs=[pl.BlockSpec(memory_space=pltpu.SMEM), anywhere, vmem, pl.BlockSpec(memory_space=pltpu.HBM)],
        out_specs=(vmem, vmem, anywhere),
        scratch_shapes=vocab_scratch(hidden, weight, 0),
        compiler_params=pltpu.CompilerParams(vmem_limit_bytes=24 << 20),
        cost_estimate=pl.CostEstimate(
            flops=2 * NODES * groups * span * columns, transcendentals=0, bytes_accessed=10 << 20
        ),
        name="vocab_first",
    )(side, hidden, gain, weight)
    return y, squares, pltpu.with_memory_space_constraint(handed, pltpu.VMEM)


def vocab_second(side, hidden, gain, weight, y_first, sq_first, held, target, copies):
    groups, _, span, columns = weight.shape

    def kernel(side_ref, h_any, g_ref, w_hbm, y0_ref, sq0_ref, held_ref, t_ref, o_ref, acc, sq, *scratch):
        acc[...] = y0_ref[...]
        sq[...] = sq0_ref[...]
        vocab_sum(side_ref[0], h_any, g_ref, w_hbm, acc, sq, *scratch, held=held_ref)
        mean = jnp.sum(sq[...], axis=1, keepdims=True) / D
        logits = acc[...] * lax.rsqrt(mean + EPSILON)
        peak = jnp.max(logits, axis=1, keepdims=True)
        total = jnp.sum(jnp.exp(logits - peak), axis=1, keepdims=True)
        lse = peak + jnp.log(total)
        column = lax.broadcasted_iota(jnp.int32, (NODES, columns), 1)
        chosen = jnp.sum(jnp.where(column == t_ref[...], logits, 0.0), axis=1, keepdims=True)
        lane = lax.broadcasted_iota(jnp.int32, (NODES, 128), 1)
        rows = jnp.where(lane == 0, lse, jnp.where(lane == 1, chosen, 0.0)).T
        row = jnp.concatenate([rows[0:1, :], rows[1:2, :]], axis=1)
        for i in range(copies):
            o_ref[i] = row

    vmem = pl.BlockSpec(memory_space=pltpu.VMEM)
    anywhere = pl.BlockSpec(memory_space=pl.ANY)
    return pl.pallas_call(
        kernel,
        out_shape=jax.ShapeDtypeStruct((copies, 1, 2 * NODES), F32),
        in_specs=[pl.BlockSpec(memory_space=pltpu.SMEM), anywhere, vmem, pl.BlockSpec(memory_space=pltpu.HBM)] + [vmem] * 4,
        out_specs=vmem,
        scratch_shapes=[VM((NODES, columns), F32), VM((NODES, 128), F32)] + vocab_scratch(hidden, weight, HANDED),
        compiler_params=pltpu.CompilerParams(vmem_limit_bytes=24 << 20),
        cost_estimate=pl.CostEstimate(
            flops=2 * NODES * groups * span * columns, transcendentals=1 << 16, bytes_accessed=10 << 20
        ),
        name="vocab_second",
    )(side, hidden, gain, weight, y_first, sq_first, held, target)


def final_score(stats, amateur):
    def kernel(s_ref, a_ref, o_ref):
        lse = s_ref[:, 0, 0:NODES]
        chosen = s_ref[:, 0, NODES : 2 * NODES]
        best = jnp.max(lse, axis=0, keepdims=True)
        total = jnp.sum(jnp.exp(lse - best), axis=0, keepdims=True)
        picked = jnp.sum(chosen, axis=0, keepdims=True)
        o_ref[...] = picked - (best + jnp.log(total)) - a_ref[...]

    vmem = pl.BlockSpec(memory_space=pltpu.VMEM)
    return pl.pallas_call(
        kernel,
        out_shape=jax.ShapeDtypeStruct((1, NODES), F32),
        in_specs=[vmem, vmem],
        out_specs=vmem,
        compiler_params=pltpu.CompilerParams(vmem_limit_bytes=8 << 20),
        name="final_score",
    )(stats, amateur)


def body(
    queries,
    cache_keys,
    cache_values,
    tree_keys,
    tree_values,
    ancestors,
    filled_extents,
    out_weight,
    residual,
    norm_gain,
    vocab_weight,
    candidates,
    amateur,
):
    positions = cache_keys.shape[1]
    seq_index = lax.axis_index(SEQ)
    head_index = lax.axis_index(HEAD)
    core = lax.axis_index("c")
    seq_size = lax.axis_size(SEQ)
    cores = lax.axis_size("c")
    chips = lax.axis_size(CHIPS)
    devices = chips * cores

    def scalar(x):
        return x.astype(jnp.int32).reshape(1)

    def swap(x):
        return lax.ppermute(x, "c", [(0, 1), (1, 0)])

    def in_hbm(x):
        return pltpu.with_memory_space_constraint(x, pltpu.HBM)

    own, other = scalar(core), scalar(1 - core)
    place = jnp.stack([seq_index * positions, core]).astype(jnp.int32)
    keep, send = attention(in_hbm(queries), in_hbm(cache_keys), in_hbm(cache_values), in_hbm(filled_extents), place)
    parts = merge(keep, swap(send))
    parts = lax.all_to_all(parts, ROWS, 0, 0, tiled=True)
    tree_sums, tree_stats = tree_part(queries, tree_keys, tree_values, ancestors, scalar(seq_index))
    attended = combine(parts, tree_sums, tree_stats)
    rows, columns = out_weight.shape
    weight = in_hbm(out_weight.reshape(rows // HD // cores, cores, HD, columns))
    attended = lax.all_to_all(attended, ROWS, 0, 0, tiled=True)
    swapped = swap(attended)
    projected, fetched = project_own(own, attended, weight)
    shares = project_other(swapped, fetched, projected)
    shares = lax.all_to_all(shares, HEAD, 0, 0, tiled=True)
    hidden, repeated = finish_hidden(shares, residual, scalar(head_index), chips)
    own_side = lax.all_to_all(repeated, CHIPS, 0, 0, tiled=True)
    vocab_local = vocab_weight.shape[1]
    groups = seq_size // cores
    span = D // seq_size
    weight = in_hbm(vocab_weight.reshape(groups, cores, span, vocab_local))
    other_side = swap(own_side)
    gain = norm_gain.reshape(groups, cores, span // 128, 128)
    y, squares, handed = vocab_first(own, own_side, gain, weight)
    target = (candidates - lax.axis_index(ALL) * vocab_local).reshape(NODES, 1)
    stats = vocab_second(other, other_side, gain, weight, y, squares, handed, target, devices)
    stats = lax.all_to_all(stats, ALL, 0, 0, tiled=True)
    contrast = final_score(stats, amateur.reshape(1, NODES))
    return (hidden, contrast.reshape(NODES))


def solution(mesh):
    fine = Mesh(mesh.devices.reshape(2, 4, 2, 4, 2), ALL)
    in_specs = (
        P(None, HEAD),
        P(None, SEQ, HEAD),
        P(None, SEQ, HEAD),
        P(None, HEAD),
        P(None, HEAD),
        P(),
        P(),
        P(HEAD, SEQ),
        P(None, SEQ),
        P(),
        P(None, ALL),
        P(),
        P(),
    )
    out_specs = (P(None, ALL), P())
    return jax.shard_map(body, mesh=fine, in_specs=in_specs, out_specs=out_specs, check_vma=False)
```

```python
import math

import jax
import jax.numpy as jnp
from jax import lax
from jax.experimental import pallas as pl
from jax.experimental.pallas import tpu as pltpu
from jax.sharding import Mesh, PartitionSpec as P

NODES_REQ = 64
NODES = 128
D = 16384
HD = 128
EPSILON = 1e-05
NEG_FILL = -1e30
LOG2E = math.log2(math.e)
SCALE2 = HD ** (-0.5) * LOG2E

SEQ = ("zh", "y", "c")
HEAD = ("x", "zl")
ROWS = ("zh", "y")
CHIPS = ("zh", "y", "x", "zl")
ALL = SEQ + HEAD


F32 = jnp.float32
BF16 = jnp.bfloat16
VM = pltpu.VMEM
STAT_ROWS = 16
BLOCK_ROWS = 512
CHUNK = 2048


def nt_dot(a, b):
    return lax.dot_general(a, b, (((1,), (1,)), ((), ())), preferred_element_type=F32)


def thirds(x):
    hi = x.astype(BF16).astype(F32)
    rest = x - hi
    mid = rest.astype(BF16).astype(F32)
    return hi, mid, rest - mid


def attention(queries, keys, values, extents, place):
    requests, positions, _ = keys.shape
    heads = queries.shape[1] // HD
    per_block = BLOCK_ROWS // NODES_REQ
    blocks_req = heads // per_block
    blocks = requests * blocks_req
    chunks = positions // CHUNK

    half = heads // 2

    def kernel(ext_ref, place_ref, q_hbm, k_hbm, v_hbm, keep, send, q_ref, qs, kv, vv, bias, s_buf, m_buf, acc, stat, sem):
        q_copy = pltpu.make_async_copy(q_hbm, q_ref, sem.at[2 * requests])
        q_copy.start()
        core = place_ref[1]
        copies = []
        for b in range(requests):
            copies.append(
                (
                    pltpu.make_async_copy(k_hbm.at[b], kv.at[b], sem.at[2 * b]),
                    pltpu.make_async_copy(v_hbm.at[b], vv.at[b, :, pl.ds(0, HD)], sem.at[2 * b + 1]),
                )
            )
        copies[0][0].start()
        lane = lax.broadcasted_iota(jnp.int32, (8, positions), 1)
        for b in range(requests):
            left = ext_ref[b] - place_ref[0]
            bias[b] = jnp.where(lane < left, 0.0, NEG_FILL).astype(F32)
        for b in range(requests):
            vv[b, :, HD : 2 * HD] = jnp.ones((positions, HD), BF16)
        stat[...] = jnp.zeros_like(stat)
        q_copy.wait()
        for g in range(heads):
            head = 2 * g + core if g < half else 2 * (g - half) + 1 - core
            at = pl.multiple_of(head * HD, HD)
            for b in range(requests):
                qs[b * blocks_req + g // per_block, (g % per_block) * NODES_REQ : (g % per_block + 1) * NODES_REQ, :] = (
                    q_ref[b * NODES_REQ : (b + 1) * NODES_REQ, pl.ds(at, HD)]
                )

        def scores(block, chunk, slot):
            b = block // blocks_req
            at = pl.multiple_of(chunk * CHUNK, CHUNK)
            s = nt_dot(qs[block], kv[b, pl.ds(at, CHUNK), :])
            best = m_buf[slot]
            for t in range(CHUNK // 128):
                piece = s[:, t * 128 : (t + 1) * 128]
                shift = bias[b, :, pl.ds(pl.multiple_of(at + t * 128, 128), 128)]
                piece = (piece.reshape(BLOCK_ROWS // 8, 8, 128) + shift[None]).reshape(BLOCK_ROWS, 128)
                s_buf[slot, chunk, :, t * 128 : (t + 1) * 128] = piece
                best = jnp.maximum(best, piece)
            m_buf[slot] = best

        def weigh(block, chunk, slot, top):
            b = block // blocks_req
            at = pl.multiple_of(chunk * CHUNK, CHUNK)
            pieces = []
            for t in range(CHUNK // 128):
                w = jnp.exp2(s_buf[slot, chunk, :, t * 128 : (t + 1) * 128] * SCALE2 - top)
                pieces.append(w.astype(BF16))
            acc[...] += jnp.dot(
                jnp.concatenate(pieces, axis=1), vv[b, pl.ds(at, CHUNK), :], preferred_element_type=F32
            )

        copies[0][0].wait()
        for copy in [copy for pair in copies for copy in pair][1:]:
            copy.start()
        m_buf[0] = jnp.full((BLOCK_ROWS, 128), NEG_FILL, F32)

        @pl.loop(0, chunks)
        def _(chunk):
            scores(0, chunk, 0)

        def finish(block, best):
            total = acc[:, HD : HD + 1]
            b = block // blocks_req
            j = block % blocks_req
            slots = lax.broadcasted_iota(jnp.int32, (NODES_REQ, 128), 1)
            rows = slice(b * NODES_REQ, (b + 1) * NODES_REQ)
            held = stat[rows, :]
            for i in range(per_block):
                g = j * per_block + i
                part = slice(i * NODES_REQ, (i + 1) * NODES_REQ)
                out = keep if g < half else send
                out[g % half, rows, :] = acc[part, 0:HD].astype(BF16)
                for n, column in enumerate(thirds(best[part]) + thirds(total[part])):
                    held = jnp.where(slots == g * 8 + n, column, held)
            stat[rows, :] = held

        for block in range(blocks):
            last = block == blocks - 1
            slot = block % 2
            if block % blocks_req == 0:
                copies[block // blocks_req][1].wait()
            if not last and (block + 1) % blocks_req == 0:
                copies[(block + 1) // blocks_req][0].wait()
            best = jnp.max(m_buf[slot], axis=1, keepdims=True)
            best = jnp.maximum(best, 0.5 * NEG_FILL) * SCALE2
            top = jnp.broadcast_to(best, (BLOCK_ROWS, 128))
            acc[...] = jnp.zeros_like(acc)
            if not last:
                m_buf[1 - slot] = jnp.full((BLOCK_ROWS, 128), NEG_FILL, F32)

            @pl.loop(0, chunks)
            def _(chunk):
                if not last:
                    scores(block + 1, chunk, 1 - slot)
                weigh(block, chunk, slot, top)

            finish(block, best)

        turned = stat[...].T
        for g in range(heads):
            out = keep if g < half else send
            out[g % half, NODES : NODES + STAT_ROWS, :] = jnp.concatenate(
                [turned[g * 8 : (g + 1) * 8, :], jnp.zeros((STAT_ROWS - 8, NODES), F32)], axis=0
            ).astype(BF16)

    smem = pl.BlockSpec(memory_space=pltpu.SMEM)
    vmem = pl.BlockSpec(memory_space=pltpu.VMEM)
    hbm = pl.BlockSpec(memory_space=pltpu.HBM)
    out = jax.ShapeDtypeStruct((half, NODES + STAT_ROWS, HD), BF16)
    return pl.pallas_call(
        kernel,
        out_shape=(out, out),
        in_specs=[smem, smem, hbm, hbm, hbm],
        out_specs=(vmem, vmem),
        scratch_shapes=[
            VM((NODES, heads * HD), BF16),
            VM((blocks, BLOCK_ROWS, HD), BF16),
            VM((requests, positions, HD), BF16),
            VM((requests, positions, 2 * HD), BF16),
            VM((requests, 8, positions), F32),
            VM((2, chunks, BLOCK_ROWS, CHUNK), F32),
            VM((2, BLOCK_ROWS, 128), F32),
            VM((BLOCK_ROWS, 2 * HD), F32),
            VM((NODES, 128), F32),
            pltpu.SemaphoreType.DMA((2 * requests + 1,)),
        ],
        compiler_params=pltpu.CompilerParams(vmem_limit_bytes=48 << 20),
        cost_estimate=pl.CostEstimate(
            flops=4 * NODES * heads * positions * HD, transcendentals=NODES * heads * positions, bytes_accessed=5 << 20
        ),
        name="attention",
    )(extents, place, queries, keys, values)


def tree_part(queries, tree_keys, tree_values, ancestors, head):
    requests = ancestors.shape[0]

    def kernel(head_ref, q_ref, k_ref, v_ref, a_ref, o_ref, st_ref):
        at = pl.multiple_of(head_ref[0] * HD, HD)
        slots = lax.broadcasted_iota(jnp.int32, (NODES_REQ, 128), 1)
        for b in range(requests):
            rows = slice(b * NODES_REQ, (b + 1) * NODES_REQ)
            s = nt_dot(q_ref[rows, pl.ds(at, HD)], k_ref[rows, :])
            live = a_ref[b] > 0
            s = jnp.where(live, s * SCALE2, NEG_FILL)
            top = jnp.max(s, axis=1, keepdims=True)
            w = jnp.where(live, jnp.exp2(s - top), 0.0)
            total = jnp.sum(w, axis=1, keepdims=True)
            o_ref[rows, :] = jnp.dot(w.astype(BF16), v_ref[rows, :], preferred_element_type=F32)
            st_ref[rows, :] = jnp.where(slots == 0, top, jnp.where(slots == 1, total, 0.0))
        st_ref[...] = st_ref[...].T

    vmem = pl.BlockSpec(memory_space=pltpu.VMEM)
    return pl.pallas_call(
        kernel,
        out_shape=(jax.ShapeDtypeStruct((NODES, HD), F32), jax.ShapeDtypeStruct((128, NODES), F32)),
        in_specs=[pl.BlockSpec(memory_space=pltpu.SMEM)] + [vmem] * 4,
        out_specs=(vmem, vmem),
        compiler_params=pltpu.CompilerParams(vmem_limit_bytes=8 << 20),
        cost_estimate=pl.CostEstimate(flops=1 << 22, transcendentals=8192, bytes_accessed=1 << 20),
        name="tree_part",
    )(head, queries, tree_keys, tree_values, ancestors)


def merge(first, second):
    heads = first.shape[0]

    def kernel(a_ref, b_ref, o_ref):
        rows = []
        columns = []
        for g in range(heads):
            a = a_ref[g, NODES : NODES + STAT_ROWS, :].astype(F32)
            b = b_ref[g, NODES : NODES + STAT_ROWS, :].astype(F32)
            top_a = a[0:1] + a[1:2] + a[2:3]
            top_b = b[0:1] + b[1:2] + b[2:3]
            top = jnp.maximum(top_a, top_b)
            fa = jnp.exp2(top_a - top)
            fb = jnp.exp2(top_b - top)
            total = fa * (a[3:4] + a[4:5] + a[5:6]) + fb * (b[3:4] + b[4:5] + b[5:6])
            rows.append(jnp.concatenate(thirds(top) + thirds(total) + (jnp.zeros((STAT_ROWS - 6, NODES), F32),), axis=0))
            columns += [fa, fb]
        columns.append(jnp.zeros((128 - 2 * heads, NODES), F32))
        factor = jnp.concatenate(columns, axis=0).T
        for g in range(heads):
            o_ref[g, 0:NODES, :] = (
                a_ref[g, 0:NODES, :].astype(F32) * factor[:, 2 * g : 2 * g + 1]
                + b_ref[g, 0:NODES, :].astype(F32) * factor[:, 2 * g + 1 : 2 * g + 2]
            ).astype(BF16)
            o_ref[g, NODES : NODES + STAT_ROWS, :] = rows[g].astype(BF16)

    vmem = pl.BlockSpec(memory_space=pltpu.VMEM)
    return pl.pallas_call(
        kernel,
        out_shape=jax.ShapeDtypeStruct(first.shape, BF16),
        in_specs=[vmem] * 2,
        out_specs=vmem,
        compiler_params=pltpu.CompilerParams(vmem_limit_bytes=8 << 20),
        cost_estimate=pl.CostEstimate(flops=1 << 20, transcendentals=4096, bytes_accessed=1 << 20),
        name="merge",
    )(first, second)


def combine(parts, tree_sums, tree_stats):
    sources = parts.shape[0]

    def kernel(p_ref, t_ref, ts_ref, o_ref):
        tops = []
        totals = []
        for s in range(sources):
            st = p_ref[s, NODES : NODES + STAT_ROWS, :].astype(F32)
            tops.append(st[0:1] + st[1:2] + st[2:3])
            totals.append(st[3:4] + st[4:5] + st[5:6])
        tops.append(ts_ref[0:1, :])
        totals.append(ts_ref[1:2, :])
        tops = jnp.concatenate(tops + [jnp.full((24 - sources - 1, NODES), NEG_FILL, F32)], axis=0)
        totals = jnp.concatenate(totals + [jnp.zeros((24 - sources - 1, NODES), F32)], axis=0)
        best = jnp.max(tops, axis=0, keepdims=True)
        factor = jnp.exp2(tops - best)
        factor = factor / jnp.sum(factor * totals, axis=0, keepdims=True)
        factor = jnp.concatenate([factor, jnp.zeros((128 - 24, NODES), F32)], axis=0).T
        out = t_ref[...] * factor[:, sources : sources + 1]
        for s in range(sources):
            out = out + p_ref[s, 0:NODES, :].astype(F32) * factor[:, s : s + 1]
        out = out.astype(BF16)
        for s in range(sources):
            o_ref[s] = out

    vmem = pl.BlockSpec(memory_space=pltpu.VMEM)
    return pl.pallas_call(
        kernel,
        out_shape=jax.ShapeDtypeStruct((sources, NODES, HD), BF16),
        in_specs=[vmem] * 3,
        out_specs=vmem,
        compiler_params=pltpu.CompilerParams(vmem_limit_bytes=8 << 20),
        cost_estimate=pl.CostEstimate(flops=1 << 20, transcendentals=4096, bytes_accessed=1 << 20),
        name="combine",
    )(parts, tree_sums, tree_stats)


def own_rows(attended, w):
    heads, span, columns = w.shape
    x = jnp.concatenate([attended[g] for g in range(heads)], axis=1)
    return jnp.dot(x, w[...].reshape(heads * span, columns), preferred_element_type=F32)


def project_own(side, attended, weight):
    heads, _, span, columns = weight.shape

    def kernel(side_ref, a_ref, w_hbm, y_ref, o_ref, w, sem):
        own = side_ref[0]
        mine = [pltpu.make_async_copy(w_hbm.at[g, own], w.at[g], sem.at[g]) for g in range(heads)]
        others = [pltpu.make_async_copy(w_hbm.at[g, 1 - own], o_ref.at[g], sem.at[heads + g]) for g in range(heads)]
        for copy in mine + others:
            copy.start()
        for copy in mine:
            copy.wait()
        y_ref[...] = own_rows(a_ref, w)
        for copy in others:
            copy.wait()

    vmem = pl.BlockSpec(memory_space=pltpu.VMEM)
    rows = (heads, span, columns)
    y, fetched = pl.pallas_call(
        kernel,
        out_shape=(jax.ShapeDtypeStruct((NODES, columns), F32), jax.ShapeDtypeStruct(rows, BF16)),
        in_specs=[pl.BlockSpec(memory_space=pltpu.SMEM), vmem, pl.BlockSpec(memory_space=pltpu.HBM)],
        out_specs=(vmem, pl.BlockSpec(memory_space=pl.ANY)),
        scratch_shapes=[VM(rows, BF16), pltpu.SemaphoreType.DMA((2 * heads,))],
        compiler_params=pltpu.CompilerParams(vmem_limit_bytes=8 << 20),
        cost_estimate=pl.CostEstimate(flops=2 * NODES * heads * span * columns, transcendentals=0, bytes_accessed=6 << 20),
        name="project_own",
    )(side, attended, weight)
    return y, pltpu.with_memory_space_constraint(fetched, pltpu.VMEM)


def project_other(attended, fetched, so_far):
    columns = fetched.shape[2]

    def kernel(a_ref, w_ref, y_ref, o_ref):
        y = (y_ref[...] + own_rows(a_ref, w_ref)).astype(BF16)
        for i in range(columns // 128):
            o_ref[i] = y[:, i * 128 : (i + 1) * 128]

    vmem = pl.BlockSpec(memory_space=pltpu.VMEM)
    return pl.pallas_call(
        kernel,
        out_shape=jax.ShapeDtypeStruct((columns // 128, NODES, 128), BF16),
        in_specs=[vmem] * 3,
        out_specs=vmem,
        compiler_params=pltpu.CompilerParams(vmem_limit_bytes=8 << 20),
        cost_estimate=pl.CostEstimate(flops=2 * NODES * fetched.size, transcendentals=0, bytes_accessed=1 << 20),
        name="project_other",
    )(attended, fetched, so_far)


def finish_hidden(shares, residual, position, copies):
    sources = shares.shape[0]

    def kernel(pos_ref, s_ref, r_ref, h_ref, o_ref):
        at = pl.multiple_of(pos_ref[0] * 128, 128)
        total = s_ref[0].astype(F32)
        for s in range(1, sources):
            total = total + s_ref[s].astype(F32)
        h = (r_ref[:, pl.ds(at, 128)].astype(F32) + total).astype(BF16)
        h_ref[...] = h
        for i in range(copies):
            o_ref[i] = h

    vmem = pl.BlockSpec(memory_space=pltpu.VMEM)
    return pl.pallas_call(
        kernel,
        out_shape=(
            jax.ShapeDtypeStruct((NODES, 128), BF16),
            jax.ShapeDtypeStruct((copies, NODES, 128), BF16),
        ),
        in_specs=[pl.BlockSpec(memory_space=pltpu.SMEM), vmem, vmem],
        out_specs=(vmem, vmem),
        compiler_params=pltpu.CompilerParams(vmem_limit_bytes=8 << 20),
        cost_estimate=pl.CostEstimate(flops=1 << 18, transcendentals=0, bytes_accessed=3 << 20),
        name="finish_hidden",
    )(position, shares, residual)


HANDED = 4


def vocab_sum(side, h_any, g_ref, w_hbm, y_ref, sq_ref, h_buf, w_buf, sem, held=None, handed=None):
    groups, _, span, _ = w_hbm.shape
    blocks = span // 128
    ready = 0 if held is None else HANDED

    def arrival(group):
        at = pl.ds(group * blocks, blocks)
        return pltpu.make_async_copy(h_any.at[at], h_buf.at[at], sem.at[2 * group])

    def fetch(group):
        return pltpu.make_async_copy(w_hbm.at[group, side], w_buf.at[group - ready], sem.at[2 * group + 1])

    for group in range(groups):
        arrival(group).start()
        if group >= ready:
            fetch(group).start()
    extra = []
    if handed is not None:
        for group in range(HANDED):
            extra.append(pltpu.make_async_copy(w_hbm.at[group, 1 - side], handed.at[group], sem.at[2 * groups + group]))
            extra[-1].start()

    def add(group, rows):
        pieces = []
        squares = sq_ref[...]
        for i in range(blocks):
            h = h_buf[group * blocks + i].astype(F32)
            squares = squares + h * h
            pieces.append((h * g_ref[group, side, i : i + 1, :].astype(F32)).astype(BF16))
        sq_ref[...] = squares
        x = jnp.concatenate(pieces, axis=1)
        y_ref[...] += jnp.dot(x, rows, preferred_element_type=F32)

    if ready:

        @pl.loop(0, ready)
        def _(group):
            arrival(group).wait()
            add(group, held[group])

    @pl.loop(ready, groups)
    def _(group):
        arrival(group).wait()
        fetch(group).wait()
        add(group, w_buf[group - ready])

    for copy in extra:
        copy.wait()


def vocab_scratch(hidden, weight, ready):
    groups, _, span, columns = weight.shape
    return [
        VM(hidden.shape, BF16),
        VM((groups - ready, span, columns), BF16),
        pltpu.SemaphoreType.DMA((2 * groups + HANDED,)),
    ]


def vocab_first(side, hidden, gain, weight):
    groups, _, span, columns = weight.shape

    def kernel(side_ref, h_any, g_ref, w_hbm, y_ref, sq_ref, handed, *scratch):
        y_ref[...] = jnp.zeros_like(y_ref)
        sq_ref[...] = jnp.zeros_like(sq_ref)
        vocab_sum(side_ref[0], h_any, g_ref, w_hbm, y_ref, sq_ref, *scratch, handed=handed)

    vmem = pl.BlockSpec(memory_space=pltpu.VMEM)
    anywhere = pl.BlockSpec(memory_space=pl.ANY)
    y, squares, handed = pl.pallas_call(
        kernel,
        out_shape=(
            jax.ShapeDtypeStruct((NODES, columns), F32),
            jax.ShapeDtypeStruct((NODES, 128), F32),
            jax.ShapeDtypeStruct((HANDED, span, columns), BF16),
        ),
        in_specs=[pl.BlockSpec(memory_space=pltpu.SMEM), anywhere, vmem, pl.BlockSpec(memory_space=pltpu.HBM)],
        out_specs=(vmem, vmem, anywhere),
        scratch_shapes=vocab_scratch(hidden, weight, 0),
        compiler_params=pltpu.CompilerParams(vmem_limit_bytes=24 << 20),
        cost_estimate=pl.CostEstimate(
            flops=2 * NODES * groups * span * columns, transcendentals=0, bytes_accessed=10 << 20
        ),
        name="vocab_first",
    )(side, hidden, gain, weight)
    return y, squares, pltpu.with_memory_space_constraint(handed, pltpu.VMEM)


def vocab_second(side, hidden, gain, weight, y_first, sq_first, held, target, copies):
    groups, _, span, columns = weight.shape

    def kernel(side_ref, h_any, g_ref, w_hbm, y0_ref, sq0_ref, held_ref, t_ref, o_ref, acc, sq, *scratch):
        acc[...] = y0_ref[...]
        sq[...] = sq0_ref[...]
        vocab_sum(side_ref[0], h_any, g_ref, w_hbm, acc, sq, *scratch, held=held_ref)
        mean = jnp.sum(sq[...], axis=1, keepdims=True) / D
        logits = acc[...] * lax.rsqrt(mean + EPSILON)
        peak = jnp.max(logits, axis=1, keepdims=True)
        total = jnp.sum(jnp.exp(logits - peak), axis=1, keepdims=True)
        lse = peak + jnp.log(total)
        column = lax.broadcasted_iota(jnp.int32, (NODES, columns), 1)
        chosen = jnp.sum(jnp.where(column == t_ref[...], logits, 0.0), axis=1, keepdims=True)
        lane = lax.broadcasted_iota(jnp.int32, (NODES, 128), 1)
        rows = jnp.where(lane == 0, lse, jnp.where(lane == 1, chosen, 0.0)).T
        row = jnp.concatenate([rows[0:1, :], rows[1:2, :]], axis=1)
        for i in range(copies):
            o_ref[i] = row

    vmem = pl.BlockSpec(memory_space=pltpu.VMEM)
    anywhere = pl.BlockSpec(memory_space=pl.ANY)
    return pl.pallas_call(
        kernel,
        out_shape=jax.ShapeDtypeStruct((copies, 1, 2 * NODES), F32),
        in_specs=[pl.BlockSpec(memory_space=pltpu.SMEM), anywhere, vmem, pl.BlockSpec(memory_space=pltpu.HBM)] + [vmem] * 4,
        out_specs=vmem,
        scratch_shapes=[VM((NODES, columns), F32), VM((NODES, 128), F32)] + vocab_scratch(hidden, weight, HANDED),
        compiler_params=pltpu.CompilerParams(vmem_limit_bytes=24 << 20),
        cost_estimate=pl.CostEstimate(
            flops=2 * NODES * groups * span * columns, transcendentals=1 << 16, bytes_accessed=10 << 20
        ),
        name="vocab_second",
    )(side, hidden, gain, weight, y_first, sq_first, held, target)


def final_score(stats, amateur):
    def kernel(s_ref, a_ref, o_ref):
        lse = s_ref[:, 0, 0:NODES]
        chosen = s_ref[:, 0, NODES : 2 * NODES]
        best = jnp.max(lse, axis=0, keepdims=True)
        total = jnp.sum(jnp.exp(lse - best), axis=0, keepdims=True)
        picked = jnp.sum(chosen, axis=0, keepdims=True)
        o_ref[...] = picked - (best + jnp.log(total)) - a_ref[...]

    vmem = pl.BlockSpec(memory_space=pltpu.VMEM)
    return pl.pallas_call(
        kernel,
        out_shape=jax.ShapeDtypeStruct((1, NODES), F32),
        in_specs=[vmem, vmem],
        out_specs=vmem,
        compiler_params=pltpu.CompilerParams(vmem_limit_bytes=8 << 20),
        name="final_score",
    )(stats, amateur)


def body(
    queries,
    cache_keys,
    cache_values,
    tree_keys,
    tree_values,
    ancestors,
    filled_extents,
    out_weight,
    residual,
    norm_gain,
    vocab_weight,
    candidates,
    amateur,
):
    positions = cache_keys.shape[1]
    seq_index = lax.axis_index(SEQ)
    head_index = lax.axis_index(HEAD)
    core = lax.axis_index("c")
    seq_size = lax.axis_size(SEQ)
    cores = lax.axis_size("c")
    chips = lax.axis_size(CHIPS)
    devices = chips * cores

    def scalar(x):
        return x.astype(jnp.int32).reshape(1)

    def swap(x):
        return lax.ppermute(x, "c", [(0, 1), (1, 0)])

    def in_hbm(x):
        return pltpu.with_memory_space_constraint(x, pltpu.HBM)

    own, other = scalar(core), scalar(1 - core)
    place = jnp.stack([seq_index * positions, core]).astype(jnp.int32)
    keep, send = attention(in_hbm(queries), in_hbm(cache_keys), in_hbm(cache_values), in_hbm(filled_extents), place)
    parts = merge(keep, swap(send))
    parts = lax.all_to_all(parts, ROWS, 0, 0, tiled=True)
    tree_sums, tree_stats = tree_part(queries, tree_keys, tree_values, ancestors, scalar(seq_index))
    attended = combine(parts, tree_sums, tree_stats)
    rows, columns = out_weight.shape
    weight = in_hbm(out_weight.reshape(rows // HD // cores, cores, HD, columns))
    attended = lax.all_to_all(attended, ROWS, 0, 0, tiled=True)
    swapped = swap(attended)
    projected, fetched = project_own(own, attended, weight)
    shares = project_other(swapped, fetched, projected)
    shares = lax.all_to_all(shares, HEAD, 0, 0, tiled=True)
    hidden, repeated = finish_hidden(shares, residual, scalar(head_index), chips)
    own_side = lax.all_to_all(repeated, CHIPS, 0, 0, tiled=True)
    vocab_local = vocab_weight.shape[1]
    groups = seq_size // cores
    span = D // seq_size
    weight = in_hbm(vocab_weight.reshape(groups, cores, span, vocab_local))
    other_side = swap(own_side)
    gain = norm_gain.reshape(groups, cores, span // 128, 128)
    y, squares, handed = vocab_first(own, own_side, gain, weight)
    target = (candidates - lax.axis_index(ALL) * vocab_local).reshape(NODES, 1)
    stats = vocab_second(other, other_side, gain, weight, y, squares, handed, target, devices)
    stats = lax.all_to_all(stats, ALL, 0, 0, tiled=True)
    contrast = final_score(stats, amateur.reshape(1, NODES))
    return (hidden, contrast.reshape(NODES))


def solution(mesh):
    fine = Mesh(mesh.devices.reshape(2, 4, 2, 4, 2), ALL)
    in_specs = (
        P(None, HEAD),
        P(None, SEQ, HEAD),
        P(None, SEQ, HEAD),
        P(None, HEAD),
        P(None, HEAD),
        P(),
        P(),
        P(HEAD, SEQ),
        P(None, SEQ),
        P(),
        P(None, ALL),
        P(),
        P(),
    )
    out_specs = (P(None, ALL), P())
    return jax.shard_map(body, mesh=fine, in_specs=in_specs, out_specs=out_specs, check_vma=False)
```
